32 devices in a mesh: head: 4 (over y, core), seq: 8 (over z, x).
Axes of the slice: x: 2, y: 2, z: 4, core: 2. Of those that a mesh axis runs over, the one named last changes fastest.
Arguments:
- queries: bfloat16 [4096, 4096], P('seq', 'head'), may hold values from -6 to 6
- keys: bfloat16 [4096, 4096], P('seq', 'head'), may hold values from -6 to 6
- values: bfloat16 [4096, 4096], P('seq', 'head'), may hold values from -6 to 6
- rate: float32 [8, 4096], P('head', 'seq'), may hold values from 0.0001 to 0.001
- fast_gate: float32 [8, 512, 512], P('head', 'seq'), may hold values from -3 to 3
- fast_up: float32 [8, 512, 512], P('head', 'seq'), may hold values from -3 to 3
- fast_down: float32 [8, 512, 512], P('head', 'seq'), may hold values from -8 to 8
- out_gain: float32 [4096], P('head'), may hold values from 0.25 to 1.75
Outputs:
- mixed: bfloat16 [4096, 4096], P('seq', 'head')
- new_gate: float32 [8, 512, 512], P('head', 'seq')
- new_up: float32 [8, 512, 512], P('head', 'seq')
- new_down: float32 [8, 512, 512], P('head', 'seq')
The draws below stay inside these ranges and needn't reach their ends.
All inputs are finite; a program needn't handle non-finite values.
Results may differ from the reference program's by a relative error of at most 0.012.
Values may be sent and summed in bfloat16 or wider, within the bound.
A program may use at most 128 MiB of HBM per device.

```python
import math
import jax
import jax.numpy as jnp
from jax import lax

HEADS = 8
HD = 512
FAST = 512
WINDOW = 512
GROUP = 4096


def query_key_pair(key):
    key_q, key_k = jax.random.split(jax.random.fold_in(key, 7), 2)
    width = HEADS * HD
    q_vals = 1.3 * jax.random.truncated_normal(key_q, -4.0, 4.0, (GROUP, width), jnp.float32)
    k_vals = 1.3 * jax.random.truncated_normal(key_k, -4.0, 4.0, (GROUP, width), jnp.float32)
    return (q_vals, k_vals)


def draw_queries(key, part):
    return query_key_pair(key)[0].astype(jnp.bfloat16)


def draw_keys(key, part):
    return query_key_pair(key)[1].astype(jnp.bfloat16)


def fast_matrix(key, salt, rows_n, cols_n, rising):
    key_base, key_cols = jax.random.split(jax.random.fold_in(key, salt))
    base = jax.random.truncated_normal(key_base, -4.0, 4.0, (HEADS, rows_n, cols_n), jnp.float32)
    row_scale = 10.0 ** (jnp.arange(rows_n, dtype=jnp.float32) / (rows_n - 1))
    col_scale = jnp.exp(jax.random.uniform(key_cols, (HEADS, 1, cols_n), jnp.float32, 0.0, math.log(10.0)))
    overall = jnp.sqrt(jnp.mean(row_scale * row_scale) * jnp.mean(col_scale * col_scale))
    if rising:
        head_scale = jnp.exp(jnp.arange(HEADS, dtype=jnp.float32) / max(HEADS - 1, 1) * math.log(3.0))
    else:
        head_scale = jnp.ones((HEADS,), jnp.float32)
    result = base * row_scale[None, :, None] * col_scale / overall / math.sqrt(rows_n)
    return (result * head_scale[:, None, None]).astype(jnp.float32)


def draw_fast_gate(key, part):
    return fast_matrix(key, 11, HD, FAST, False)


def draw_fast_up(key, part):
    return fast_matrix(key, 13, HD, FAST, False)


def draw_fast_down(key, part):
    return fast_matrix(key, 17, FAST, HD, True)


def block_scale(key, extent, cuts, least, high):
    loudness, own = 1.0, jax.random.fold_in(key, 6)
    for dim, blocks in cuts:
        heights = jnp.exp(jax.random.uniform(jax.random.fold_in(own, dim), (blocks,), jnp.float32, least / len(cuts), high / len(cuts)))
        loudness = loudness * jnp.repeat(heights, extent[dim] // blocks).reshape([-1 if axis == dim else 1 for axis in range(len(extent))])
    return loudness


def centred(key, dims, deviation, limit, cuts=(), kind=jnp.bfloat16):
    loudness = block_scale(key, dims, cuts, -0.22, 0.18) if cuts else 1.0
    values = jax.random.normal(key, dims, jnp.float32) * deviation * loudness
    return jnp.minimum(jnp.maximum(values, -limit), limit).astype(kind)


def setup_inputs(seed: int = 0) -> dict:
    key_list = jax.random.split(jax.random.key(seed), 9)
    return {
        "queries": draw_queries(jax.random.fold_in(key_list[8], 71), 0),
        "keys": draw_keys(jax.random.fold_in(key_list[8], 71), 0),
        "values": centred(key_list[2], (GROUP, HEADS * HD), 1.0, 6.0, ((0, 8), (1, 4))),
        "rate": jnp.clip(jnp.exp(math.log(0.001) - 2.3025852 * jax.random.uniform(key_list[3], (HEADS, GROUP), jnp.float32) ** block_scale(key_list[3], (HEADS, GROUP), ((0, 4), (1, 8)), -0.2, 0.2)), 0.0001, 0.001),
        "fast_gate": draw_fast_gate(jax.random.fold_in(key_list[8], 71), 0),
        "fast_up": draw_fast_up(jax.random.fold_in(key_list[8], 71), 0),
        "fast_down": draw_fast_down(jax.random.fold_in(key_list[8], 71), 0),
        "out_gain": jnp.clip(1.0 + 0.15 * jax.random.normal(key_list[7], (HEADS * HD,), jnp.float32), 0.25, 1.75),
    }


EPS = 1e-06

def rescale(old, upd):
    old_sq = lax.optimization_barrier(jnp.sum(old * old, axis=0))
    new_sq = lax.optimization_barrier(jnp.sum(upd * upd, axis=0))
    return upd * (jnp.sqrt(old_sq) / jnp.sqrt(new_sq + EPS))[None, :]

def head_update(inputs):
    qh, kh, vh, eta, w_one, w_three, w_two = inputs
    w1b = w_one.astype(jnp.bfloat16)
    w3b = w_three.astype(jnp.bfloat16)
    w2b = w_two.astype(jnp.bfloat16)
    pre_a = jnp.dot(kh, w1b, preferred_element_type=jnp.float32)
    pre_b = jnp.dot(kh, w3b, preferred_element_type=jnp.float32)
    sigma = jax.nn.sigmoid(pre_a)
    hidden = (pre_a * sigma * pre_b).astype(jnp.bfloat16)
    scaled = (eta[:, None] * vh.astype(jnp.float32)).astype(jnp.bfloat16)
    grad_two = jnp.dot(hidden.T, scaled, preferred_element_type=jnp.float32)
    back = jnp.dot(scaled, w2b.T, preferred_element_type=jnp.float32)
    d_gate = (back * pre_b * sigma * (1.0 + pre_a * (1.0 - sigma))).astype(jnp.bfloat16)
    d_up = (back * pre_a * sigma).astype(jnp.bfloat16)
    grad_one = jnp.dot(kh.T, d_gate, preferred_element_type=jnp.float32)
    grad_three = jnp.dot(kh.T, d_up, preferred_element_type=jnp.float32)
    new_one = rescale(w_one, w_one + grad_one)
    new_three = rescale(w_three, w_three + grad_three)
    new_two = rescale(w_two, w_two + grad_two)
    apply_a = jnp.dot(qh, new_one.astype(jnp.bfloat16), preferred_element_type=jnp.float32)
    apply_b = jnp.dot(qh, new_three.astype(jnp.bfloat16), preferred_element_type=jnp.float32)
    apply_h = (apply_a * jax.nn.sigmoid(apply_a) * apply_b).astype(jnp.bfloat16)
    result = jnp.dot(apply_h, new_two.astype(jnp.bfloat16), preferred_element_type=jnp.float32)
    return (result, new_one, new_three, new_two)

def reference(queries, keys, values, rate, fast_gate, fast_up, fast_down, out_gain):
    q_three = queries.reshape(GROUP, HEADS, HD)
    k_three = keys.reshape(GROUP, HEADS, HD)
    v_three = values.reshape(GROUP, HEADS, HD)
    lead = jnp.zeros((WINDOW, HEADS, HD), jnp.bfloat16)
    padded_k = jnp.concatenate([lead, k_three], axis=0)
    padded_v = jnp.concatenate([lead, v_three], axis=0)
    scale = 1.0 / math.sqrt(HD)
    rows_i = jnp.arange(WINDOW, dtype=jnp.int32)[:, None]
    cols_j = jnp.arange(2 * WINDOW, dtype=jnp.int32)[None, :]

    def attend(block):
        start = (block * WINDOW).astype(jnp.int32)
        q_blk = lax.dynamic_slice_in_dim(q_three, start, WINDOW, 0).astype(jnp.float32)
        k_blk = lax.dynamic_slice_in_dim(padded_k, start, 2 * WINDOW, 0).astype(jnp.float32)
        v_blk = lax.dynamic_slice_in_dim(padded_v, start, 2 * WINDOW, 0).astype(jnp.float32)
        scores = jnp.einsum('qhd,khd->hqk', q_blk, k_blk) * scale
        valid = (cols_j > rows_i) & (cols_j <= rows_i + WINDOW) & (start + cols_j >= WINDOW)
        scores = jnp.where(valid[None], scores, -jnp.inf)
        top = lax.optimization_barrier(jnp.max(scores, axis=-1, keepdims=True))
        expo = jnp.exp(scores - top)
        probs = (expo / lax.optimization_barrier(jnp.sum(expo, axis=-1, keepdims=True))).astype(jnp.bfloat16)
        return jnp.einsum('hqk,khd->qhd', probs.astype(jnp.float32), v_blk)
    attn = lax.map(attend, jnp.arange(GROUP // WINDOW, dtype=jnp.int32)).reshape(GROUP, HEADS, HD)
    result, new_gate, new_up, new_down = lax.map(head_update, (q_three.transpose(1, 0, 2), k_three.transpose(1, 0, 2), v_three.transpose(1, 0, 2), rate, fast_gate, fast_up, fast_down))
    branch = result.transpose(1, 0, 2)
    mean_sq = lax.optimization_barrier(jnp.mean(branch * branch, axis=(1, 2)))
    inv = lax.rsqrt(mean_sq + EPS)
    gain = out_gain.reshape(HEADS, HD)
    mixed = (attn + branch * inv[:, None, None] * gain[None]).astype(jnp.bfloat16)
    return (mixed.reshape(GROUP, HEADS * HD), new_gate, new_up, new_down)
```

```python
import functools
import math

import jax
import jax.numpy as jnp
from jax import lax
from jax.experimental import pallas as pl
from jax.experimental.pallas import tpu as pltpu
from jax.sharding import PartitionSpec as P

WINDOW = 512
EPS = 1e-06
TILE = 128
WIDE = 256
LAG = 3
FIRST = 1
PARTS = 4
NONE = -1e30
MESH = pl.DeviceIdType.MESH
F32 = jnp.float32
BF16 = jnp.bfloat16
scope = jax.named_scope


def dot(a, b):
    return jnp.dot(a, b, preferred_element_type=F32)


def dot_lhs_t(a, b):
    return lax.dot_general(a, b, (((0,), (0,)), ((), ())), preferred_element_type=F32)


def dot_rhs_t(a, b):
    return lax.dot_general(a, b, (((1,), (1,)), ((), ())), preferred_element_type=F32)


def kernel(
    n, hn,
    q, k, v, rate, gain, w1, w3, w2,
    mixed, o1, o3, o2,
    w_in, rate_in, gain_in, wg, ug, pg, sum_out, sum_in, sum_x, wb_out, g_in,
    ratio_out, ratio_in, qx, kx, vx, kt, eta_x, gv, hid, dab, pre, attn,
    attn_out, attn_in, h2, branch, f_out, f_in, sq, sq_in,
    ag_s, ag_r, in_s, in_r, ex_s, ex_r, ou_s, ou_r, l_s, x_s, x_r, v_s, v_r, halo_s, halo_r,
    g_s, g_r, a_s, a_r, f_s, f_r, sq_s, sq_r,
):
    rows, width = q.shape
    heads, shard, hd = w1.shape
    half = hd // 2
    line = n // 2
    tiles = rows // TILE
    me = lax.axis_index("seq")
    hme = lax.axis_index("head")
    m = lax.div(me, 2)
    c = lax.rem(me, 2)
    oc = 1 - c
    partner = 2 * m + oc
    step_to = (1, -1)
    chunks = [(0, 0), (1, 0), (0, 1), (1, 1), (2, 0), (2, 1)]
    middle = line // 2
    parts = math.gcd(PARTS, line)
    deep = line // parts
    left = m < middle
    inward = jnp.where(left, 1, -1)
    edge = jnp.where(left, m, line - 1 - m)
    inner = edge == middle - 1

    def seq_at(b):
        return 2 * lax.rem(b + line, line) + c

    def lanes(i):
        return pl.ds(pl.multiple_of(i * hd, hd), hd)

    def block(i):
        return pl.ds(pl.multiple_of(i * rows, rows), rows)

    def after_pad(i):
        return pl.ds(pl.multiple_of(WINDOW + i * rows, TILE), rows)

    def tile_at(i):
        return pl.ds(pl.multiple_of(i * TILE, TILE), TILE)

    def halves(h):
        return slice(h * half, (h + 1) * half)

    barrier = pltpu.get_barrier_semaphore()
    for s in (partner, seq_at(m + 1), seq_at(m - 1)):
        pl.semaphore_signal(barrier, inc=1, device_id={"seq": s}, device_id_type=MESH)
    for d in range(1, hn):
        peer = lax.rem(hme + d, hn)
        for s in (me, partner):
            pl.semaphore_signal(
                barrier, inc=1, device_id={"seq": s, "head": peer}, device_id_type=MESH
            )

    loads = [
        pltpu.make_async_copy(src, dst, l_s.at[i])
        for i, (src, dst) in enumerate(
            (
                (w1, w_in.at[0]), (w3, w_in.at[1]), (w2, w_in.at[2]),
                (k.at[:, lanes(c)], kx.at[after_pad(c)]),
                (v.at[:, lanes(c)], vx.at[after_pad(c)]),
                (q.at[:, lanes(c)], qx.at[block(c)]),
                (rate, rate_in), (gain, gain_in),
            )
        )
    ]
    for copy in loads:
        copy.start()
    with scope("a_load"):
        for j in range(3):
            loads[j].wait()
            wg[j, m, c] = w_in[j, c].astype(BF16)
            wb_out[j] = w_in[j, oc].astype(BF16)
    with scope("a_barrier"):
        pl.semaphore_wait(barrier, 3 + 2 * (hn - 1))

    pending = []

    def start(copy, when=None):
        if when is None:
            copy.start()
        else:
            pl.when(when)(copy.start)
        pending.append((copy, when))

    def wait(copy, when):
        pl.when(when)(copy.wait_recv)

    def remote(src, dst, ss, rr, **where):
        return pltpu.make_async_remote_copy(
            src_ref=src, dst_ref=dst, send_sem=ss, recv_sem=rr,
            device_id=where, device_id_type=MESH,
        )

    def to_partner(i, src, dst):
        return remote(src, dst, x_s.at[i], x_r.at[i], seq=partner)

    x_w = to_partner(0, wb_out, wg.at[:, m, c])
    x_k = to_partner(1, k.at[:, lanes(oc)], kx.at[after_pad(c)])
    x_e = to_partner(2, rate, eta_x)
    x_q = to_partner(3, q.at[:, lanes(oc)], qx.at[block(c)])
    x_n = to_partner(4, ratio_out, ratio_in)
    x_v = [
        remote(
            v.at[i * TILE:(i + 1) * TILE, lanes(oc)],
            vx.at[pl.ds(pl.multiple_of(WINDOW + c * rows + i * TILE, TILE), TILE)],
            v_s.at[i], v_r.at[i], seq=partner,
        )
        for i in range(tiles)
    ]
    x_g = [
        remote(ug.at[i, m, oc], g_in.at[i], g_s.at[i], g_r.at[i], seq=partner) for i in range(6)
    ]
    has_next = m < line - 1
    has_prev = m > 0

    def halo(x, first, count, i):
        return remote(
            x.at[2 * rows + first:2 * rows + first + count], x.at[first:first + count],
            halo_s.at[i], halo_r.at[i], seq=seq_at(m + 1),
        )

    halo_k = halo(kx, 0, WINDOW, 0)
    halo_v = [halo(vx, i * TILE, TILE, 1 + i) for i in range(WINDOW // TILE)]

    def link(ss, rr, src, dst, d, i, s):
        return remote(
            src, dst, ss.at[d, i, s - 1], rr.at[d, i, s - 1], seq=seq_at(m + step_to[d])
        )

    def ahead(d):
        return line - 1 - m if d == 0 else m

    def w_piece(i, b):
        return wg.at[i % 3, b, c if i < 3 else oc]

    def gather_copy(i, d, s):
        b = lax.rem(m - step_to[d] * (s - 1) + line, line)
        return link(ag_s, ag_r, w_piece(i, b), w_piece(i, b), d, i, s)

    def gather_arrived(i, d, s, passing):
        b = lax.rem(m - step_to[d] * s + line, line)
        onward = ahead(d) >= 1 if passing else ahead(d) == 0
        wait(
            link(ag_s, ag_r, w_piece(i, b), w_piece(i, b), d, i, s),
            jnp.logical_and(ahead(1 - d) >= s, onward),
        )

    def gather_send(i, s):
        for d in range(2):
            if s > 1:
                gather_arrived(i, d, s - 1, True)
            start(
                gather_copy(i, d, s),
                jnp.logical_and(ahead(d) >= 1, ahead(1 - d) >= s - 1),
            )

    def gather_finish(i):
        for d in range(2):
            for s in range(1, line):
                gather_arrived(i, d, s, False)

    def part(r):
        return slice(r * deep, (r + 1) * deep)

    def inward_copy(i, r, across):
        return remote(
            sum_out.at[i, part(r)], (sum_x if across else sum_in).at[i, part(r)],
            (ex_s if across else in_s).at[i, r], (ex_r if across else in_r).at[i, r],
            seq=seq_at(m + inward),
        )

    def outward_copy(i, r):
        piece = ug.at[i, part(r)]
        return remote(piece, piece, ou_s.at[i, r], ou_r.at[i, r], seq=seq_at(m - inward))

    def sum_first(i, r):
        @pl.when(edge == 0)
        def _():
            sum_out[i, part(r)] = pg[i, part(r)].astype(BF16)

        start(inward_copy(i, r, False), jnp.logical_and(edge == 0, jnp.logical_not(inner)))
        start(inward_copy(i, r, True), jnp.logical_and(edge == 0, inner))

    def sum_on(i, r):
        @pl.when(edge > 0)
        def _():
            inward_copy(i, r, False).wait_recv()
            total = pg[i, part(r)] + sum_in[i, part(r)].astype(F32)
            pg[i, part(r)] = total
            sum_out[i, part(r)] = total.astype(BF16)

        start(inward_copy(i, r, False), jnp.logical_and(edge > 0, jnp.logical_not(inner)))
        start(inward_copy(i, r, True), jnp.logical_and(edge > 0, inner))

    def sum_back(i, r):
        j, h = chunks[i]

        @pl.when(inner)
        def _():
            inward_copy(i, r, True).wait_recv()
            total = pg[i, part(r)] + sum_x[i, part(r)].astype(F32)
            ug[i, part(r)] = (total + wg[j, part(r), :, :, halves(h)].astype(F32)).astype(BF16)

        wait(outward_copy(i, r), jnp.logical_not(inner))
        start(outward_copy(i, r), edge > 0)

    def column(row):
        return jnp.transpose(jnp.broadcast_to(row, (TILE, row.shape[1])))

    def as_row(col):
        return jnp.transpose(jnp.broadcast_to(col, (TILE, TILE)))[:8]

    def w_cols(j, h):
        return wg[j, :, :, :, halves(h)].reshape(n * shard, half)

    def w_rows(j, h):
        return wg[j].reshape(n * shard, hd)[halves(h)]

    def u_all(i):
        return ug[i].reshape(n * shard, half)

    def forward(b):
        for h in range(2):

            @pl.loop(0, rows // WIDE)
            def _(i):
                at = pl.ds(pl.multiple_of(b * rows + i * WIDE, WIDE), WIDE)
                kt = kx[pl.ds(pl.multiple_of(WINDOW + b * rows + i * WIDE, WIDE), WIDE), :]
                a = dot(kt, w_cols(0, h))
                up = dot(kt, w_cols(1, h))
                g = jax.nn.sigmoid(a)
                ag = a * g
                hid[at, halves(h)] = (ag * up).astype(BF16)
                pre[0, at, halves(h)] = up * g * (1.0 + a * (1.0 - g))
                pre[1, at, halves(h)] = ag

    def scaled_values(b):
        eta = column((rate_in if b is c else eta_x)[pl.ds(c, 1), :])[:, :1]
        vb = vx[after_pad(b), :]
        gv[block(b), :] = (eta * vb.astype(F32)).astype(BF16)

    def backward(b, h):
        @pl.loop(0, rows // WIDE)
        def _(i):
            at = pl.ds(pl.multiple_of(b * rows + i * WIDE, WIDE), WIDE)
            back = dot_rhs_t(gv[at, :], w_rows(2, h))
            dab[0, at, halves(h)] = (back * pre[0, at, halves(h)]).astype(BF16)
            dab[1, at, halves(h)] = (back * pre[1, at, halves(h)]).astype(BF16)

    def product(i):
        j, h = chunks[i]
        if j == 2:
            g = dot_lhs_t(hid[...], gv[:, halves(h)])
        else:
            g = dot(kt[...], dab[j, :, halves(h)])
        pg[i] = g.reshape(line, 2, shard, half)

    def softmax(s, ok):
        s = jnp.where(ok, s * (1.0 / math.sqrt(hd)), NONE)
        top = jnp.max(s, axis=1, keepdims=True)
        e = jnp.exp(s - top)
        total = jnp.sum(e, axis=1, keepdims=True)
        return (e * (1.0 / total)).astype(BF16)

    def local_attention(b, i):
        span = WINDOW + TILE
        base = pl.multiple_of(b * rows + i * TILE, TILE)
        s = dot_rhs_t(qx[pl.ds(base, TILE), :], kx[pl.ds(base, span), :])
        r = lax.broadcasted_iota(jnp.int32, (TILE, span), 0)
        u = lax.broadcasted_iota(jnp.int32, (TILE, span), 1)
        ok = (u > r) & (u <= r + WINDOW) & (base + u + m * 2 * rows >= WINDOW)
        p = softmax(s, ok)
        attn[b, tile_at(i), :] = dot(p, vx[pl.ds(base, span), :])

    def attn_to(i):
        at = slice(i * TILE, (i + 1) * TILE)
        return remote(attn_out.at[at], attn_in.at[at], a_s.at[i], a_r.at[i], seq=partner)

    def attention_out(i):
        attn_out[i * TILE:(i + 1) * TILE, :] = attn[oc, i * TILE:(i + 1) * TILE, :].astype(BF16)
        start(attn_to(i))

    def squares(x):
        x = x.astype(F32)
        return jnp.sum(x * x, axis=0, keepdims=True)

    def set_ratio(i):
        j, h = chunks[i]
        old = ratio_out[j:j + 1, halves(h)]
        ratio_out[j:j + 1, halves(h)] = old / jnp.sqrt(squares(u_all(i)) + EPS)

    def hidden_two(h, i):
        at = slice(i * WIDE, (i + 1) * WIDE)
        a = dot(qx[at, :], u_all(2 * h)) * ratio_out[0:1, halves(h)]
        g = dot(qx[at, :], u_all(2 * h + 1)) * ratio_out[1:2, halves(h)]
        h2[at, halves(h)] = (a * jax.nn.sigmoid(a) * g).astype(BF16)

    def f_copy(i, h):
        at = tile_at(i)
        return remote(
            f_out.at[at, halves(h)], f_in.at[at, halves(h)],
            f_s.at[h, i], f_r.at[h, i], seq=partner,
        )

    def apply_tile(b, i, h):
        ht = h2[pl.ds(pl.multiple_of(b * rows + i * TILE, TILE), TILE), :]
        f = dot(ht, u_all(4 + h)) * ratio_out[2:3, halves(h)]
        part = as_row(jnp.sum(f * f, axis=1, keepdims=True))
        where = 0 if b is c else 1
        if h == 0:
            sq[where, :, tile_at(i)] = part
        else:
            sq[where, :, tile_at(i)] = sq[where, :, tile_at(i)] + part
        return f

    def apply_out(h):
        @pl.loop(0, tiles)
        def _(i):
            f_out[tile_at(i), halves(h)] = apply_tile(oc, i, h).astype(BF16)
            f_copy(i, h).start()

    def apply_own(h):
        @pl.loop(0, tiles)
        def _(i):
            branch[tile_at(i), halves(h)] = apply_tile(c, i, h)

    start(x_w)
    start(x_k)
    start(x_e)
    for copy in x_v:
        start(copy)
    start(x_q)
    for j in range(3):
        gather_send(j, 1)

    @pl.when(m == 0)
    def _():
        for x in (kx, vx):
            x[:WINDOW, :] = jnp.zeros((WINDOW, hd), BF16)

    for copy in loads[3:]:
        copy.wait()
    with scope("b_xw"):
        x_w.wait_recv()
    for j in range(3):
        gather_send(3 + j, 1)
    local_early = jnp.logical_and(jnp.logical_and(c == 1, m == 0), has_next)
    local_late = jnp.logical_and(jnp.logical_and(c == 1, m > 0), has_next)
    passed = jnp.logical_and(c == 0, has_next)
    for copy in [halo_k] + halo_v:
        start(copy, local_early)
    with scope("b_relay"):
        for s in range(2, line):
            for j in range(3):
                gather_send(j, s)
                gather_send(3 + j, s)
    for copy in [halo_k] + halo_v:
        start(copy, local_late)
    with scope("b_xk"):
        x_k.wait_recv()
    start(halo_k, passed)
    with scope("b_kt"):
        kt[...] = jnp.transpose(kx[WINDOW:, :])
    with scope("b_w13"):
        for j in range(2):
            gather_finish(j)
            gather_finish(3 + j)
    with scope("b_fwd_own"):
        forward(c)
    with scope("b_fwd_oc"):
        forward(oc)
    scaled_values(c)
    for j in range(2):
        ratio_out[j:j + 1] = jnp.sqrt(squares(wg[j].reshape(n * shard, hd)))
    with scope("b_w2"):
        gather_finish(2)
        gather_finish(5)
    with scope("b_bwd_own"):
        for h in range(2):
            backward(c, h)
        ratio_out[2:3] = jnp.sqrt(squares(wg[2].reshape(n * shard, hd)))
    with scope("b_xv"):
        x_e.wait_recv()
        for i in range(tiles):
            x_v[i].wait_recv()
            start(halo_v[i], passed)
    with scope("b_bwd_oc"):
        scaled_values(oc)
        for h in range(2):
            backward(oc, h)

    with scope("prods"):
        for i in range(6):
            product(i)
            for r in range(parts):
                sum_first(i, r)

    def halo_wait():
        for copy in [halo_k] + halo_v:
            wait(copy, has_prev)

    tasks = (
        [lambda: pl.when(c == 0)(x_q.wait_recv)]
        + [lambda i=i: local_attention(1, i) for i in range(tiles)]
        + [lambda: pl.when(c == 1)(x_q.wait_recv), halo_wait]
        + [lambda i=i: local_attention(0, i) for i in range(tiles)]
        + [lambda i=i: attention_out(i) for i in range(tiles)]
    )
    done = []

    def task():
        if tasks:
            with scope("task%d" % len(done)):
                tasks.pop(0)()
            done.append(0)

    def finished(i):
        set_ratio(i)
        start(x_g[i])
        if i == 1 or i == 3:
            for b in range(2 * rows // WIDE):
                tasks.append(lambda b=b: hidden_two(i // 2, b))

    pieces = [(i, r) for i in range(6) for r in range(parts)]
    for p in range(len(pieces) + LAG):
        with scope("p%d" % p):
            if p < len(pieces):
                sum_on(*pieces[p])
            if p >= LAG:
                sum_back(*pieces[p - LAG])
        if p >= LAG:
            i, r = pieces[p - LAG]
            if r == parts - 1:
                finished(i)
            if i == 4 and r == parts - 1:
                while tasks:
                    task()
                with scope("apply0"):
                    apply_out(0)
                    apply_own(0)
        if p >= FIRST:
            task()

    with scope("t_out"):
        start(x_n)
        apply_out(1)
    mine = []
    for d in range(hn):
        slot = hn - 1 + d
        mine.append(
            remote(
                sq.at[1], sq_in.at[slot], sq_s.at[slot], sq_r.at[slot],
                seq=partner, head=lax.rem(hme + d, hn),
            )
        )
    for copy in mine:
        copy.start()
    with scope("t_own"):
        apply_own(1)
    for d in range(1, hn):
        copy = remote(
            sq.at[0], sq_in.at[d - 1], sq_s.at[d - 1], sq_r.at[d - 1],
            head=lax.rem(hme + d, hn),
        )
        copy.start()
        mine.append(copy)
    with scope("t_outs"):
        x_n.wait_recv()
        for copy in x_g:
            copy.wait_recv()
        for i, (j, h) in enumerate(chunks):
            out = (o1, o3, o2)[j]
            at = halves(h)
            out[c, :, at] = ug[i, m, c].astype(F32) * ratio_out[j:j + 1, at]
            out[oc, :, at] = g_in[i].astype(F32) * ratio_in[j:j + 1, at]
    with scope("t_sends"):
        for copy, when in pending:
            if when is None:
                copy.wait_send()
            else:
                pl.when(when)(copy.wait_send)
    with scope("t_sq"):
        total = sq[0]
        for copy in mine:
            copy.wait_recv()
        for slot in range(2 * hn - 1):
            total = total + sq_in[slot]
        for copy in mine:
            copy.wait_send()
        sq[0] = lax.rsqrt(total * (1.0 / (hn * width)) + EPS)

    with scope("t_mix_own"):

        @pl.loop(0, tiles)
        def _(i):
            at = tile_at(i)
            inv = column(sq[0, 0:1, at])[:, :1]
            own_part = branch[at, :] * inv * gain_in[:, lanes(c)]
            mixed[at, lanes(c)] = (attn[c, at, :] + own_part).astype(BF16)

    with scope("t_mix_oc"):
        for i in range(tiles):
            attn_to(i).wait_recv()

        @pl.loop(0, tiles)
        def _(i):
            at = tile_at(i)
            for h in range(2):
                f_copy(i, h).wait_recv()
                f_copy(i, h).wait_send()
            inv = column(sq[0, 0:1, at])[:, :1]
            other = f_in[at, :].astype(F32) * inv * gain_in[:, lanes(oc)]
            mixed[at, lanes(oc)] = (attn_in[at, :].astype(F32) + other).astype(BF16)


def local(n, hn, queries, keys, values, rate, fast_gate, fast_up, fast_down, out_gain):
    rows, width = queries.shape
    heads, shard, hd = fast_gate.shape
    line = n // 2
    half = hd // 2
    tiles = rows // TILE
    sums = (6, line, 2, shard, half)
    dma = pltpu.SemaphoreType.DMA
    vmem = pl.BlockSpec(memory_space=pltpu.VMEM)
    hbm = pl.BlockSpec(memory_space=pltpu.HBM)
    return pl.pallas_call(
        functools.partial(kernel, n, hn),
        out_shape=(
            jax.ShapeDtypeStruct((rows, width), BF16),
            jax.ShapeDtypeStruct(fast_gate.shape, F32),
            jax.ShapeDtypeStruct(fast_up.shape, F32),
            jax.ShapeDtypeStruct(fast_down.shape, F32),
        ),
        in_specs=[hbm] * 8,
        out_specs=(vmem,) * 4,
        scratch_shapes=[
            pltpu.VMEM((3, 2, shard, hd), F32),
            pltpu.VMEM(rate.shape, F32),
            pltpu.VMEM((1, width), F32),
            pltpu.VMEM((3, line, 2, shard, hd), BF16),
            pltpu.VMEM(sums, BF16),
            pltpu.VMEM(sums, F32),
            pltpu.VMEM(sums, BF16),
            pltpu.VMEM(sums, BF16),
            pltpu.VMEM(sums, BF16),
            pltpu.VMEM((3, shard, hd), BF16),
            pltpu.VMEM((6, shard, half), BF16),
            pltpu.VMEM((8, hd), F32),
            pltpu.VMEM((8, hd), F32),
            pltpu.VMEM((2 * rows, hd), BF16),
            pltpu.VMEM((WINDOW + 2 * rows, hd), BF16),
            pltpu.VMEM((WINDOW + 2 * rows, hd), BF16),
            pltpu.VMEM((hd, 2 * rows), BF16),
            pltpu.VMEM(rate.shape, F32),
            pltpu.VMEM((2 * rows, hd), BF16),
            pltpu.VMEM((2 * rows, hd), BF16),
            pltpu.VMEM((2, 2 * rows, hd), BF16),
            pltpu.VMEM((2, 2 * rows, hd), F32),
            pltpu.VMEM((2, rows, hd), F32),
            pltpu.VMEM((rows, hd), BF16),
            pltpu.VMEM((rows, hd), BF16),
            pltpu.VMEM((2 * rows, hd), BF16),
            pltpu.VMEM((rows, hd), F32),
            pltpu.VMEM((rows, hd), BF16),
            pltpu.VMEM((rows, hd), BF16),
            pltpu.VMEM((2, 8, rows), F32),
            pltpu.VMEM((2 * hn - 1, 8, rows), F32),
        ]
        + [dma((2, 6, line - 1))] * 2
        + [dma((6, math.gcd(PARTS, line)))] * 6
        + [dma((8,))]
        + [dma((5,))] * 2
        + [dma((tiles,))] * 2
        + [dma((1 + WINDOW // TILE,))] * 2
        + [dma((6,))] * 2
        + [dma((tiles,))] * 2
        + [dma((2, tiles))] * 2
        + [dma((2 * hn - 1,))] * 2,
        compiler_params=pltpu.CompilerParams(
            collective_id=0, has_side_effects=True, vmem_limit_bytes=60 * 1024 * 1024
        ),
        name="ttt_layer",
    )(queries, keys, values, rate, out_gain.reshape(1, width), fast_gate, fast_up, fast_down)


def solution(mesh):
    weights = P("head", "seq", None)
    tokens = P("seq", "head")
    return jax.shard_map(
        functools.partial(local, mesh.shape["seq"], mesh.shape["head"]),
        mesh=mesh,
        in_specs=(tokens, tokens, tokens, P("head", "seq"), weights, weights, weights, P("head")),
        out_specs=(tokens, weights, weights, weights),
        check_vma=False,
    )
```

```python
import functools
import math

import jax
import jax.numpy as jnp
from jax import lax
from jax.experimental import pallas as pl
from jax.experimental.pallas import tpu as pltpu
from jax.sharding import PartitionSpec as P

WINDOW = 512
EPS = 1e-06
TILE = 128
WIDE = 256
LAG = 3
FIRST = 1
PARTS = 4
NONE = -1e30
MESH = pl.DeviceIdType.MESH
F32 = jnp.float32
BF16 = jnp.bfloat16
scope = jax.named_scope


def dot(a, b):
    return jnp.dot(a, b, preferred_element_type=F32)


def dot_lhs_t(a, b):
    return lax.dot_general(a, b, (((0,), (0,)), ((), ())), preferred_element_type=F32)


def dot_rhs_t(a, b):
    return lax.dot_general(a, b, (((1,), (1,)), ((), ())), preferred_element_type=F32)


def kernel(
    n, hn,
    q, k, v, rate, gain, w1, w3, w2,
    mixed_to, o1_to, o3_to, o2_to,
    mixed, o_all, w_in, rate_in, gain_in, wg, ug_a, ug_b, pg_a, pg_b, out_a, out_b, in_a, in_b, ex_a, ex_b, wb_out, gi_a, gi_b,
    ratio_out, ratio_in, qx, kx, vx, kt, eta_x, gv, hid, dab, pre, attn,
    attn_out, attn_in, h2, branch, f_out, f_in, sq, sq_in,
    ag_s, ag_r, in_r, back_r, l_s, x_s, x_r, k_r, v_r, halo_r, one_s, g_r,
):
    rows, width = q.shape
    heads, shard, hd = w1.shape
    half = hd // 2
    line = n // 2
    tiles = rows // TILE
    me = lax.axis_index("seq")
    hme = lax.axis_index("head")
    m = lax.div(me, 2)
    c = lax.rem(me, 2)
    oc = 1 - c
    partner = 2 * m + oc
    step_to = (1, -1)
    quarter = hd // 4
    chunks = [
        (j, slice(h * half, (h + 1) * half)) for h in range(2) for j in range(2)
    ] + [(2, slice(h * quarter, (h + 1) * quarter)) for h in range(4)]
    sends = {
        name: one_s.at[i]
        for i, name in enumerate(
            ("in_a", "in_b", "out_a", "out_b", "k", "v", "hk", "hv", "g_a", "g_b", "a", "ar",
             "f", "fr", "q", "qr", "mixed", "new")
        )
    }
    us, pgs = (ug_a, ug_b), (pg_a, pg_b)
    outs, ins, exs, gis = (out_a, out_b), (in_a, in_b), (ex_a, ex_b), (gi_a, gi_b)
    middle = line // 2

    def parts(i):
        return math.gcd(PARTS if i < 4 else PARTS // 2, line)

    def chunk(bufs, i):
        return bufs[0].at[i] if i < 4 else bufs[1].at[i - 4]

    def part(bufs, i, r):
        deep = line // parts(i)
        return chunk(bufs, i).at[r * deep:(r + 1) * deep]

    left = m < middle
    inward = jnp.where(left, 1, -1)
    edge = jnp.where(left, m, line - 1 - m)
    inner = edge == middle - 1

    def seq_at(b):
        return 2 * lax.rem(b + line, line) + c

    def lanes(i):
        return pl.ds(pl.multiple_of(i * hd, hd), hd)

    def block(i):
        return pl.ds(pl.multiple_of(i * rows, rows), rows)

    def after_pad(i):
        return pl.ds(pl.multiple_of(WINDOW + i * rows, TILE), rows)

    def tile_at(i):
        return pl.ds(pl.multiple_of(i * TILE, TILE), TILE)

    def halves(h):
        return slice(h * half, (h + 1) * half)

    barrier = pltpu.get_barrier_semaphore()
    for s in (partner, seq_at(m + 1), seq_at(m - 1)):
        pl.semaphore_signal(barrier, inc=1, device_id={"seq": s}, device_id_type=MESH)
    for d in range(1, hn):
        peer = lax.rem(hme + d, hn)
        for s in (me, partner):
            pl.semaphore_signal(
                barrier, inc=1, device_id={"seq": s, "head": peer}, device_id_type=MESH
            )

    loads = [
        pltpu.make_async_copy(src, dst, l_s.at[i])
        for i, (src, dst) in enumerate(
            (
                (w1, w_in.at[0]), (w3, w_in.at[1]), (w2, w_in.at[2]),
                (k.at[:, lanes(c)], kx.at[after_pad(c)]),
                (v.at[:, lanes(c)], vx.at[after_pad(c)]),
                (q.at[:, lanes(c)], qx.at[block(c)]),
                (rate, rate_in), (gain, gain_in),
            )
        )
    ]
    for copy in loads:
        copy.start()
    with scope("a_load"):
        for j in range(3):
            loads[j].wait()
            wg[j, m, c] = w_in[j, c].astype(BF16)
            wb_out[j] = w_in[j, oc].astype(BF16)
    with scope("a_barrier"):
        pl.semaphore_wait(barrier, 3 + 2 * (hn - 1))

    pending = []

    def start(copy, when=None, alone=True):
        if when is None:
            copy.start()
        else:
            pl.when(when)(copy.start)
        if alone:
            pending.append((copy, when))

    def wait(copy, when):
        pl.when(when)(copy.wait_recv)

    def remote(src, dst, ss, rr, **where):
        return pltpu.make_async_remote_copy(
            src_ref=src, dst_ref=dst, send_sem=ss, recv_sem=rr,
            device_id=where, device_id_type=MESH,
        )

    def group(ref, ss, rr):
        return remote(ref, ref, ss, rr, seq=partner)

    def to_partner(i, src, dst):
        return remote(src, dst, x_s.at[i], x_r.at[i], seq=partner)

    x_w = to_partner(0, wb_out, wg.at[:, m, c])
    def token_copies(src, dst, name, rr):
        return [
            remote(
                src.at[i * TILE:(i + 1) * TILE, lanes(oc)],
                dst.at[pl.ds(pl.multiple_of(WINDOW + c * rows + i * TILE, TILE), TILE)],
                sends[name], rr.at[i], seq=partner,
            )
            for i in range(tiles)
        ]

    x_k = token_copies(k, kx, "k", k_r)
    x_v = token_copies(v, vx, "v", v_r)
    x_e = to_partner(1, rate, eta_x)
    x_q = to_partner(2, q.at[:, lanes(oc)], qx.at[block(c)])
    x_n = to_partner(3, ratio_out, ratio_in)
    x_g = [
        remote(
            chunk(us, i).at[m, oc], chunk(gis, i), sends["g_a" if i < 4 else "g_b"],
            g_r.at[0 if i < 4 else 1], seq=partner,
        )
        for i in range(8)
    ]
    has_next = m < line - 1
    has_prev = m > 0

    def halo(x, i, base):
        return remote(
            x.at[2 * rows + i * TILE:2 * rows + (i + 1) * TILE],
            x.at[i * TILE:(i + 1) * TILE],
            sends["hv" if base else "hk"], halo_r.at[base + i], seq=seq_at(m + 1),
        )

    halo_k = [halo(kx, i, 0) for i in range(WINDOW // TILE)]
    halo_v = [halo(vx, i, WINDOW // TILE) for i in range(WINDOW // TILE)]

    def link(ss, rr, src, dst, d, i, s):
        return remote(
            src, dst, ss.at[d, s - 1], rr.at[d, i, s - 1], seq=seq_at(m + step_to[d])
        )

    def ahead(d):
        return line - 1 - m if d == 0 else m

    def w_piece(i, b):
        return wg.at[i % 3, b, c if i < 3 else oc]

    def gather_copy(i, d, s):
        b = lax.rem(m - step_to[d] * (s - 1) + line, line)
        return link(ag_s, ag_r, w_piece(i, b), w_piece(i, b), d, i, s)

    def gather_arrived(i, d, s, passing):
        b = lax.rem(m - step_to[d] * s + line, line)
        onward = ahead(d) >= 1 if passing else ahead(d) == 0
        wait(
            link(ag_s, ag_r, w_piece(i, b), w_piece(i, b), d, i, s),
            jnp.logical_and(ahead(1 - d) >= s, onward),
        )

    def gather_send(i, s):
        for d in range(2):
            if s > 1:
                gather_arrived(i, d, s - 1, True)
            start(
                gather_copy(i, d, s),
                jnp.logical_and(ahead(d) >= 1, ahead(1 - d) >= s - 1), False,
            )

    def gather_finish(i):
        for d in range(2):
            for s in range(1, line):
                gather_arrived(i, d, s, False)

    def number(i, r):
        return sum(parts(t) for t in range(i)) + r

    def inward_copy(i, r, across):
        return remote(
            part(outs, i, r), part(exs if across else ins, i, r),
            sends["in_a" if i < 4 else "in_b"], (back_r if across else in_r).at[number(i, r)],
            seq=seq_at(m + inward),
        )

    def outward_copy(i, r):
        piece = part(us, i, r)
        return remote(
            piece, piece, sends["out_a" if i < 4 else "out_b"], back_r.at[number(i, r)],
            seq=seq_at(m - inward),
        )

    def sum_first(i, r):
        @pl.when(edge == 0)
        def _():
            part(outs, i, r)[...] = part(pgs, i, r)[...].astype(BF16)

        start(inward_copy(i, r, False), jnp.logical_and(edge == 0, jnp.logical_not(inner)), False)
        start(inward_copy(i, r, True), jnp.logical_and(edge == 0, inner), False)

    def sum_on(i, r):
        @pl.when(edge > 0)
        def _():
            inward_copy(i, r, False).wait_recv()
            total = part(pgs, i, r)[...] + part(ins, i, r)[...].astype(F32)
            part(pgs, i, r)[...] = total
            part(outs, i, r)[...] = total.astype(BF16)

        start(inward_copy(i, r, False), jnp.logical_and(edge > 0, jnp.logical_not(inner)), False)
        start(inward_copy(i, r, True), jnp.logical_and(edge > 0, inner), False)

    def sum_back(i, r):
        j, cols = chunks[i]
        deep = line // parts(i)

        @pl.when(inner)
        def _():
            inward_copy(i, r, True).wait_recv()
            total = part(pgs, i, r)[...] + part(exs, i, r)[...].astype(F32)
            old = wg[j, r * deep:(r + 1) * deep, :, :, cols].astype(F32)
            part(us, i, r)[...] = (total + old).astype(BF16)

        wait(outward_copy(i, r), jnp.logical_not(inner))
        start(outward_copy(i, r), edge > 0, False)

    def column(row):
        return jnp.transpose(jnp.broadcast_to(row, (TILE, row.shape[1])))

    def as_row(col):
        return jnp.transpose(jnp.broadcast_to(col, (col.shape[0], TILE)))[:8]

    def w_cols(j, h):
        return wg[j, :, :, :, halves(h)].reshape(n * shard, half)

    def w_rows(j, h):
        return wg[j].reshape(n * shard, hd)[halves(h)]

    def u_all(i):
        u = chunk(us, i)[...]
        return u.reshape(n * shard, u.shape[-1])

    def forward(b):
        for h in range(2):

            @pl.loop(0, rows // WIDE)
            def _(i):
                at = pl.ds(pl.multiple_of(b * rows + i * WIDE, WIDE), WIDE)
                kt = kx[pl.ds(pl.multiple_of(WINDOW + b * rows + i * WIDE, WIDE), WIDE), :]
                a = dot(kt, w_cols(0, h))
                up = dot(kt, w_cols(1, h))
                g = jax.nn.sigmoid(a)
                ag = a * g
                hid[at, halves(h)] = (ag * up).astype(BF16)
                pre[0, at, halves(h)] = up * g * (1.0 + a * (1.0 - g))
                pre[1, at, halves(h)] = ag

    def scaled_values(b):
        eta = column((rate_in if b is c else eta_x)[pl.ds(c, 1), :])[:, :1]
        vb = vx[after_pad(b), :]
        gv[block(b), :] = (eta * vb.astype(F32)).astype(BF16)

    def backward(b, h):
        @pl.loop(0, rows // WIDE)
        def _(i):
            at = pl.ds(pl.multiple_of(b * rows + i * WIDE, WIDE), WIDE)
            back = dot_rhs_t(gv[at, :], w_rows(2, h))
            dab[h, at, halves(0)] = (back * pre[0, at, halves(h)]).astype(BF16)
            dab[h, at, halves(1)] = (back * pre[1, at, halves(h)]).astype(BF16)

    def product(h):
        g = dot(kt[...], dab[h]) if h < 2 else dot_lhs_t(hid[...], gv[...])
        for i, at in ((2 * h, 0), (2 * h + 1, half)) if h < 2 else zip(
            range(4, 8), range(0, hd, quarter)
        ):
            dst = chunk(pgs, i)
            dst[...] = g[:, at:at + dst.shape[-1]].reshape(dst.shape)

    def softmax(s, ok):
        s = jnp.where(ok, s * (1.0 / math.sqrt(hd)), NONE)
        top = jnp.max(s, axis=1, keepdims=True)
        e = jnp.exp(s - top)
        total = jnp.sum(e, axis=1, keepdims=True)
        return (e * (1.0 / total)).astype(BF16)

    def local_attention(b, i):
        span = WINDOW + TILE
        base = pl.multiple_of(b * rows + i * TILE, TILE)
        s = dot_rhs_t(qx[pl.ds(base, TILE), :], kx[pl.ds(base, span), :])
        r = lax.broadcasted_iota(jnp.int32, (TILE, span), 0)
        u = lax.broadcasted_iota(jnp.int32, (TILE, span), 1)
        ok = (u > r) & (u <= r + WINDOW) & (base + u + m * 2 * rows >= WINDOW)
        p = softmax(s, ok)
        attn[b, tile_at(i), :] = dot(p, vx[pl.ds(base, span), :])

    def attn_to(i):
        at = slice(i * TILE, (i + 1) * TILE)
        return remote(attn_out.at[at], attn_in.at[at], sends["a"], sends["ar"], seq=partner)

    def attention_out(i):
        attn_out[i * TILE:(i + 1) * TILE, :] = attn[oc, i * TILE:(i + 1) * TILE, :].astype(BF16)
        attn_to(i).start()

    def squares(x):
        x = x.astype(F32)
        return jnp.sum(x * x, axis=0, keepdims=True)

    def set_ratio(i):
        j, cols = chunks[i]
        old = ratio_out[j:j + 1, cols]
        ratio_out[j:j + 1, cols] = old / jnp.sqrt(squares(u_all(i)) + EPS)

    def hidden_two(h, i):
        at = slice(i * WIDE, (i + 1) * WIDE)
        a = dot(qx[at, :], u_all(2 * h)) * ratio_out[0:1, halves(h)]
        g = dot(qx[at, :], u_all(2 * h + 1)) * ratio_out[1:2, halves(h)]
        h2[at, halves(h)] = (a * jax.nn.sigmoid(a) * g).astype(BF16)

    def wide_at(i):
        return pl.ds(pl.multiple_of(i * WIDE, WIDE), WIDE)

    def f_copy(i, h):
        piece = (wide_at(i), chunks[4 + h][1])
        return remote(f_out.at[piece], f_in.at[piece], sends["f"], sends["fr"], seq=partner)

    def apply_tile(b, i, h):
        ht = h2[pl.ds(pl.multiple_of(b * rows + i * WIDE, WIDE), WIDE), :]
        f = dot(ht, u_all(4 + h)) * ratio_out[2:3, chunks[4 + h][1]]
        squared = as_row(jnp.sum(f * f, axis=1, keepdims=True))
        where = 0 if b is c else 1
        if h == 0:
            sq[where, :, wide_at(i)] = squared
        else:
            sq[where, :, wide_at(i)] = sq[where, :, wide_at(i)] + squared
        return f

    def apply_out(h):
        for i in range(rows // WIDE):
            f_out[wide_at(i), chunks[4 + h][1]] = apply_tile(oc, i, h).astype(BF16)
            f_copy(i, h).start()

    def apply_own(h):
        for i in range(rows // WIDE):
            branch[wide_at(i), chunks[4 + h][1]] = apply_tile(c, i, h)

    start(x_w)
    for copy in x_k:
        copy.start()
    start(x_e)
    for copy in x_v:
        copy.start()
    start(x_q)
    for j in range(3):
        gather_send(j, 1)

    @pl.when(m == 0)
    def _():
        for x in (kx, vx):
            x[:WINDOW, :] = jnp.zeros((WINDOW, hd), BF16)

    for copy in loads[3:]:
        copy.wait()
    with scope("b_relay0"):
        if line > 2:
            for j in range(3):
                gather_send(j, 2)
    with scope("b_xw"):
        x_w.wait_recv()
    for j in range(3):
        gather_send(3 + j, 1)
    with_next = functools.partial(jnp.logical_and, has_next)
    local_early = with_next(jnp.logical_and(c == 1, m == 0))
    local_late = with_next(jnp.logical_and(c == 1, m > 0))
    passed = with_next(c == 0)
    for copy in halo_k + halo_v:
        start(copy, local_early, False)

    def pass_keys(when):
        for i in range(tiles):
            wait(x_k[i], when)
            start(halo_k[i], jnp.logical_and(passed, when), False)

    def pass_value(i):
        with scope("b_xv"):
            x_v[i].wait_recv()
        start(halo_v[i], passed, False)

    pass_keys(m == 0)
    with scope("b_relay"):
        if line > 2:
            for j in range(3):
                gather_send(3 + j, 2)
        for s in range(3, line):
            for j in range(3):
                gather_send(j, s)
                gather_send(3 + j, s)
    for copy in halo_k + halo_v:
        start(copy, local_late, False)
    with scope("b_xk"):
        pass_keys(m > 0)
    with scope("b_kt"):
        kt[...] = jnp.transpose(kx[WINDOW:, :])
    for i in range(tiles // 2):
        pass_value(i)
    with scope("b_w13"):
        for j in range(2):
            gather_finish(j)
            gather_finish(3 + j)
    with scope("b_fwd_own"):
        forward(c)
    for i in range(tiles // 2, tiles - 1):
        pass_value(i)
    with scope("b_fwd_oc"):
        forward(oc)
    scaled_values(c)
    for j in range(2):
        ratio_out[j:j + 1] = jnp.sqrt(squares(wg[j].reshape(n * shard, hd)))
    with scope("b_w2"):
        gather_finish(2)
        gather_finish(5)
    with scope("b_bwd_own"):
        for h in range(2):
            backward(c, h)
        ratio_out[2:3] = jnp.sqrt(squares(wg[2].reshape(n * shard, hd)))
    x_e.wait_recv()
    pass_value(tiles - 1)
    with scope("b_bwd_oc"):
        scaled_values(oc)
        for h in range(2):
            backward(oc, h)

    for h in range(3):
        with scope("prod%d" % h):
            product(h)
        for i in ((0, 1), (2, 3), (4, 5, 6, 7))[h]:
            for r in range(parts(i)):
                sum_first(i, r)

    def halo_wait():
        for copy in halo_k + halo_v:
            wait(copy, has_prev)

    tasks = (
        [lambda: pl.when(c == 0)(x_q.wait_recv)]
        + [lambda i=i: local_attention(1, i) for i in range(tiles)]
        + [lambda: pl.when(c == 1)(x_q.wait_recv), halo_wait]
        + [lambda i=i: local_attention(0, i) for i in range(tiles)]
        + [lambda i=i: attention_out(i) for i in range(tiles)]
    )
    done = []

    def task():
        if tasks:
            with scope("task%d" % len(done)):
                tasks.pop(0)()
            done.append(0)

    def finished(i):
        set_ratio(i)
        x_g[i].start()
        if i == 1 or i == 3:
            for b in range(2 * rows // WIDE):
                tasks.append(lambda b=b: hidden_two(i // 2, b))

    pieces = [(i, r) for i in range(8) for r in range(parts(i))]
    for p in range(len(pieces) + LAG):
        with scope("p%d" % p):
            if p < len(pieces):
                sum_on(*pieces[p])
            if p >= LAG:
                sum_back(*pieces[p - LAG])
        if p >= LAG:
            i, r = pieces[p - LAG]
            if r == parts(i) - 1:
                finished(i)
                if 4 <= i < 7:
                    while tasks:
                        task()
                    with scope("apply%d" % i):
                        apply_out(i - 4)
                        apply_own(i - 4)
        if p >= FIRST:
            task()

    with scope("t_out"):
        start(x_n)
        apply_out(3)
    mine = []
    for d in range(hn):
        slot = hn - 1 + d
        mine.append(
            remote(
                sq.at[1], sq_in.at[slot], sends["q"], sends["qr"],
                seq=partner, head=lax.rem(hme + d, hn),
            )
        )
    for copy in mine:
        copy.start()
    with scope("t_own"):
        apply_own(3)
    for d in range(1, hn):
        copy = remote(
            sq.at[0], sq_in.at[d - 1], sends["q"], sends["qr"],
            head=lax.rem(hme + d, hn),
        )
        copy.start()
        mine.append(copy)
    with scope("t_outs"):
        x_n.wait_recv()
        for t in range(2):
            group(gis[t], g_r.at[t], g_r.at[t]).wait_recv()
        for i, (j, cols) in enumerate(chunks):
            out = o_all.at[j]
            new = chunk(us, i)[m, c].astype(F32) * ratio_out[j:j + 1, cols]
            out[c, :, cols] = new
            other = chunk(gis, i)[...].astype(F32) * ratio_in[j:j + 1, cols]
            out[oc, :, cols] = other
    stores = [
        pltpu.make_async_copy(o_all.at[j], out, sends["new"])
        for j, out in enumerate((o1_to, o3_to, o2_to))
    ]
    for copy in stores:
        copy.start()
    with scope("t_sends"):
        for copy, when in pending:
            if when is None:
                copy.wait_send()
            else:
                pl.when(when)(copy.wait_send)

        def sent(ref, name, when=None):
            copy = group(ref, sends[name] if isinstance(name, str) else name, sends["ar"])
            if when is None:
                copy.wait_send()
            else:
                pl.when(when)(copy.wait_send)

        for d in range(2):
            for s in range(1, line):
                sent(
                    wg.at[:, 0], ag_s.at[d, s - 1],
                    jnp.logical_and(ahead(d) >= 1, ahead(1 - d) >= s - 1),
                )
        for t, name in enumerate(("a", "b")):
            sent(outs[t], "in_" + name)
            sent(us[t], "out_" + name, edge > 0)
            sent(gis[t], "g_" + name)
        sent(attn_out, "k")
        sent(attn_out, "v")
        sent(kx.at[:WINDOW], "hk", has_next)
        sent(vx.at[:WINDOW], "hv", has_next)
        sent(attn_out, "a")
        sent(f_out, "f")
    with scope("t_sq"):
        total = sq[0]
        group(sq_in, sends["q"], sends["qr"]).wait_recv()
        for slot in range(2 * hn - 1):
            total = total + sq_in[slot]
        group(sq_in, sends["q"], sends["qr"]).wait_send()
        sq[0] = lax.rsqrt(total * (1.0 / (hn * width)) + EPS)

    def tile_store(i, b):
        piece = (tile_at(i), lanes(b))
        return pltpu.make_async_copy(mixed.at[piece], mixed_to.at[piece], sends["mixed"])

    with scope("t_mix"):
        for i in range(tiles):
            at = tile_at(i)
            inv = column(sq[0, 0:1, i * TILE:(i + 1) * TILE])[:, :1]
            own_part = branch[at, :] * inv * gain_in[:, lanes(c)]
            mixed[at, lanes(c)] = (attn[c, at, :] + own_part).astype(BF16)
            tile_store(i, c).start()
            if i == 0:
                group(attn_in, sends["a"], sends["ar"]).wait_recv()
                group(f_in, sends["f"], sends["fr"]).wait_recv()
            other = f_in[at, :].astype(F32) * inv * gain_in[:, lanes(oc)]
            mixed[at, lanes(oc)] = (attn_in[at, :].astype(F32) + other).astype(BF16)
            tile_store(i, oc).start()
    with scope("t_stores"):
        pltpu.make_async_copy(o_all, o_all, sends["new"]).wait()
        pltpu.make_async_copy(mixed, mixed_to, sends["mixed"]).wait()


def store(*refs):
    sems = refs[-1]
    copies = [pltpu.make_async_copy(refs[i], refs[4 + i], sems.at[i]) for i in range(4)]
    for copy in copies:
        copy.start()
    for copy in copies:
        copy.wait()


def local(n, hn, queries, keys, values, rate, fast_gate, fast_up, fast_down, out_gain):
    rows, width = queries.shape
    heads, shard, hd = fast_gate.shape
    line = n // 2
    half = hd // 2
    tiles = rows // TILE
    sums = (4, line, 2, shard, half)
    sums_b = (4, line, 2, shard, hd // 4)
    dma = pltpu.SemaphoreType.DMA
    vmem = pl.BlockSpec(memory_space=pltpu.VMEM)
    hbm = pl.BlockSpec(memory_space=pltpu.HBM)
    results = pl.pallas_call(
        functools.partial(kernel, n, hn),
        out_shape=(
            pltpu.VMEM((rows, width), BF16),
            pltpu.VMEM(fast_gate.shape, F32),
            pltpu.VMEM(fast_up.shape, F32),
            pltpu.VMEM(fast_down.shape, F32),
        ),
        in_specs=[hbm] * 8,
        out_specs=(pl.BlockSpec(memory_space=pl.ANY),) * 4,
        scratch_shapes=[
            pltpu.VMEM((rows, width), BF16),
            pltpu.VMEM((3,) + fast_gate.shape, F32),
            pltpu.VMEM((3, 2, shard, hd), F32),
            pltpu.VMEM(rate.shape, F32),
            pltpu.VMEM((1, width), F32),
            pltpu.VMEM((3, line, 2, shard, hd), BF16),
            pltpu.VMEM(sums, BF16),
            pltpu.VMEM(sums_b, BF16),
            pltpu.VMEM(sums, F32),
            pltpu.VMEM(sums_b, F32),
            pltpu.VMEM(sums, BF16),
            pltpu.VMEM(sums_b, BF16),
            pltpu.VMEM(sums, BF16),
            pltpu.VMEM(sums_b, BF16),
            pltpu.VMEM(sums, BF16),
            pltpu.VMEM(sums_b, BF16),
            pltpu.VMEM((3, shard, hd), BF16),
            pltpu.VMEM((4, shard, half), BF16),
            pltpu.VMEM((4, shard, hd // 4), BF16),
            pltpu.VMEM((8, hd), F32),
            pltpu.VMEM((8, hd), F32),
            pltpu.VMEM((2 * rows, hd), BF16),
            pltpu.VMEM((WINDOW + 2 * rows, hd), BF16),
            pltpu.VMEM((WINDOW + 2 * rows, hd), BF16),
            pltpu.VMEM((hd, 2 * rows), BF16),
            pltpu.VMEM(rate.shape, F32),
            pltpu.VMEM((2 * rows, hd), BF16),
            pltpu.VMEM((2 * rows, hd), BF16),
            pltpu.VMEM((2, 2 * rows, hd), BF16),
            pltpu.VMEM((2, 2 * rows, hd), F32),
            pltpu.VMEM((2, rows, hd), F32),
            pltpu.VMEM((rows, hd), BF16),
            pltpu.VMEM((rows, hd), BF16),
            pltpu.VMEM((2 * rows, hd), BF16),
            pltpu.VMEM((rows, hd), F32),
            pltpu.VMEM((rows, hd), BF16),
            pltpu.VMEM((rows, hd), BF16),
            pltpu.VMEM((2, 8, rows), F32),
            pltpu.VMEM((2 * hn - 1, 8, rows), F32),
        ]
        + [dma((2, line - 1)), dma((2, 6, line - 1))]
        + [dma((4 * math.gcd(PARTS, line) + 4 * math.gcd(PARTS // 2, line),))] * 2
        + [dma((8,)), dma((4,)), dma((4,)), dma((tiles,)), dma((tiles,))]
        + [dma((2 * WINDOW // TILE,)), dma((18,)), dma((2,))],
        compiler_params=pltpu.CompilerParams(
            collective_id=0, has_side_effects=True, vmem_limit_bytes=42 * 1024 * 1024
        ),
        name="ttt_layer",
    )(
        *(
            pltpu.with_memory_space_constraint(x, pltpu.HBM)
            for x in (
                queries, keys, values, rate, out_gain.reshape(1, width),
                fast_gate, fast_up, fast_down,
            )
        )
    )
    return pl.pallas_call(
        store,
        out_shape=tuple(jax.ShapeDtypeStruct(x.shape, x.dtype) for x in results),
        in_specs=[vmem] * 4,
        out_specs=(hbm,) * 4,
        scratch_shapes=[dma((4,))],
        compiler_params=pltpu.CompilerParams(vmem_limit_bytes=1024 * 1024),
        name="store",
    )(*results)


def solution(mesh):
    weights = P("head", "seq", None)
    tokens = P("seq", "head")
    return jax.shard_map(
        functools.partial(local, mesh.shape["seq"], mesh.shape["head"]),
        mesh=mesh,
        in_specs=(tokens, tokens, tokens, P("head", "seq"), weights, weights, weights, P("head")),
        out_specs=(tokens, weights, weights, weights),
        check_vma=False,
    )
```

```python
import functools
import math

import jax
import jax.numpy as jnp
from jax import lax
from jax.experimental import pallas as pl
from jax.experimental.pallas import tpu as pltpu
from jax.sharding import PartitionSpec as P

WINDOW = 512
EPS = 1e-06
TILE = 128
WIDE = 256
LAG = 3
FIRST = 2
PARTS = 4
BACK = 2
NONE = -1e30
MESH = pl.DeviceIdType.MESH
F32 = jnp.float32
BF16 = jnp.bfloat16
scope = jax.named_scope


def dot(a, b):
    return jnp.dot(a, b, preferred_element_type=F32)


def dot_lhs_t(a, b):
    return lax.dot_general(a, b, (((0,), (0,)), ((), ())), preferred_element_type=F32)


def dot_rhs_t(a, b):
    return lax.dot_general(a, b, (((1,), (1,)), ((), ())), preferred_element_type=F32)


def kernel(
    n, hn,
    q, k, v, rate, gain, w1, w3, w2,
    mixed_to, o1_to, o3_to, o2_to,
    mixed, o_all, w_in, rate_in, gain_in, wg, ug_a, ug_b, pg_a, pg_b, out_a, out_b, in_a, in_b, ex_a, ex_b, wb_out, gi_a, gi_b,
    ratio_out, ratio_in, qx, kx, vx, kt, eta_x, gv, hid, dab, pre, attn,
    lse, qn, part_out, part_in, lse_out, lse_in,
    attn_out, attn_in, h2, branch, f_out, f_in, sq, sq_in,
    ag_s, ag_r, in_r, back_r, l_s, x_s, x_r, k_r, v_r, halo_r, q_r, qb_r, pt_r, one_s, g_r,
):
    rows, width = q.shape
    heads, shard, hd = w1.shape
    half = hd // 2
    line = n // 2
    tiles = rows // TILE
    me = lax.axis_index("seq")
    hme = lax.axis_index("head")
    m = lax.div(me, 2)
    c = lax.rem(me, 2)
    oc = 1 - c
    partner = 2 * m + oc
    step_to = (1, -1)
    quarter = hd // 4
    chunks = [
        (j, slice(h * half, (h + 1) * half)) for h in range(2) for j in range(2)
    ] + [(2, slice(h * quarter, (h + 1) * quarter)) for h in range(4)]
    sends = {
        name: one_s.at[i]
        for i, name in enumerate(
            ("in_a", "in_b", "out_a", "out_b", "k", "v", "hk", "hv", "g_a", "g_b", "a", "ar",
             "f", "fr", "q", "qr", "mixed", "new", "xq", "qb", "pt", "pl")
        )
    }
    us, pgs = (ug_a, ug_b), (pg_a, pg_b)
    outs, ins, exs, gis = (out_a, out_b), (in_a, in_b), (ex_a, ex_b), (gi_a, gi_b)
    middle = line // 2

    def parts(i):
        return math.gcd(PARTS if i < 4 else PARTS // 2, line)

    def chunk(bufs, i):
        return bufs[0].at[i] if i < 4 else bufs[1].at[i - 4]

    def part(bufs, i, r):
        deep = line // parts(i)
        return chunk(bufs, i).at[r * deep:(r + 1) * deep]

    left = m < middle
    inward = jnp.where(left, 1, -1)
    edge = jnp.where(left, m, line - 1 - m)
    inner = edge == middle - 1

    def seq_at(b):
        return 2 * lax.rem(b + line, line) + c

    def lanes(i):
        return pl.ds(pl.multiple_of(i * hd, hd), hd)

    def block(i):
        return pl.ds(pl.multiple_of(i * rows, rows), rows)

    def after_pad(i):
        return pl.ds(pl.multiple_of(WINDOW + i * rows, TILE), rows)

    def tile_at(i):
        return pl.ds(pl.multiple_of(i * TILE, TILE), TILE)

    def halves(h):
        return slice(h * half, (h + 1) * half)

    barrier = pltpu.get_barrier_semaphore()
    for s in (partner, seq_at(m + 1), seq_at(m - 1)):
        pl.semaphore_signal(barrier, inc=1, device_id={"seq": s}, device_id_type=MESH)
    for d in range(1, hn):
        peer = lax.rem(hme + d, hn)
        for s in (me, partner):
            pl.semaphore_signal(
                barrier, inc=1, device_id={"seq": s, "head": peer}, device_id_type=MESH
            )

    loads = [
        pltpu.make_async_copy(src, dst, l_s.at[i])
        for i, (src, dst) in enumerate(
            (
                (w1, w_in.at[0]), (w3, w_in.at[1]), (w2, w_in.at[2]),
                (k.at[:, lanes(c)], kx.at[after_pad(c)]),
                (v.at[:, lanes(c)], vx.at[after_pad(c)]),
                (q.at[:, lanes(c)], qx.at[block(c)]),
                (rate, rate_in), (gain, gain_in),
            )
        )
    ]
    for copy in loads:
        copy.start()
    with scope("a_load"):
        for j in range(3):
            loads[j].wait()
            wg[j, m, c] = w_in[j, c].astype(BF16)
            wb_out[j] = w_in[j, oc].astype(BF16)
    with scope("a_barrier"):
        pl.semaphore_wait(barrier, 3 + 2 * (hn - 1))

    pending = []

    def start(copy, when=None, alone=True):
        if when is None:
            copy.start()
        else:
            pl.when(when)(copy.start)
        if alone:
            pending.append((copy, when))

    def wait(copy, when):
        pl.when(when)(copy.wait_recv)

    def remote(src, dst, ss, rr, **where):
        return pltpu.make_async_remote_copy(
            src_ref=src, dst_ref=dst, send_sem=ss, recv_sem=rr,
            device_id=where, device_id_type=MESH,
        )

    def group(ref, ss, rr):
        return remote(ref, ref, ss, rr, seq=partner)

    def to_partner(i, src, dst):
        return remote(src, dst, x_s.at[i], x_r.at[i], seq=partner)

    x_w = to_partner(0, wb_out, wg.at[:, m, c])
    def token_copies(src, dst, name, rr):
        return [
            remote(
                src.at[i * TILE:(i + 1) * TILE, lanes(oc)],
                dst.at[pl.ds(pl.multiple_of(WINDOW + c * rows + i * TILE, TILE), TILE)],
                sends[name], rr.at[i], seq=partner,
            )
            for i in range(tiles)
        ]

    x_k = token_copies(k, kx, "k", k_r)
    x_v = token_copies(v, vx, "v", v_r)
    x_e = to_partner(1, rate, eta_x)
    x_q = [
        remote(
            q.at[i * TILE:(i + 1) * TILE, lanes(oc)],
            qx.at[pl.ds(pl.multiple_of(c * rows + i * TILE, TILE), TILE)],
            sends["xq"], q_r.at[i], seq=partner,
        )
        for i in range(tiles)
    ]
    x_n = to_partner(3, ratio_out, ratio_in)
    x_g = [
        remote(
            chunk(us, i).at[m, oc], chunk(gis, i), sends["g_a" if i < 4 else "g_b"],
            g_r.at[0 if i < 4 else 1], seq=partner,
        )
        for i in range(8)
    ]
    has_next = m < line - 1
    has_prev = m > 0
    asks = jnp.logical_and(has_prev, m >= middle)
    answers = jnp.logical_and(has_next, m + 1 >= middle)
    to_other = jnp.logical_and(has_next, jnp.logical_not(answers))
    takes_all = jnp.logical_and(has_prev, jnp.logical_not(asks))

    def halo(x, i, base):
        return remote(
            x.at[2 * rows + i * TILE:2 * rows + (i + 1) * TILE],
            x.at[i * TILE:(i + 1) * TILE],
            sends["hv" if base else "hk"], halo_r.at[base + i], seq=seq_at(m + 1),
        )

    halo_k = [halo(kx, i, 0) for i in range(tiles)]
    halo_v = [halo(vx, i, tiles) for i in range(tiles)]
    back = BACK * TILE

    def back_tile(i):
        return slice(i * TILE, (i + 1) * TILE)

    q_back = [
        remote(
            qx.at[back_tile(i)], qn.at[back_tile(i)], sends["qb"], qb_r.at[i], seq=seq_at(m - 1)
        )
        for i in range(BACK)
    ]
    part_on = [
        remote(
            part_out.at[back_tile(i)], part_in.at[back_tile(i)], sends["pt"], pt_r.at[i],
            seq=seq_at(m + 1),
        )
        for i in range(BACK)
    ]
    lse_on = remote(lse_out, lse_in, sends["pl"], pt_r.at[BACK], seq=seq_at(m + 1))

    def link(ss, rr, src, dst, d, i, s):
        return remote(
            src, dst, ss.at[d, s - 1], rr.at[d, i, s - 1], seq=seq_at(m + step_to[d])
        )

    def ahead(d):
        return line - 1 - m if d == 0 else m

    def w_piece(i, b):
        return wg.at[i % 3, b, c if i < 3 else oc]

    def gather_copy(i, d, s):
        b = lax.rem(m - step_to[d] * (s - 1) + line, line)
        return link(ag_s, ag_r, w_piece(i, b), w_piece(i, b), d, i, s)

    def gather_arrived(i, d, s, passing):
        b = lax.rem(m - step_to[d] * s + line, line)
        onward = ahead(d) >= 1 if passing else ahead(d) == 0
        wait(
            link(ag_s, ag_r, w_piece(i, b), w_piece(i, b), d, i, s),
            jnp.logical_and(ahead(1 - d) >= s, onward),
        )

    def gather_send(i, s):
        for d in range(2):
            if s > 1:
                gather_arrived(i, d, s - 1, True)
            start(
                gather_copy(i, d, s),
                jnp.logical_and(ahead(d) >= 1, ahead(1 - d) >= s - 1), False,
            )

    def gather_finish(i):
        for d in range(2):
            for s in range(1, line):
                gather_arrived(i, d, s, False)

    def number(i, r):
        return sum(parts(t) for t in range(i)) + r

    def inward_copy(i, r, across):
        return remote(
            part(outs, i, r), part(exs if across else ins, i, r),
            sends["in_a" if i < 4 else "in_b"], (back_r if across else in_r).at[number(i, r)],
            seq=seq_at(m + inward),
        )

    def outward_copy(i, r):
        piece = part(us, i, r)
        return remote(
            piece, piece, sends["out_a" if i < 4 else "out_b"], back_r.at[number(i, r)],
            seq=seq_at(m - inward),
        )

    def sum_first(i, r):
        @pl.when(edge == 0)
        def _():
            part(outs, i, r)[...] = part(pgs, i, r)[...].astype(BF16)

        start(inward_copy(i, r, False), jnp.logical_and(edge == 0, jnp.logical_not(inner)), False)
        start(inward_copy(i, r, True), jnp.logical_and(edge == 0, inner), False)

    def sum_on(i, r):
        @pl.when(edge > 0)
        def _():
            inward_copy(i, r, False).wait_recv()
            total = part(pgs, i, r)[...] + part(ins, i, r)[...].astype(F32)
            part(pgs, i, r)[...] = total
            part(outs, i, r)[...] = total.astype(BF16)

        start(inward_copy(i, r, False), jnp.logical_and(edge > 0, jnp.logical_not(inner)), False)
        start(inward_copy(i, r, True), jnp.logical_and(edge > 0, inner), False)

    def sum_back(i, r):
        j, cols = chunks[i]
        deep = line // parts(i)

        @pl.when(inner)
        def _():
            inward_copy(i, r, True).wait_recv()
            total = part(pgs, i, r)[...] + part(exs, i, r)[...].astype(F32)
            old = wg[j, r * deep:(r + 1) * deep, :, :, cols].astype(F32)
            part(us, i, r)[...] = (total + old).astype(BF16)

        wait(outward_copy(i, r), jnp.logical_not(inner))
        start(outward_copy(i, r), edge > 0, False)

    def column(row):
        return jnp.transpose(jnp.broadcast_to(row, (TILE, row.shape[1])))

    def as_row(col):
        return jnp.transpose(jnp.broadcast_to(col, (col.shape[0], TILE)))[:8]

    def w_cols(j, h):
        return wg[j, :, :, :, halves(h)].reshape(n * shard, half)

    def w_rows(j, h):
        return wg[j].reshape(n * shard, hd)[halves(h)]

    def u_all(i):
        u = chunk(us, i)[...]
        return u.reshape(n * shard, u.shape[-1])

    def forward(b):
        for h in range(2):

            @pl.loop(0, rows // WIDE)
            def _(i):
                at = pl.ds(pl.multiple_of(b * rows + i * WIDE, WIDE), WIDE)
                kt = kx[pl.ds(pl.multiple_of(WINDOW + b * rows + i * WIDE, WIDE), WIDE), :]
                a = dot(kt, w_cols(0, h))
                up = dot(kt, w_cols(1, h))
                g = jax.nn.sigmoid(a)
                ag = a * g
                hid[at, halves(h)] = (ag * up).astype(BF16)
                pre[0, at, halves(h)] = up * g * (1.0 + a * (1.0 - g))
                pre[1, at, halves(h)] = ag

    def scaled_values(b):
        eta = column((rate_in if b is c else eta_x)[pl.ds(c, 1), :])[:, :1]
        vb = vx[after_pad(b), :]
        gv[block(b), :] = (eta * vb.astype(F32)).astype(BF16)

    def backward(b, h):
        @pl.loop(0, rows // WIDE)
        def _(i):
            at = pl.ds(pl.multiple_of(b * rows + i * WIDE, WIDE), WIDE)
            back = dot_rhs_t(gv[at, :], w_rows(2, h))
            dab[h, at, halves(0)] = (back * pre[0, at, halves(h)]).astype(BF16)
            dab[h, at, halves(1)] = (back * pre[1, at, halves(h)]).astype(BF16)

    def product(h):
        g = dot(kt[...], dab[h]) if h < 2 else dot_lhs_t(hid[...], gv[...])
        for i, at in ((2 * h, 0), (2 * h + 1, half)) if h < 2 else zip(
            range(4, 8), range(0, hd, quarter)
        ):
            dst = chunk(pgs, i)
            dst[...] = g[:, at:at + dst.shape[-1]].reshape(dst.shape)

    def softmax(s, ok):
        s = jnp.where(ok, s * (1.0 / math.sqrt(hd)), NONE)
        top = jnp.max(s, axis=1, keepdims=True)
        e = jnp.exp(s - top)
        total = jnp.sum(e, axis=1, keepdims=True)
        return (e * (1.0 / total)).astype(BF16), top + jnp.log(total)

    first_key = jnp.where(m == 0, WINDOW, jnp.where(asks, back, 0))

    def local_attention(b, i):
        span = WINDOW + TILE
        base = pl.multiple_of(b * rows + i * TILE, TILE)
        s = dot_rhs_t(qx[pl.ds(base, TILE), :], kx[pl.ds(base, span), :])
        r = lax.broadcasted_iota(jnp.int32, (TILE, span), 0)
        u = lax.broadcasted_iota(jnp.int32, (TILE, span), 1)
        ok = (u > r) & (u <= r + WINDOW) & (base + u >= first_key)
        p, stat = softmax(s, ok)
        attn[b, tile_at(i), :] = dot(p, vx[pl.ds(base, span), :])
        if b == 0 and i < BACK:
            lse[back_tile(i), :] = jnp.broadcast_to(stat, (TILE, TILE))

    def next_attention(i):
        keys = slice(WINDOW + rows + i * TILE, WINDOW + rows + back)
        span = back - i * TILE

        @pl.when(answers)
        def _():
            q_back[i].wait_recv()
            s = dot_rhs_t(qn[back_tile(i), :], kx[keys, :])
            r = lax.broadcasted_iota(jnp.int32, (TILE, span), 0)
            u = lax.broadcasted_iota(jnp.int32, (TILE, span), 1)
            p, stat = softmax(s, u > r)
            stat = jnp.where(lax.broadcasted_iota(jnp.int32, stat.shape, 0) < span - 1, stat, NONE)
            part_out[back_tile(i), :] = dot(p, vx[keys, :]).astype(BF16)
            lse_out[:, back_tile(i)] = as_row(stat)

        if i == BACK - 1:
            start(lse_on, answers)
        start(part_on[i], answers, False)

    def combine(i):
        at = back_tile(i)

        @pl.when(asks)
        def _():
            if i == 0:
                lse_on.wait_recv()
            part_on[i].wait_recv()
            here = lse[at, :1]
            before = column(lse_in[0:1, at])[:, :1]
            keep = jax.nn.sigmoid(here - before)
            attn[0, at, :] = keep * attn[0, at, :] + (1.0 - keep) * part_in[at, :].astype(F32)

    def attn_to(i):
        at = slice(i * TILE, (i + 1) * TILE)
        return remote(attn_out.at[at], attn_in.at[at], sends["a"], sends["ar"], seq=partner)

    def attention_out(when, some):
        @pl.when(when)
        def _():
            for i in some:
                at = slice(i * TILE, (i + 1) * TILE)
                attn_out[at, :] = attn[oc, at, :].astype(BF16)
                attn_to(i).start()

    def squares(x):
        x = x.astype(F32)
        return jnp.sum(x * x, axis=0, keepdims=True)

    def set_ratio(i):
        j, cols = chunks[i]
        old = ratio_out[j:j + 1, cols]
        ratio_out[j:j + 1, cols] = old / jnp.sqrt(squares(u_all(i)) + EPS)

    def hidden_two(h, i):
        at = slice(i * WIDE, (i + 1) * WIDE)
        a = dot(qx[at, :], u_all(2 * h)) * ratio_out[0:1, halves(h)]
        g = dot(qx[at, :], u_all(2 * h + 1)) * ratio_out[1:2, halves(h)]
        h2[at, halves(h)] = (a * jax.nn.sigmoid(a) * g).astype(BF16)

    def wide_at(i):
        return pl.ds(pl.multiple_of(i * WIDE, WIDE), WIDE)

    def f_copy(i, h):
        piece = (wide_at(i), chunks[4 + h][1])
        return remote(f_out.at[piece], f_in.at[piece], sends["f"], sends["fr"], seq=partner)

    def apply_tile(b, i, h):
        ht = h2[pl.ds(pl.multiple_of(b * rows + i * WIDE, WIDE), WIDE), :]
        f = dot(ht, u_all(4 + h)) * ratio_out[2:3, chunks[4 + h][1]]
        squared = as_row(jnp.sum(f * f, axis=1, keepdims=True))
        where = 0 if b is c else 1
        if h == 0:
            sq[where, :, wide_at(i)] = squared
        else:
            sq[where, :, wide_at(i)] = sq[where, :, wide_at(i)] + squared
        return f

    def apply_out(h):
        for i in range(rows // WIDE):
            f_out[wide_at(i), chunks[4 + h][1]] = apply_tile(oc, i, h).astype(BF16)
            f_copy(i, h).start()

    def apply_own(h):
        for i in range(rows // WIDE):
            branch[wide_at(i), chunks[4 + h][1]] = apply_tile(c, i, h)

    start(x_w)
    for copy in x_k:
        copy.start()
    start(x_e)
    soon = jnp.logical_and(c == 0, asks)
    for i in range(BACK):
        start(x_q[i], soon, False)
    for copy in x_v:
        copy.start()
    for i in range(tiles):
        if i < BACK:
            start(x_q[i], jnp.logical_not(soon), False)
        else:
            x_q[i].start()
    for j in range(3):
        gather_send(j, 1)

    @pl.when(asks)
    def _():
        for x in (kx, vx):
            x[:back, :] = jnp.zeros((back, hd), BF16)

    @pl.when(m == 0)
    def _():
        for x in (kx, vx):
            x[:WINDOW, :] = jnp.zeros((WINDOW, hd), BF16)

    for copy in loads[3:]:
        copy.wait()
    with scope("b_relay0"):
        if line > 2:
            for j in range(3):
                gather_send(j, 2)
    with scope("b_xw"):
        x_w.wait_recv()
    for j in range(3):
        gather_send(3 + j, 1)
    def forward_halo(copies, i, when):
        sent_on = to_other if i < BACK else has_next
        start(copies[i], jnp.logical_and(sent_on, when), False)

    for i in range(2 * tiles):
        forward_halo((halo_k, halo_v)[i // tiles], i % tiles, jnp.logical_and(c == 1, m == 0))

    def pass_keys(when):
        for i in range(tiles):
            wait(x_k[i], when)
            forward_halo(halo_k, i, jnp.logical_and(c == 0, when))

    def pass_value(i):
        with scope("b_xv"):
            x_v[i].wait_recv()
        forward_halo(halo_v, i, c == 0)

    pass_keys(m == 0)
    with scope("b_relay"):
        if line > 2:
            for j in range(3):
                gather_send(3 + j, 2)
        for s in range(3, line):
            for j in range(3):
                gather_send(j, s)
                gather_send(3 + j, s)
    for i in range(2 * tiles):
        forward_halo((halo_k, halo_v)[i // tiles], i % tiles, jnp.logical_and(c == 1, m > 0))
    for copy in q_back:
        start(copy, jnp.logical_and(c == 0, asks), False)
    with scope("b_xk"):
        pass_keys(m > 0)
    def tokens_in(when, some):
        for i in some:
            wait(x_q[i], when)

    with scope("b_qb"):
        ask = jnp.logical_and(c == 1, asks)
        tokens_in(ask, range(BACK))
        for copy in q_back:
            start(copy, ask, False)
    with scope("b_kt"):
        kt[...] = jnp.transpose(kx[WINDOW:, :])
    for i in range(tiles // 2):
        pass_value(i)
    with scope("b_w13"):
        for j in range(2):
            gather_finish(j)
            gather_finish(3 + j)
    with scope("b_fwd_own"):
        forward(c)
    for i in range(tiles // 2, tiles - 1):
        pass_value(i)
    with scope("b_fwd_oc"):
        forward(oc)
    scaled_values(c)
    for j in range(2):
        ratio_out[j:j + 1] = jnp.sqrt(squares(wg[j].reshape(n * shard, hd)))
    with scope("b_w2"):
        gather_finish(2)
        gather_finish(5)
    with scope("b_bwd_own"):
        for h in range(2):
            backward(c, h)
        ratio_out[2:3] = jnp.sqrt(squares(wg[2].reshape(n * shard, hd)))
    x_e.wait_recv()
    pass_value(tiles - 1)
    with scope("b_bwd_oc"):
        scaled_values(oc)
        for h in range(2):
            backward(oc, h)

    for h in range(3):
        with scope("prod%d" % h):
            product(h)
        for i in ((0, 1), (2, 3), (4, 5, 6, 7))[h]:
            for r in range(parts(i)):
                sum_first(i, r)

    def halo_wait():
        for i in range(tiles):
            for copies in (halo_k, halo_v):
                wait(
                    copies[i],
                    takes_all if i < BACK else has_prev,
                )

    def first_tokens():
        tokens_in(c == 0, range(tiles))

    def rest_tokens():
        tokens_in(jnp.logical_and(c == 1, jnp.logical_not(asks)), range(BACK))
        tokens_in(c == 1, range(BACK, tiles))
        halo_wait()

    def attend(b, i):
        return lambda: local_attention(b, i)

    ones = [attend(1, i) for i in range(tiles)]
    zeros = [attend(0, i) for i in range(BACK, tiles)] + [attend(0, i) for i in range(BACK)]
    tasks = (
        [lambda: (first_tokens(), ones[0]())]
        + ones[1:]
        + [lambda: (attention_out(c == 0, range(tiles)), rest_tokens(), zeros[0]())]
        + zeros[1:]
        + [lambda: attention_out(c == 1, range(BACK, tiles))]
        + [lambda i=i: combine(i) for i in range(BACK)]
        + [lambda: attention_out(c == 1, range(BACK))]
    )
    done = []
    with scope("b_next"):
        for i in range(BACK):
            next_attention(i)

    def task():
        if tasks:
            with scope("task%d" % len(done)):
                tasks.pop(0)()
            done.append(0)

    def finished(i):
        set_ratio(i)
        x_g[i].start()
        if i == 1 or i == 3:
            for b in range(2 * rows // WIDE):
                tasks.append(lambda b=b: hidden_two(i // 2, b))

    pieces = [(i, r) for i in range(8) for r in range(parts(i))]
    for p in range(len(pieces) + LAG):
        with scope("p%d" % p):
            if p < len(pieces):
                sum_on(*pieces[p])
            if p >= LAG:
                sum_back(*pieces[p - LAG])
        if p >= LAG:
            i, r = pieces[p - LAG]
            if r == parts(i) - 1:
                finished(i)
                if 4 <= i < 7:
                    while tasks:
                        task()
                    with scope("apply%d" % i):
                        apply_out(i - 4)
                        apply_own(i - 4)
        for _ in range(0 if p < FIRST else 1 if p < len(pieces) - LAG * 2 else 2):
            task()

    with scope("t_out"):
        start(x_n)
        apply_out(3)
    mine = []
    for d in range(hn):
        slot = hn - 1 + d
        mine.append(
            remote(
                sq.at[1], sq_in.at[slot], sends["q"], sends["qr"],
                seq=partner, head=lax.rem(hme + d, hn),
            )
        )
    for copy in mine:
        copy.start()
    with scope("t_own"):
        apply_own(3)
    for d in range(1, hn):
        copy = remote(
            sq.at[0], sq_in.at[d - 1], sends["q"], sends["qr"],
            head=lax.rem(hme + d, hn),
        )
        copy.start()
        mine.append(copy)
    with scope("t_outs"):
        x_n.wait_recv()
        for t in range(2):
            group(gis[t], g_r.at[t], g_r.at[t]).wait_recv()
        for i, (j, cols) in enumerate(chunks):
            out = o_all.at[j]
            new = chunk(us, i)[m, c].astype(F32) * ratio_out[j:j + 1, cols]
            out[c, :, cols] = new
            other = chunk(gis, i)[...].astype(F32) * ratio_in[j:j + 1, cols]
            out[oc, :, cols] = other
    stores = [
        pltpu.make_async_copy(o_all.at[j], out, sends["new"])
        for j, out in enumerate((o1_to, o3_to, o2_to))
    ]
    for copy in stores:
        copy.start()
    with scope("t_sends"):
        for copy, when in pending:
            if when is None:
                copy.wait_send()
            else:
                pl.when(when)(copy.wait_send)

        def sent(ref, name, when=None):
            copy = group(ref, sends[name] if isinstance(name, str) else name, sends["ar"])
            if when is None:
                copy.wait_send()
            else:
                pl.when(when)(copy.wait_send)

        for d in range(2):
            for s in range(1, line):
                sent(
                    wg.at[:, 0], ag_s.at[d, s - 1],
                    jnp.logical_and(ahead(d) >= 1, ahead(1 - d) >= s - 1),
                )
        for t, name in enumerate(("a", "b")):
            sent(outs[t], "in_" + name)
            sent(us[t], "out_" + name, edge > 0)
            sent(gis[t], "g_" + name)
        sent(attn_out, "k")
        sent(attn_out, "v")
        sent(attn_out, "xq")
        for x, name in ((kx, "hk"), (vx, "hv")):
            sent(x.at[:WINDOW], name, to_other)
            sent(x.at[back:WINDOW], name, answers)
        sent(part_out, "pt", answers)
        sent(qn, "qb", asks)
        sent(attn_out, "a")
        sent(f_out, "f")
    with scope("t_sq"):
        total = sq[0]
        group(sq_in, sends["q"], sends["qr"]).wait_recv()
        for slot in range(2 * hn - 1):
            total = total + sq_in[slot]
        group(sq_in, sends["q"], sends["qr"]).wait_send()
        sq[0] = lax.rsqrt(total * (1.0 / (hn * width)) + EPS)

    def tile_store(i, b):
        piece = (tile_at(i), lanes(b))
        return pltpu.make_async_copy(mixed.at[piece], mixed_to.at[piece], sends["mixed"])

    with scope("t_mix"):
        for i in range(tiles):
            at = tile_at(i)
            inv = column(sq[0, 0:1, i * TILE:(i + 1) * TILE])[:, :1]
            own_part = branch[at, :] * inv * gain_in[:, lanes(c)]
            mixed[at, lanes(c)] = (attn[c, at, :] + own_part).astype(BF16)
            tile_store(i, c).start()
            if i == 0:
                group(attn_in, sends["a"], sends["ar"]).wait_recv()
                group(f_in, sends["f"], sends["fr"]).wait_recv()
            other = f_in[at, :].astype(F32) * inv * gain_in[:, lanes(oc)]
            mixed[at, lanes(oc)] = (attn_in[at, :].astype(F32) + other).astype(BF16)
            tile_store(i, oc).start()
    with scope("t_stores"):
        pltpu.make_async_copy(o_all, o_all, sends["new"]).wait()
        pltpu.make_async_copy(mixed, mixed_to, sends["mixed"]).wait()


def store(*refs):
    sems = refs[-1]
    copies = [pltpu.make_async_copy(refs[i], refs[4 + i], sems.at[i]) for i in range(4)]
    for copy in copies:
        copy.start()
    for copy in copies:
        copy.wait()


def local(n, hn, queries, keys, values, rate, fast_gate, fast_up, fast_down, out_gain):
    rows, width = queries.shape
    heads, shard, hd = fast_gate.shape
    line = n // 2
    half = hd // 2
    tiles = rows // TILE
    sums = (4, line, 2, shard, half)
    sums_b = (4, line, 2, shard, hd // 4)
    dma = pltpu.SemaphoreType.DMA
    vmem = pl.BlockSpec(memory_space=pltpu.VMEM)
    hbm = pl.BlockSpec(memory_space=pltpu.HBM)
    results = pl.pallas_call(
        functools.partial(kernel, n, hn),
        out_shape=(
            pltpu.VMEM((rows, width), BF16),
            pltpu.VMEM(fast_gate.shape, F32),
            pltpu.VMEM(fast_up.shape, F32),
            pltpu.VMEM(fast_down.shape, F32),
        ),
        in_specs=[hbm] * 8,
        out_specs=(pl.BlockSpec(memory_space=pl.ANY),) * 4,
        scratch_shapes=[
            pltpu.VMEM((rows, width), BF16),
            pltpu.VMEM((3,) + fast_gate.shape, F32),
            pltpu.VMEM((3, 2, shard, hd), F32),
            pltpu.VMEM(rate.shape, F32),
            pltpu.VMEM((1, width), F32),
            pltpu.VMEM((3, line, 2, shard, hd), BF16),
            pltpu.VMEM(sums, BF16),
            pltpu.VMEM(sums_b, BF16),
            pltpu.VMEM(sums, F32),
            pltpu.VMEM(sums_b, F32),
            pltpu.VMEM(sums, BF16),
            pltpu.VMEM(sums_b, BF16),
            pltpu.VMEM(sums, BF16),
            pltpu.VMEM(sums_b, BF16),
            pltpu.VMEM(sums, BF16),
            pltpu.VMEM(sums_b, BF16),
            pltpu.VMEM((3, shard, hd), BF16),
            pltpu.VMEM((4, shard, half), BF16),
            pltpu.VMEM((4, shard, hd // 4), BF16),
            pltpu.VMEM((8, hd), F32),
            pltpu.VMEM((8, hd), F32),
            pltpu.VMEM((2 * rows, hd), BF16),
            pltpu.VMEM((WINDOW + 2 * rows, hd), BF16),
            pltpu.VMEM((WINDOW + 2 * rows, hd), BF16),
            pltpu.VMEM((hd, 2 * rows), BF16),
            pltpu.VMEM(rate.shape, F32),
            pltpu.VMEM((2 * rows, hd), BF16),
            pltpu.VMEM((2 * rows, hd), BF16),
            pltpu.VMEM((2, 2 * rows, hd), BF16),
            pltpu.VMEM((2, 2 * rows, hd), F32),
            pltpu.VMEM((2, rows, hd), F32),
            pltpu.VMEM((BACK * TILE, TILE), F32),
            pltpu.VMEM((BACK * TILE, hd), BF16),
            pltpu.VMEM((BACK * TILE, hd), BF16),
            pltpu.VMEM((BACK * TILE, hd), BF16),
            pltpu.VMEM((8, BACK * TILE), F32),
            pltpu.VMEM((8, BACK * TILE), F32),
            pltpu.VMEM((rows, hd), BF16),
            pltpu.VMEM((rows, hd), BF16),
            pltpu.VMEM((2 * rows, hd), BF16),
            pltpu.VMEM((rows, hd), F32),
            pltpu.VMEM((rows, hd), BF16),
            pltpu.VMEM((rows, hd), BF16),
            pltpu.VMEM((2, 8, rows), F32),
            pltpu.VMEM((2 * hn - 1, 8, rows), F32),
        ]
        + [dma((2, line - 1)), dma((2, 6, line - 1))]
        + [dma((4 * math.gcd(PARTS, line) + 4 * math.gcd(PARTS // 2, line),))] * 2
        + [dma((8,)), dma((4,)), dma((4,)), dma((tiles,)), dma((tiles,))]
        + [dma((2 * WINDOW // TILE,)), dma((tiles,)), dma((BACK,)), dma((BACK + 1,))]
        + [dma((22,)), dma((2,))],
        compiler_params=pltpu.CompilerParams(
            collective_id=0, has_side_effects=True, vmem_limit_bytes=42 * 1024 * 1024
        ),
        name="ttt_layer",
    )(
        *(
            pltpu.with_memory_space_constraint(x, pltpu.HBM)
            for x in (
                queries, keys, values, rate, out_gain.reshape(1, width),
                fast_gate, fast_up, fast_down,
            )
        )
    )
    return pl.pallas_call(
        store,
        out_shape=tuple(jax.ShapeDtypeStruct(x.shape, x.dtype) for x in results),
        in_specs=[vmem] * 4,
        out_specs=(hbm,) * 4,
        scratch_shapes=[dma((4,))],
        compiler_params=pltpu.CompilerParams(vmem_limit_bytes=1024 * 1024),
        name="store",
    )(*results)


def solution(mesh):
    weights = P("head", "seq", None)
    tokens = P("seq", "head")
    return jax.shard_map(
        functools.partial(local, mesh.shape["seq"], mesh.shape["head"]),
        mesh=mesh,
        in_specs=(tokens, tokens, tokens, P("head", "seq"), weights, weights, weights, P("head")),
        out_specs=(tokens, weights, weights, weights),
        check_vma=False,
    )
```

```python
import functools
import math

import jax
import jax.numpy as jnp
from jax import lax
from jax.experimental import pallas as pl
from jax.experimental.pallas import tpu as pltpu
from jax.sharding import PartitionSpec as P

WINDOW = 512
EPS = 1e-06
TILE = 128
WIDE = 256
LAG = 3
FIRST = 2
PARTS = 4
BACK = 2
NONE = -1e30
MESH = pl.DeviceIdType.MESH
F32 = jnp.float32
BF16 = jnp.bfloat16
scope = jax.named_scope


def dot(a, b):
    return jnp.dot(a, b, preferred_element_type=F32)


def dot_lhs_t(a, b):
    return lax.dot_general(a, b, (((0,), (0,)), ((), ())), preferred_element_type=F32)


def dot_rhs_t(a, b):
    return lax.dot_general(a, b, (((1,), (1,)), ((), ())), preferred_element_type=F32)


def kernel(
    n, hn,
    q, k, v, rate, gain, w1, w3, w2,
    mixed_to, o1_to, o3_to, o2_to,
    mixed, o_all, w_in, rate_in, gain_in, wg, ug_a, ug_b, pg_a, pg_b, out_a, out_b, in_a, in_b, ex_a, ex_b, wb_out, gi_a, gi_b,
    ratio_out, ratio_in, qx, kx, vx, kt, eta_x, gv, hid, dab, pre, attn,
    inv_all, lse, qn, part_out, part_in, lse_out, lse_in,
    attn_out, attn_in, h2, branch, f_out, f_in, sq, sq_in,
    ag_s, ag_r, in_r, back_r, l_s, x_s, x_r, k_r, v_r, halo_r, q_r, qb_r, pt_r, one_s, g_r,
):
    rows, width = q.shape
    heads, shard, hd = w1.shape
    half = hd // 2
    line = n // 2
    tiles = rows // TILE
    me = lax.axis_index("seq")
    hme = lax.axis_index("head")
    m = lax.div(me, 2)
    c = lax.rem(me, 2)
    oc = 1 - c
    partner = 2 * m + oc
    step_to = (1, -1)
    quarter = hd // 4
    chunks = [
        (j, slice(h * half, (h + 1) * half)) for h in range(2) for j in range(2)
    ] + [(2, slice(h * quarter, (h + 1) * quarter)) for h in range(4)]
    sends = {
        name: one_s.at[i]
        for i, name in enumerate(
            ("in_a", "in_b", "out_a", "out_b", "k", "v", "hk", "hv", "g_a", "g_b", "a", "ar",
             "f", "fr", "q", "qr", "mixed", "new", "xq", "qb", "pt", "pl",
             "fr_last")
        )
    }
    us, pgs = (ug_a, ug_b), (pg_a, pg_b)
    outs, ins, exs, gis = (out_a, out_b), (in_a, in_b), (ex_a, ex_b), (gi_a, gi_b)
    middle = line // 2

    def parts(i):
        return math.gcd(PARTS if i < 4 else PARTS // 2, line)

    def chunk(bufs, i):
        return bufs[0].at[i] if i < 4 else bufs[1].at[i - 4]

    def part(bufs, i, r):
        deep = line // parts(i)
        return chunk(bufs, i).at[r * deep:(r + 1) * deep]

    left = m < middle
    inward = jnp.where(left, 1, -1)
    edge = jnp.where(left, m, line - 1 - m)
    inner = edge == middle - 1

    def seq_at(b):
        return 2 * lax.rem(b + line, line) + c

    def lanes(i):
        return pl.ds(pl.multiple_of(i * hd, hd), hd)

    def block(i):
        return pl.ds(pl.multiple_of(i * rows, rows), rows)

    def after_pad(i):
        return pl.ds(pl.multiple_of(WINDOW + i * rows, TILE), rows)

    def tile_at(i):
        return pl.ds(pl.multiple_of(i * TILE, TILE), TILE)

    def halves(h):
        return slice(h * half, (h + 1) * half)

    barrier = pltpu.get_barrier_semaphore()
    for s in (partner, seq_at(m + 1), seq_at(m - 1)):
        pl.semaphore_signal(barrier, inc=1, device_id={"seq": s}, device_id_type=MESH)
    for d in range(1, hn):
        peer = lax.rem(hme + d, hn)
        for s in (me, partner):
            pl.semaphore_signal(
                barrier, inc=1, device_id={"seq": s, "head": peer}, device_id_type=MESH
            )

    loads = [
        pltpu.make_async_copy(src, dst, l_s.at[i])
        for i, (src, dst) in enumerate(
            (
                (w1, w_in.at[0]), (w3, w_in.at[1]), (w2, w_in.at[2]),
                (k.at[:, lanes(c)], kx.at[after_pad(c)]),
                (v.at[:, lanes(c)], vx.at[after_pad(c)]),
                (q.at[:, lanes(c)], qx.at[block(c)]),
                (rate, rate_in), (gain, gain_in),
            )
        )
    ]
    for copy in loads:
        copy.start()
    with scope("a_load"):
        for j in range(3):
            loads[j].wait()
            wg[j, m, c] = w_in[j, c].astype(BF16)
            wb_out[j] = w_in[j, oc].astype(BF16)
    with scope("a_barrier"):
        pl.semaphore_wait(barrier, 3 + 2 * (hn - 1))

    pending = []

    def start(copy, when=None, alone=True):
        if when is None:
            copy.start()
        else:
            pl.when(when)(copy.start)
        if alone:
            pending.append((copy, when))

    def wait(copy, when):
        pl.when(when)(copy.wait_recv)

    def remote(src, dst, ss, rr, **where):
        return pltpu.make_async_remote_copy(
            src_ref=src, dst_ref=dst, send_sem=ss, recv_sem=rr,
            device_id=where, device_id_type=MESH,
        )

    def group(ref, ss, rr):
        return remote(ref, ref, ss, rr, seq=partner)

    def to_partner(i, src, dst):
        return remote(src, dst, x_s.at[i], x_r.at[i], seq=partner)

    x_w = to_partner(0, wb_out, wg.at[:, m, c])
    def token_copies(src, dst, name, rr):
        return [
            remote(
                src.at[i * TILE:(i + 1) * TILE, lanes(oc)],
                dst.at[pl.ds(pl.multiple_of(WINDOW + c * rows + i * TILE, TILE), TILE)],
                sends[name], rr.at[i], seq=partner,
            )
            for i in range(tiles)
        ]

    x_k = token_copies(k, kx, "k", k_r)
    x_v = token_copies(v, vx, "v", v_r)
    x_e = to_partner(1, rate, eta_x)
    x_q = [
        remote(
            q.at[i * TILE:(i + 1) * TILE, lanes(oc)],
            qx.at[pl.ds(pl.multiple_of(c * rows + i * TILE, TILE), TILE)],
            sends["xq"], q_r.at[i], seq=partner,
        )
        for i in range(tiles)
    ]
    x_n = to_partner(3, ratio_out, ratio_in)
    x_g = [
        remote(
            chunk(us, i).at[m, oc], chunk(gis, i), sends["g_a" if i < 4 else "g_b"],
            g_r.at[0 if i < 4 else 1], seq=partner,
        )
        for i in range(8)
    ]
    has_next = m < line - 1
    has_prev = m > 0
    asks = jnp.logical_and(has_prev, m >= middle)
    answers = jnp.logical_and(has_next, m + 1 >= middle)
    to_other = jnp.logical_and(has_next, jnp.logical_not(answers))
    takes_all = jnp.logical_and(has_prev, jnp.logical_not(asks))

    def halo(x, i, base):
        return remote(
            x.at[2 * rows + i * TILE:2 * rows + (i + 1) * TILE],
            x.at[i * TILE:(i + 1) * TILE],
            sends["hv" if base else "hk"], halo_r.at[base + i], seq=seq_at(m + 1),
        )

    halo_k = [halo(kx, i, 0) for i in range(tiles)]
    halo_v = [halo(vx, i, tiles) for i in range(tiles)]
    back = BACK * TILE

    def back_tile(i):
        return slice(i * TILE, (i + 1) * TILE)

    q_back = [
        remote(
            qx.at[back_tile(i)], qn.at[back_tile(i)], sends["qb"], qb_r.at[i], seq=seq_at(m - 1)
        )
        for i in range(BACK)
    ]
    part_on = [
        remote(
            part_out.at[back_tile(i)], part_in.at[back_tile(i)], sends["pt"], pt_r.at[i],
            seq=seq_at(m + 1),
        )
        for i in range(BACK)
    ]
    lse_on = remote(lse_out, lse_in, sends["pl"], pt_r.at[BACK], seq=seq_at(m + 1))

    def link(ss, rr, src, dst, d, i, s):
        return remote(
            src, dst, ss.at[d, s - 1], rr.at[d, i, s - 1], seq=seq_at(m + step_to[d])
        )

    def ahead(d):
        return line - 1 - m if d == 0 else m

    def w_piece(i, b):
        return wg.at[i % 3, b, c if i < 3 else oc]

    def gather_copy(i, d, s):
        b = lax.rem(m - step_to[d] * (s - 1) + line, line)
        return link(ag_s, ag_r, w_piece(i, b), w_piece(i, b), d, i, s)

    def gather_arrived(i, d, s, passing):
        b = lax.rem(m - step_to[d] * s + line, line)
        onward = ahead(d) >= 1 if passing else ahead(d) == 0
        wait(
            link(ag_s, ag_r, w_piece(i, b), w_piece(i, b), d, i, s),
            jnp.logical_and(ahead(1 - d) >= s, onward),
        )

    def gather_send(i, s):
        for d in range(2):
            if s > 1:
                gather_arrived(i, d, s - 1, True)
            start(
                gather_copy(i, d, s),
                jnp.logical_and(ahead(d) >= 1, ahead(1 - d) >= s - 1), False,
            )

    def gather_finish(i):
        for d in range(2):
            for s in range(1, line):
                gather_arrived(i, d, s, False)

    def number(i, r):
        return sum(parts(t) for t in range(i)) + r

    def inward_copy(i, r, across):
        return remote(
            part(outs, i, r), part(exs if across else ins, i, r),
            sends["in_a" if i < 4 else "in_b"], (back_r if across else in_r).at[number(i, r)],
            seq=seq_at(m + inward),
        )

    def outward_copy(i, r):
        piece = part(us, i, r)
        return remote(
            piece, piece, sends["out_a" if i < 4 else "out_b"], back_r.at[number(i, r)],
            seq=seq_at(m - inward),
        )

    def sum_first(i, r):
        @pl.when(edge == 0)
        def _():
            part(outs, i, r)[...] = part(pgs, i, r)[...].astype(BF16)

        start(inward_copy(i, r, False), jnp.logical_and(edge == 0, jnp.logical_not(inner)), False)
        start(inward_copy(i, r, True), jnp.logical_and(edge == 0, inner), False)

    def sum_on(i, r):
        @pl.when(edge > 0)
        def _():
            inward_copy(i, r, False).wait_recv()
            total = part(pgs, i, r)[...] + part(ins, i, r)[...].astype(F32)
            part(pgs, i, r)[...] = total
            part(outs, i, r)[...] = total.astype(BF16)

        start(inward_copy(i, r, False), jnp.logical_and(edge > 0, jnp.logical_not(inner)), False)
        start(inward_copy(i, r, True), jnp.logical_and(edge > 0, inner), False)

    def sum_back(i, r):
        j, cols = chunks[i]
        deep = line // parts(i)

        @pl.when(inner)
        def _():
            inward_copy(i, r, True).wait_recv()
            total = part(pgs, i, r)[...] + part(exs, i, r)[...].astype(F32)
            old = wg[j, r * deep:(r + 1) * deep, :, :, cols].astype(F32)
            part(us, i, r)[...] = (total + old).astype(BF16)

        wait(outward_copy(i, r), jnp.logical_not(inner))
        start(outward_copy(i, r), edge > 0, False)

    def column(row):
        return jnp.transpose(jnp.broadcast_to(row, (TILE, row.shape[1])))

    def as_row(col):
        return jnp.transpose(jnp.broadcast_to(col, (col.shape[0], TILE)))[:8]

    def w_cols(j, h):
        return wg[j, :, :, :, halves(h)].reshape(n * shard, half)

    def w_rows(j, h):
        return wg[j].reshape(n * shard, hd)[halves(h)]

    def u_all(i):
        u = chunk(us, i)[...]
        return u.reshape(n * shard, u.shape[-1])

    def forward(b):
        for h in range(2):

            @pl.loop(0, rows // WIDE)
            def _(i):
                at = pl.ds(pl.multiple_of(b * rows + i * WIDE, WIDE), WIDE)
                kt = kx[pl.ds(pl.multiple_of(WINDOW + b * rows + i * WIDE, WIDE), WIDE), :]
                a = dot(kt, w_cols(0, h))
                up = dot(kt, w_cols(1, h))
                g = jax.nn.sigmoid(a)
                ag = a * g
                hid[at, halves(h)] = (ag * up).astype(BF16)
                pre[0, at, halves(h)] = up * g * (1.0 + a * (1.0 - g))
                pre[1, at, halves(h)] = ag

    def scaled_values(b, i):
        at = pl.ds(pl.multiple_of(b * rows + i * WIDE, WIDE), WIDE)
        lane = slice(i * WIDE, (i + 1) * WIDE)
        eta = column((rate_in if b is c else eta_x)[pl.ds(c, 1), lane])[:, :1]
        vb = vx[pl.ds(pl.multiple_of(WINDOW + b * rows + i * WIDE, TILE), WIDE), :]
        gv[at, :] = (eta * vb.astype(F32)).astype(BF16)

    def backward(b, i):
        scaled_values(b, i)
        at = pl.ds(pl.multiple_of(b * rows + i * WIDE, WIDE), WIDE)
        for h in range(2):
            back = dot_rhs_t(gv[at, :], w_rows(2, h))
            dab[h, at, halves(0)] = (back * pre[0, at, halves(h)]).astype(BF16)
            dab[h, at, halves(1)] = (back * pre[1, at, halves(h)]).astype(BF16)

    def product(h, top):
        deep = line // parts(0) * (parts(0) // 2) if parts(0) > 1 else line
        count = line // deep
        if top >= count:
            return
        size = n * shard // count
        at_rows = slice(top * size, (top + 1) * size)
        g = (
            dot(kt[at_rows, :], dab[h]) if h < 2
            else dot_lhs_t(hid[:, at_rows], gv[...])
        )
        for i, at in ((2 * h, 0), (2 * h + 1, half)) if h < 2 else zip(
            range(4, 8), range(0, hd, quarter)
        ):
            dst = chunk(pgs, i).at[top * deep:(top + 1) * deep]
            dst[...] = g[:, at:at + dst.shape[-1]].reshape(dst.shape)

    def softmax(s, ok):
        s = jnp.where(ok, s * (1.0 / math.sqrt(hd)), NONE)
        top = jnp.max(s, axis=1, keepdims=True)
        e = jnp.exp(s - top)
        total = jnp.sum(e, axis=1, keepdims=True)
        return (e * (1.0 / total)).astype(BF16), top + jnp.log(total)

    first_key = jnp.where(m == 0, WINDOW, jnp.where(asks, back, 0))

    def local_attention(b, i):
        span = WINDOW + TILE
        base = pl.multiple_of(b * rows + i * TILE, TILE)
        s = dot_rhs_t(qx[pl.ds(base, TILE), :], kx[pl.ds(base, span), :])
        r = lax.broadcasted_iota(jnp.int32, (TILE, span), 0)
        u = lax.broadcasted_iota(jnp.int32, (TILE, span), 1)
        ok = (u > r) & (u <= r + WINDOW) & (base + u >= first_key)
        p, stat = softmax(s, ok)
        attn[b, tile_at(i), :] = dot(p, vx[pl.ds(base, span), :])
        if b == 0 and i < BACK:
            lse[back_tile(i), :] = jnp.broadcast_to(stat, (TILE, TILE))

    def next_attention(i):
        keys = slice(WINDOW + rows + i * TILE, WINDOW + rows + back)
        span = back - i * TILE

        @pl.when(answers)
        def _():
            q_back[i].wait_recv()
            s = dot_rhs_t(qn[back_tile(i), :], kx[keys, :])
            r = lax.broadcasted_iota(jnp.int32, (TILE, span), 0)
            u = lax.broadcasted_iota(jnp.int32, (TILE, span), 1)
            p, stat = softmax(s, u > r)
            stat = jnp.where(lax.broadcasted_iota(jnp.int32, stat.shape, 0) < span - 1, stat, NONE)
            part_out[back_tile(i), :] = dot(p, vx[keys, :]).astype(BF16)
            lse_out[:, back_tile(i)] = as_row(stat)

        if i == BACK - 1:
            start(lse_on, answers)
        start(part_on[i], answers, False)

    def combine(i):
        at = back_tile(i)

        @pl.when(asks)
        def _():
            if i == 0:
                lse_on.wait_recv()
            part_on[i].wait_recv()
            here = lse[at, :1]
            before = column(lse_in[0:1, at])[:, :1]
            keep = jax.nn.sigmoid(here - before)
            attn[0, at, :] = keep * attn[0, at, :] + (1.0 - keep) * part_in[at, :].astype(F32)

    def attn_to(i):
        at = slice(i * TILE, (i + 1) * TILE)
        return remote(attn_out.at[at], attn_in.at[at], sends["a"], sends["ar"], seq=partner)

    def attention_out(when, some):
        @pl.when(when)
        def _():
            for i in some:
                at = slice(i * TILE, (i + 1) * TILE)
                attn_out[at, :] = attn[oc, at, :].astype(BF16)
                attn_to(i).start()

    def squares(x):
        x = x.astype(F32)
        return jnp.sum(x * x, axis=0, keepdims=True)

    def set_ratio(i):
        j, cols = chunks[i]
        old = ratio_out[j:j + 1, cols]
        ratio_out[j:j + 1, cols] = old / jnp.sqrt(squares(u_all(i)) + EPS)

    def hidden_two(h, i):
        at = slice(i * WIDE, (i + 1) * WIDE)
        a = dot(qx[at, :], u_all(2 * h)) * ratio_out[0:1, halves(h)]
        g = dot(qx[at, :], u_all(2 * h + 1)) * ratio_out[1:2, halves(h)]
        h2[at, halves(h)] = (a * jax.nn.sigmoid(a) * g).astype(BF16)

    def wide_at(i):
        return pl.ds(pl.multiple_of(i * WIDE, WIDE), WIDE)

    def f_copy(i, h):
        piece = (wide_at(i), chunks[4 + h][1])
        arrived = sends["fr" if h < 3 else "fr_last"]
        return remote(f_out.at[piece], f_in.at[piece], sends["f"], arrived, seq=partner)

    def apply_tile(b, i, h):
        ht = h2[pl.ds(pl.multiple_of(b * rows + i * WIDE, WIDE), WIDE), :]
        f = dot(ht, u_all(4 + h)) * ratio_out[2:3, chunks[4 + h][1]]
        squared = as_row(jnp.sum(f * f, axis=1, keepdims=True))
        where = 0 if b is c else 1
        if h == 0:
            sq[where, :, wide_at(i)] = squared
        else:
            sq[where, :, wide_at(i)] = sq[where, :, wide_at(i)] + squared
        return f

    def apply_out(h, between=None):
        for i in range(rows // WIDE):
            f_out[wide_at(i), chunks[4 + h][1]] = apply_tile(oc, i, h).astype(BF16)
            if between is None:
                f_copy(i, h).start()
        if between is not None:
            between()
            for i in range(rows // WIDE):
                f_copy(i, h).start()

    def apply_own(h):
        for i in range(rows // WIDE):
            branch[wide_at(i), chunks[4 + h][1]] = apply_tile(c, i, h)

    start(x_w)
    for copy in x_k:
        copy.start()
    start(x_e)
    soon = jnp.logical_and(c == 0, asks)
    for i in range(BACK):
        start(x_q[i], soon, False)
    for copy in x_v:
        copy.start()
    for i in range(tiles):
        if i < BACK:
            start(x_q[i], jnp.logical_not(soon), False)
        else:
            x_q[i].start()
    for j in range(3):
        gather_send(j, 1)

    @pl.when(asks)
    def _():
        for x in (kx, vx):
            x[:back, :] = jnp.zeros((back, hd), BF16)

    @pl.when(m == 0)
    def _():
        for x in (kx, vx):
            x[:WINDOW, :] = jnp.zeros((WINDOW, hd), BF16)

    for copy in loads[3:]:
        copy.wait()
    with scope("b_relay0"):
        if line > 2:
            for j in range(3):
                gather_send(j, 2)
    with scope("b_xw"):
        x_w.wait_recv()
    for j in range(3):
        gather_send(3 + j, 1)
    def forward_halo(copies, i, when):
        sent_on = to_other if i < BACK else has_next
        start(copies[i], jnp.logical_and(sent_on, when), False)

    for i in range(2 * tiles):
        forward_halo((halo_k, halo_v)[i // tiles], i % tiles, jnp.logical_and(c == 1, m == 0))

    def pass_keys(when):
        for i in range(tiles):
            wait(x_k[i], when)
            forward_halo(halo_k, i, jnp.logical_and(c == 0, when))

    def pass_value(i):
        with scope("b_xv"):
            x_v[i].wait_recv()
        forward_halo(halo_v, i, c == 0)

    pass_keys(m == 0)
    with scope("b_relay"):
        if line > 2:
            for j in range(3):
                gather_send(3 + j, 2)
        for s in range(3, line):
            for j in range(3):
                gather_send(j, s)
                gather_send(3 + j, s)
    for i in range(2 * tiles):
        forward_halo((halo_k, halo_v)[i // tiles], i % tiles, jnp.logical_and(c == 1, m > 0))
    for copy in q_back:
        start(copy, jnp.logical_and(c == 0, asks), False)
    with scope("b_xk"):
        pass_keys(m > 0)
    def tokens_in(when, some):
        for i in some:
            wait(x_q[i], when)

    with scope("b_qb"):
        ask = jnp.logical_and(c == 1, asks)
        tokens_in(ask, range(BACK))
        for copy in q_back:
            start(copy, ask, False)
    with scope("b_kt"):
        kt[...] = jnp.transpose(kx[WINDOW:, :])
    for i in range(tiles // 2):
        pass_value(i)
    with scope("b_w13"):
        for j in range(2):
            gather_finish(j)
            gather_finish(3 + j)
    with scope("b_fwd_own"):
        forward(c)
    for i in range(tiles // 2, tiles - 1):
        pass_value(i)
    with scope("b_fwd_oc"):
        forward(oc)
    for j in range(2):
        ratio_out[j:j + 1] = jnp.sqrt(squares(wg[j].reshape(n * shard, hd)))
    with scope("b_w2"):
        gather_finish(2)
        gather_finish(5)
    with scope("b_bwd_own"):
        for i in range(rows // WIDE):
            backward(c, i)
        ratio_out[2:3] = jnp.sqrt(squares(wg[2].reshape(n * shard, hd)))
    x_e.wait_recv()
    with scope("b_bwd_oc"):
        for i in range(rows // WIDE - 1):
            backward(oc, i)
    pass_value(tiles - 1)
    with scope("b_bwd_last"):
        backward(oc, rows // WIDE - 1)

    for h in range(3):
        group_of = ((0, 1), (2, 3), (4, 5, 6, 7))[h]
        sent_first = parts(0) // 2 if h == 0 else 0
        with scope("prod%d" % h):
            product(h, 0)
            for r in range(sent_first):
                sum_first(0, r)
            product(h, 1)
        for i in group_of:
            for r in range(sent_first if i == 0 else 0, parts(i)):
                sum_first(i, r)

    def halo_wait():
        for i in range(tiles):
            for copies in (halo_k, halo_v):
                wait(
                    copies[i],
                    takes_all if i < BACK else has_prev,
                )

    def first_tokens():
        tokens_in(c == 0, range(tiles))

    def rest_tokens():
        tokens_in(jnp.logical_and(c == 1, jnp.logical_not(asks)), range(BACK))
        tokens_in(c == 1, range(BACK, tiles))
        halo_wait()

    def attend(b, i):
        return lambda: local_attention(b, i)

    ones = [attend(1, i) for i in range(tiles)]
    zeros = [attend(0, i) for i in range(BACK, tiles)] + [attend(0, i) for i in range(BACK)]
    tasks = (
        [lambda: (first_tokens(), ones[0]())]
        + ones[1:]
        + [lambda: (attention_out(c == 0, range(tiles)), rest_tokens(), zeros[0]())]
        + zeros[1:]
        + [lambda: attention_out(c == 1, range(BACK, tiles))]
        + [lambda i=i: combine(i) for i in range(BACK)]
        + [lambda: attention_out(c == 1, range(BACK))]
    )
    done = []
    with scope("b_next"):
        for i in range(BACK):
            next_attention(i)

    def task():
        if tasks:
            with scope("task%d" % len(done)):
                tasks.pop(0)()
            done.append(0)

    def finished(i):
        set_ratio(i)
        x_g[i].start()
        if i == 1 or i == 3:
            for b in range(2 * rows // WIDE):
                tasks.append(lambda b=b: hidden_two(i // 2, b))

    pieces = [(i, r) for i in range(8) for r in range(parts(i))]
    for p in range(len(pieces) + LAG):
        with scope("p%d" % p):
            if p < len(pieces):
                sum_on(*pieces[p])
            if p >= LAG:
                sum_back(*pieces[p - LAG])
        if p >= LAG:
            i, r = pieces[p - LAG]
            if r == parts(i) - 1:
                finished(i)
                if 4 <= i < 7:
                    while tasks:
                        task()
                    with scope("apply%d" % i):
                        apply_out(i - 4)
                        apply_own(i - 4)
        for _ in range(0 if p < FIRST else 1 if p < len(pieces) - LAG * 2 else 2):
            task()

    def square_to(src, slot, **where):
        return remote(sq.at[src, 0:1], sq_in.at[slot, 0:1], sends["q"], sends["qr"], **where)

    def squares_across():
        for d in range(hn):
            square_to(1, hn - 1 + d, seq=partner, head=lax.rem(hme + d, hn)).start()

    with scope("t_out"):
        start(x_n)
        apply_out(3, squares_across)
    with scope("t_own"):
        apply_own(3)
        for d in range(1, hn):
            square_to(0, d - 1, head=lax.rem(hme + d, hn)).start()
    with scope("t_outs"):
        x_n.wait_recv()
        for t in range(2):
            group(gis[t], g_r.at[t], g_r.at[t]).wait_recv()
        for i, (j, cols) in enumerate(chunks):
            out = o_all.at[j]
            new = chunk(us, i)[m, c].astype(F32) * ratio_out[j:j + 1, cols]
            out[c, :, cols] = new
            other = chunk(gis, i)[...].astype(F32) * ratio_in[j:j + 1, cols]
            out[oc, :, cols] = other
    stores = [
        pltpu.make_async_copy(o_all.at[j], out, sends["new"])
        for j, out in enumerate((o1_to, o3_to, o2_to))
    ]
    for copy in stores:
        copy.start()
    every_square = sq_in.at[:, 0:1]
    with scope("t_sq"):
        group(every_square, sends["q"], sends["qr"]).wait_recv()
        total = sq[0, 0:1]
        for slot in range(2 * hn - 1):
            total = total + sq_in[slot, 0:1]
        group(every_square, sends["q"], sends["qr"]).wait_send()
        inv_row = lax.rsqrt(total * (1.0 / (hn * width)) + EPS)
        for i in range(tiles):
            at = slice(i * TILE, (i + 1) * TILE)
            inv_all[at, :] = column(inv_row[:, at])

    def inverse(at, columns):
        return jnp.concatenate([inv_all[at, :]] * (columns // TILE), axis=1)

    def tile_store(i, b):
        piece = (tile_at(i), lanes(b))
        return pltpu.make_async_copy(mixed.at[piece], mixed_to.at[piece], sends["mixed"])

    def mix_other(i, cols):
        at = slice(i * TILE, (i + 1) * TILE)
        first = oc * hd + cols.start
        to = pl.ds(pl.multiple_of(first, TILE), cols.stop - cols.start)
        inv = inverse(at, cols.stop - cols.start)
        other = f_in[at, cols].astype(F32) * inv * gain_in[:, to]
        mixed[at, to] = (attn_in[at, cols].astype(F32) + other).astype(BF16)

    with scope("t_mix_own"):
        for i in range(tiles):
            at = slice(i * TILE, (i + 1) * TILE)
            own_part = branch[at, :] * inverse(at, hd) * gain_in[:, lanes(c)]
            mixed[at, lanes(c)] = (attn[c, at, :] + own_part).astype(BF16)
            tile_store(i, c).start()
    with scope("t_sends"):
        for copy, when in pending:
            if when is None:
                copy.wait_send()
            else:
                pl.when(when)(copy.wait_send)

        def sent(ref, name, when=None):
            copy = group(ref, sends[name] if isinstance(name, str) else name, sends["ar"])
            if when is None:
                copy.wait_send()
            else:
                pl.when(when)(copy.wait_send)

        for d in range(2):
            for s in range(1, line):
                sent(
                    wg.at[:, 0], ag_s.at[d, s - 1],
                    jnp.logical_and(ahead(d) >= 1, ahead(1 - d) >= s - 1),
                )
        for t, name in enumerate(("a", "b")):
            sent(outs[t], "in_" + name)
            sent(us[t], "out_" + name, edge > 0)
            sent(gis[t], "g_" + name)
        sent(attn_out, "k")
        sent(attn_out, "v")
        sent(attn_out, "xq")
        for x, name in ((kx, "hk"), (vx, "hv")):
            sent(x.at[:WINDOW], name, to_other)
            sent(x.at[back:WINDOW], name, answers)
        sent(part_out, "pt", answers)
        sent(qn, "qb", asks)
        sent(attn_out, "a")
        sent(f_out, "f")
    with scope("t_mix_oc"):
        group(attn_in, sends["a"], sends["ar"]).wait_recv()
        group(f_in.at[:, :3 * quarter], sends["f"], sends["fr"]).wait_recv()
        for i in range(tiles):
            mix_other(i, slice(0, 3 * quarter))
    with scope("t_last"):
        group(f_in.at[:, 3 * quarter:], sends["f"], sends["fr_last"]).wait_recv()
        for i in range(tiles):
            mix_other(i, slice(3 * quarter, hd))
            tile_store(i, oc).start()
    with scope("t_stores"):
        pltpu.make_async_copy(o_all, o_all, sends["new"]).wait()
        pltpu.make_async_copy(mixed, mixed_to, sends["mixed"]).wait()


def store(*refs):
    sems = refs[-1]
    copies = [pltpu.make_async_copy(refs[i], refs[4 + i], sems.at[i]) for i in range(4)]
    for copy in copies:
        copy.start()
    for copy in copies:
        copy.wait()


def local(n, hn, queries, keys, values, rate, fast_gate, fast_up, fast_down, out_gain):
    rows, width = queries.shape
    heads, shard, hd = fast_gate.shape
    line = n // 2
    half = hd // 2
    tiles = rows // TILE
    sums = (4, line, 2, shard, half)
    sums_b = (4, line, 2, shard, hd // 4)
    dma = pltpu.SemaphoreType.DMA
    vmem = pl.BlockSpec(memory_space=pltpu.VMEM)
    hbm = pl.BlockSpec(memory_space=pltpu.HBM)
    results = pl.pallas_call(
        functools.partial(kernel, n, hn),
        out_shape=(
            pltpu.VMEM((rows, width), BF16),
            pltpu.VMEM(fast_gate.shape, F32),
            pltpu.VMEM(fast_up.shape, F32),
            pltpu.VMEM(fast_down.shape, F32),
        ),
        in_specs=[hbm] * 8,
        out_specs=(pl.BlockSpec(memory_space=pl.ANY),) * 4,
        scratch_shapes=[
            pltpu.VMEM((rows, width), BF16),
            pltpu.VMEM((3,) + fast_gate.shape, F32),
            pltpu.VMEM((3, 2, shard, hd), F32),
            pltpu.VMEM(rate.shape, F32),
            pltpu.VMEM((1, width), F32),
            pltpu.VMEM((3, line, 2, shard, hd), BF16),
            pltpu.VMEM(sums, BF16),
            pltpu.VMEM(sums_b, BF16),
            pltpu.VMEM(sums, F32),
            pltpu.VMEM(sums_b, F32),
            pltpu.VMEM(sums, BF16),
            pltpu.VMEM(sums_b, BF16),
            pltpu.VMEM(sums, BF16),
            pltpu.VMEM(sums_b, BF16),
            pltpu.VMEM(sums, BF16),
            pltpu.VMEM(sums_b, BF16),
            pltpu.VMEM((3, shard, hd), BF16),
            pltpu.VMEM((4, shard, half), BF16),
            pltpu.VMEM((4, shard, hd // 4), BF16),
            pltpu.VMEM((8, hd), F32),
            pltpu.VMEM((8, hd), F32),
            pltpu.VMEM((2 * rows, hd), BF16),
            pltpu.VMEM((WINDOW + 2 * rows, hd), BF16),
            pltpu.VMEM((WINDOW + 2 * rows, hd), BF16),
            pltpu.VMEM((hd, 2 * rows), BF16),
            pltpu.VMEM(rate.shape, F32),
            pltpu.VMEM((2 * rows, hd), BF16),
            pltpu.VMEM((2 * rows, hd), BF16),
            pltpu.VMEM((2, 2 * rows, hd), BF16),
            pltpu.VMEM((2, 2 * rows, hd), F32),
            pltpu.VMEM((2, rows, hd), F32),
            pltpu.VMEM((rows, TILE), F32),
            pltpu.VMEM((BACK * TILE, TILE), F32),
            pltpu.VMEM((BACK * TILE, hd), BF16),
            pltpu.VMEM((BACK * TILE, hd), BF16),
            pltpu.VMEM((BACK * TILE, hd), BF16),
            pltpu.VMEM((8, BACK * TILE), F32),
            pltpu.VMEM((8, BACK * TILE), F32),
            pltpu.VMEM((rows, hd), BF16),
            pltpu.VMEM((rows, hd), BF16),
            pltpu.VMEM((2 * rows, hd), BF16),
            pltpu.VMEM((rows, hd), F32),
            pltpu.VMEM((rows, hd), BF16),
            pltpu.VMEM((rows, hd), BF16),
            pltpu.VMEM((2, 8, rows), F32),
            pltpu.VMEM((2 * hn - 1, 8, rows), F32),
        ]
        + [dma((2, line - 1)), dma((2, 6, line - 1))]
        + [dma((4 * math.gcd(PARTS, line) + 4 * math.gcd(PARTS // 2, line),))] * 2
        + [dma((8,)), dma((4,)), dma((4,)), dma((tiles,)), dma((tiles,))]
        + [dma((2 * WINDOW // TILE,)), dma((tiles,)), dma((BACK,)), dma((BACK + 1,))]
        + [dma((23,)), dma((2,))],
        compiler_params=pltpu.CompilerParams(
            collective_id=0, has_side_effects=True, vmem_limit_bytes=42 * 1024 * 1024
        ),
        name="ttt_layer",
    )(
        *(
            pltpu.with_memory_space_constraint(x, pltpu.HBM)
            for x in (
                queries, keys, values, rate, out_gain.reshape(1, width),
                fast_gate, fast_up, fast_down,
            )
        )
    )
    return pl.pallas_call(
        store,
        out_shape=tuple(jax.ShapeDtypeStruct(x.shape, x.dtype) for x in results),
        in_specs=[vmem] * 4,
        out_specs=(hbm,) * 4,
        scratch_shapes=[dma((4,))],
        compiler_params=pltpu.CompilerParams(vmem_limit_bytes=1024 * 1024),
        name="store",
    )(*results)


def solution(mesh):
    weights = P("head", "seq", None)
    tokens = P("seq", "head")
    return jax.shard_map(
        functools.partial(local, mesh.shape["seq"], mesh.shape["head"]),
        mesh=mesh,
        in_specs=(tokens, tokens, tokens, P("head", "seq"), weights, weights, weights, P("head")),
        out_specs=(tokens, weights, weights, weights),
        check_vma=False,
    )
```

```python
import functools
import math

import jax
import jax.numpy as jnp
from jax import lax
from jax.experimental import pallas as pl
from jax.experimental.pallas import tpu as pltpu
from jax.sharding import PartitionSpec as P

WINDOW = 512
EPS = 1e-06
TILE = 128
WIDE = 256
LAG = 3
FIRST = 2
PARTS = 4
BACK = 1
NONE = -1e30
MESH = pl.DeviceIdType.MESH
F32 = jnp.float32
BF16 = jnp.bfloat16
scope = jax.named_scope


def dot(a, b):
    return jnp.dot(a, b, preferred_element_type=F32)


def dot_lhs_t(a, b):
    return lax.dot_general(a, b, (((0,), (0,)), ((), ())), preferred_element_type=F32)


def dot_rhs_t(a, b):
    return lax.dot_general(a, b, (((1,), (1,)), ((), ())), preferred_element_type=F32)


def kernel(
    n, hn,
    q, k, v, rate, gain, w1, w3, w2,
    mixed_to, o1_to, o3_to, o2_to,
    mixed, o_all, w_in, rate_in, gain_in, wg, ug_a, ug_b, pg_a, pg_b, out_a, out_b, in_a, in_b, ex_a, ex_b, wb_out, gi_a, gi_b,
    ratio_out, ratio_in, qx, kx, vx, kt, eta_x, gv, hid, dab, pre, attn,
    inv_all, lse, qn, part_out, part_in, lse_out, lse_in,
    attn_out, attn_in, h2, branch, f_out, f_in, sq, sq_in,
    ag_s, ag_r, in_r, back_r, l_s, x_s, x_r, k_r, v_r, halo_r, q_r, qb_r, pt_r, one_s, g_r,
):
    rows, width = q.shape
    heads, shard, hd = w1.shape
    half = hd // 2
    line = n // 2
    tiles = rows // TILE
    me = lax.axis_index("seq")
    hme = lax.axis_index("head")
    m = lax.div(me, 2)
    c = lax.rem(me, 2)
    oc = 1 - c
    partner = 2 * m + oc
    step_to = (1, -1)
    quarter = hd // 4
    chunks = [
        (j, slice(h * half, (h + 1) * half)) for h in range(2) for j in range(2)
    ] + [(2, slice(h * quarter, (h + 1) * quarter)) for h in range(4)]
    sends = {
        name: one_s.at[i]
        for i, name in enumerate(
            ("in_a", "in_b", "out_a", "out_b", "k", "v", "hk", "hv", "g_a", "g_b", "a", "ar",
             "f", "fr", "q", "qr", "mixed", "new", "xq", "qb", "pt", "pl",
             "fr_last")
        )
    }
    us, pgs = (ug_a, ug_b), (pg_a, pg_b)
    outs, ins, exs, gis = (out_a, out_b), (in_a, in_b), (ex_a, ex_b), (gi_a, gi_b)
    middle = line // 2

    def parts(i):
        return math.gcd(PARTS if i < 4 else PARTS // 2, line)

    def chunk(bufs, i):
        return bufs[0].at[i] if i < 4 else bufs[1].at[i - 4]

    def part(bufs, i, r):
        deep = line // parts(i)
        return chunk(bufs, i).at[r * deep:(r + 1) * deep]

    left = m < middle
    inward = jnp.where(left, 1, -1)
    edge = jnp.where(left, m, line - 1 - m)
    inner = edge == middle - 1

    def seq_at(b):
        return 2 * lax.rem(b + line, line) + c

    def lanes(i):
        return pl.ds(pl.multiple_of(i * hd, hd), hd)

    def block(i):
        return pl.ds(pl.multiple_of(i * rows, rows), rows)

    def after_pad(i):
        return pl.ds(pl.multiple_of(WINDOW + i * rows, TILE), rows)

    def tile_at(i):
        return pl.ds(pl.multiple_of(i * TILE, TILE), TILE)

    def halves(h):
        return slice(h * half, (h + 1) * half)

    barrier = pltpu.get_barrier_semaphore()
    for s in (partner, seq_at(m + 1), seq_at(m - 1)):
        pl.semaphore_signal(barrier, inc=1, device_id={"seq": s}, device_id_type=MESH)
    for d in range(1, hn):
        peer = lax.rem(hme + d, hn)
        for s in (me, partner):
            pl.semaphore_signal(
                barrier, inc=1, device_id={"seq": s, "head": peer}, device_id_type=MESH
            )

    loads = [
        pltpu.make_async_copy(src, dst, l_s.at[i])
        for i, (src, dst) in enumerate(
            (
                (w1, w_in.at[0]), (w3, w_in.at[1]), (w2, w_in.at[2]),
                (k.at[:, lanes(c)], kx.at[after_pad(c)]),
                (v.at[:, lanes(c)], vx.at[after_pad(c)]),
                (q.at[:, lanes(c)], qx.at[block(c)]),
                (rate, rate_in), (gain, gain_in),
            )
        )
    ]
    for copy in loads:
        copy.start()
    with scope("a_load"):
        for j in range(3):
            loads[j].wait()
            wg[j, m, c] = w_in[j, c].astype(BF16)
            wb_out[j] = w_in[j, oc].astype(BF16)
    with scope("a_barrier"):
        pl.semaphore_wait(barrier, 3 + 2 * (hn - 1))

    pending = []

    def start(copy, when=None, alone=True):
        if when is None:
            copy.start()
        else:
            pl.when(when)(copy.start)
        if alone:
            pending.append((copy, when))

    def wait(copy, when):
        pl.when(when)(copy.wait_recv)

    def remote(src, dst, ss, rr, **where):
        return pltpu.make_async_remote_copy(
            src_ref=src, dst_ref=dst, send_sem=ss, recv_sem=rr,
            device_id=where, device_id_type=MESH,
        )

    def group(ref, ss, rr):
        return remote(ref, ref, ss, rr, seq=partner)

    def to_partner(i, src, dst):
        return remote(src, dst, x_s.at[i], x_r.at[i], seq=partner)

    x_w = to_partner(0, wb_out, wg.at[:, m, c])
    def token_copies(src, dst, name, rr):
        return [
            remote(
                src.at[i * TILE:(i + 1) * TILE, lanes(oc)],
                dst.at[pl.ds(pl.multiple_of(WINDOW + c * rows + i * TILE, TILE), TILE)],
                sends[name], rr.at[i], seq=partner,
            )
            for i in range(tiles)
        ]

    x_k = token_copies(k, kx, "k", k_r)
    x_v = token_copies(v, vx, "v", v_r)
    x_e = to_partner(1, rate, eta_x)
    x_q = [
        remote(
            q.at[i * TILE:(i + 1) * TILE, lanes(oc)],
            qx.at[pl.ds(pl.multiple_of(c * rows + i * TILE, TILE), TILE)],
            sends["xq"], q_r.at[i], seq=partner,
        )
        for i in range(tiles)
    ]
    x_n = to_partner(3, ratio_out, ratio_in)
    x_g = [
        remote(
            chunk(us, i).at[m, oc], chunk(gis, i), sends["g_a" if i < 4 else "g_b"],
            g_r.at[0 if i < 4 else 1], seq=partner,
        )
        for i in range(8)
    ]
    has_next = m < line - 1
    has_prev = m > 0
    asks = jnp.logical_and(has_prev, m >= middle)
    answers = jnp.logical_and(has_next, m + 1 >= middle)
    to_other = jnp.logical_and(has_next, jnp.logical_not(answers))
    takes_all = jnp.logical_and(has_prev, jnp.logical_not(asks))

    def halo(x, i, base):
        return remote(
            x.at[2 * rows + i * TILE:2 * rows + (i + 1) * TILE],
            x.at[i * TILE:(i + 1) * TILE],
            sends["hv" if base else "hk"], halo_r.at[base + i], seq=seq_at(m + 1),
        )

    halo_k = [halo(kx, i, 0) for i in range(tiles)]
    halo_v = [halo(vx, i, tiles) for i in range(tiles)]
    back = BACK * TILE

    def back_tile(i):
        return slice(i * TILE, (i + 1) * TILE)

    q_back = [
        remote(
            qx.at[back_tile(i)], qn.at[back_tile(i)], sends["qb"], qb_r.at[i], seq=seq_at(m - 1)
        )
        for i in range(BACK)
    ]
    part_on = [
        remote(
            part_out.at[back_tile(i)], part_in.at[back_tile(i)], sends["pt"], pt_r.at[i],
            seq=seq_at(m + 1),
        )
        for i in range(BACK)
    ]
    lse_on = remote(lse_out, lse_in, sends["pl"], pt_r.at[BACK], seq=seq_at(m + 1))

    def link(ss, rr, src, dst, d, i, s):
        return remote(
            src, dst, ss.at[d, s - 1], rr.at[d, i, s - 1], seq=seq_at(m + step_to[d])
        )

    def ahead(d):
        return line - 1 - m if d == 0 else m

    def w_piece(i, b):
        return wg.at[i % 3, b, c if i < 3 else oc]

    def gather_copy(i, d, s):
        b = lax.rem(m - step_to[d] * (s - 1) + line, line)
        return link(ag_s, ag_r, w_piece(i, b), w_piece(i, b), d, i, s)

    def gather_arrived(i, d, s, passing):
        b = lax.rem(m - step_to[d] * s + line, line)
        onward = ahead(d) >= 1 if passing else ahead(d) == 0
        wait(
            link(ag_s, ag_r, w_piece(i, b), w_piece(i, b), d, i, s),
            jnp.logical_and(ahead(1 - d) >= s, onward),
        )

    def gather_send(i, s):
        for d in range(2):
            if s > 1:
                gather_arrived(i, d, s - 1, True)
            start(
                gather_copy(i, d, s),
                jnp.logical_and(ahead(d) >= 1, ahead(1 - d) >= s - 1), False,
            )

    def gather_finish(i):
        for d in range(2):
            for s in range(1, line):
                gather_arrived(i, d, s, False)

    def number(i, r):
        return sum(parts(t) for t in range(i)) + r

    def inward_copy(i, r, across):
        return remote(
            part(outs, i, r), part(exs if across else ins, i, r),
            sends["in_a" if i < 4 else "in_b"], (back_r if across else in_r).at[number(i, r)],
            seq=seq_at(m + inward),
        )

    def outward_copy(i, r):
        piece = part(us, i, r)
        return remote(
            piece, piece, sends["out_a" if i < 4 else "out_b"], back_r.at[number(i, r)],
            seq=seq_at(m - inward),
        )

    def sum_first(i, r):
        @pl.when(edge == 0)
        def _():
            part(outs, i, r)[...] = part(pgs, i, r)[...].astype(BF16)

        start(inward_copy(i, r, False), jnp.logical_and(edge == 0, jnp.logical_not(inner)), False)
        start(inward_copy(i, r, True), jnp.logical_and(edge == 0, inner), False)

    def sum_on(i, r):
        @pl.when(edge > 0)
        def _():
            inward_copy(i, r, False).wait_recv()
            total = part(pgs, i, r)[...] + part(ins, i, r)[...].astype(F32)
            part(pgs, i, r)[...] = total
            part(outs, i, r)[...] = total.astype(BF16)

        start(inward_copy(i, r, False), jnp.logical_and(edge > 0, jnp.logical_not(inner)), False)
        start(inward_copy(i, r, True), jnp.logical_and(edge > 0, inner), False)

    def sum_back(i, r):
        j, cols = chunks[i]
        deep = line // parts(i)

        @pl.when(inner)
        def _():
            inward_copy(i, r, True).wait_recv()
            total = part(pgs, i, r)[...] + part(exs, i, r)[...].astype(F32)
            old = wg[j, r * deep:(r + 1) * deep, :, :, cols].astype(F32)
            part(us, i, r)[...] = (total + old).astype(BF16)

        wait(outward_copy(i, r), jnp.logical_not(inner))
        start(outward_copy(i, r), edge > 0, False)

    def column(row):
        return jnp.transpose(jnp.broadcast_to(row, (TILE, row.shape[1])))

    def as_row(col):
        return jnp.transpose(jnp.broadcast_to(col, (col.shape[0], TILE)))[:8]

    def w_cols(j, h):
        return wg[j, :, :, :, halves(h)].reshape(n * shard, half)

    def w_rows(j, h):
        return wg[j].reshape(n * shard, hd)[halves(h)]

    def u_all(i):
        u = chunk(us, i)[...]
        return u.reshape(n * shard, u.shape[-1])

    def forward(b):
        for h in range(2):

            @pl.loop(0, rows // WIDE)
            def _(i):
                at = pl.ds(pl.multiple_of(b * rows + i * WIDE, WIDE), WIDE)
                kt = kx[pl.ds(pl.multiple_of(WINDOW + b * rows + i * WIDE, WIDE), WIDE), :]
                a = dot(kt, w_cols(0, h))
                up = dot(kt, w_cols(1, h))
                g = jax.nn.sigmoid(a)
                ag = a * g
                hid[at, halves(h)] = (ag * up).astype(BF16)
                pre[0, at, halves(h)] = up * g * (1.0 + a * (1.0 - g))
                pre[1, at, halves(h)] = ag

    def scaled_values(b, i):
        at = pl.ds(pl.multiple_of(b * rows + i * WIDE, WIDE), WIDE)
        lane = slice(i * WIDE, (i + 1) * WIDE)
        eta = column((rate_in if b is c else eta_x)[pl.ds(c, 1), lane])[:, :1]
        vb = vx[pl.ds(pl.multiple_of(WINDOW + b * rows + i * WIDE, TILE), WIDE), :]
        gv[at, :] = (eta * vb.astype(F32)).astype(BF16)

    def backward(b, i):
        scaled_values(b, i)
        at = pl.ds(pl.multiple_of(b * rows + i * WIDE, WIDE), WIDE)
        for h in range(2):
            back = dot_rhs_t(gv[at, :], w_rows(2, h))
            dab[h, at, halves(0)] = (back * pre[0, at, halves(h)]).astype(BF16)
            dab[h, at, halves(1)] = (back * pre[1, at, halves(h)]).astype(BF16)

    def product(h, top):
        deep = line // parts(0) * (parts(0) // 2) if parts(0) > 1 else line
        count = line // deep
        if top >= count:
            return
        size = n * shard // count
        at_rows = slice(top * size, (top + 1) * size)
        g = (
            dot(kt[at_rows, :], dab[h]) if h < 2
            else dot_lhs_t(hid[:, at_rows], gv[...])
        )
        for i, at in ((2 * h, 0), (2 * h + 1, half)) if h < 2 else zip(
            range(4, 8), range(0, hd, quarter)
        ):
            dst = chunk(pgs, i).at[top * deep:(top + 1) * deep]
            dst[...] = g[:, at:at + dst.shape[-1]].reshape(dst.shape)

    def softmax(s, ok):
        s = jnp.where(ok, s * (1.0 / math.sqrt(hd)), NONE)
        top = jnp.max(s, axis=1, keepdims=True)
        e = jnp.exp(s - top)
        total = jnp.sum(e, axis=1, keepdims=True)
        return (e * (1.0 / total)).astype(BF16), top + jnp.log(total)

    first_key = jnp.where(m == 0, WINDOW, jnp.where(asks, back, 0))

    def local_attention(b, i):
        span = WINDOW + TILE
        base = pl.multiple_of(b * rows + i * TILE, TILE)
        s = dot_rhs_t(qx[pl.ds(base, TILE), :], kx[pl.ds(base, span), :])
        r = lax.broadcasted_iota(jnp.int32, (TILE, span), 0)
        u = lax.broadcasted_iota(jnp.int32, (TILE, span), 1)
        ok = (u > r) & (u <= r + WINDOW) & (base + u >= first_key)
        p, stat = softmax(s, ok)
        attn[b, tile_at(i), :] = dot(p, vx[pl.ds(base, span), :])
        if b == 0 and i < BACK:
            lse[back_tile(i), :] = jnp.broadcast_to(stat, (TILE, TILE))

    def next_attention(i):
        keys = slice(WINDOW + rows + i * TILE, WINDOW + rows + back)
        span = back - i * TILE

        @pl.when(answers)
        def _():
            q_back[i].wait_recv()
            s = dot_rhs_t(qn[back_tile(i), :], kx[keys, :])
            r = lax.broadcasted_iota(jnp.int32, (TILE, span), 0)
            u = lax.broadcasted_iota(jnp.int32, (TILE, span), 1)
            p, stat = softmax(s, u > r)
            stat = jnp.where(lax.broadcasted_iota(jnp.int32, stat.shape, 0) < span - 1, stat, NONE)
            part_out[back_tile(i), :] = dot(p, vx[keys, :]).astype(BF16)
            lse_out[:, back_tile(i)] = as_row(stat)

        if i == BACK - 1:
            start(lse_on, answers)
        start(part_on[i], answers, False)

    def combine(i):
        at = back_tile(i)

        @pl.when(asks)
        def _():
            if i == 0:
                lse_on.wait_recv()
            part_on[i].wait_recv()
            here = lse[at, :1]
            before = column(lse_in[0:1, at])[:, :1]
            keep = jax.nn.sigmoid(here - before)
            attn[0, at, :] = keep * attn[0, at, :] + (1.0 - keep) * part_in[at, :].astype(F32)

    def attn_to(i):
        at = slice(i * TILE, (i + 1) * TILE)
        return remote(attn_out.at[at], attn_in.at[at], sends["a"], sends["ar"], seq=partner)

    def attention_out(when, some):
        @pl.when(when)
        def _():
            for i in some:
                at = slice(i * TILE, (i + 1) * TILE)
                attn_out[at, :] = attn[oc, at, :].astype(BF16)
                attn_to(i).start()

    def squares(x):
        x = x.astype(F32)
        return jnp.sum(x * x, axis=0, keepdims=True)

    def set_ratio(i):
        j, cols = chunks[i]
        old = ratio_out[j:j + 1, cols]
        ratio_out[j:j + 1, cols] = old / jnp.sqrt(squares(u_all(i)) + EPS)

    def hidden_two(h, i):
        at = slice(i * WIDE, (i + 1) * WIDE)
        a = dot(qx[at, :], u_all(2 * h)) * ratio_out[0:1, halves(h)]
        g = dot(qx[at, :], u_all(2 * h + 1)) * ratio_out[1:2, halves(h)]
        h2[at, halves(h)] = (a * jax.nn.sigmoid(a) * g).astype(BF16)

    def wide_at(i):
        return pl.ds(pl.multiple_of(i * WIDE, WIDE), WIDE)

    def f_copy(i, h):
        piece = (wide_at(i), chunks[4 + h][1])
        arrived = sends["fr" if h < 3 else "fr_last"]
        return remote(f_out.at[piece], f_in.at[piece], sends["f"], arrived, seq=partner)

    def apply_tile(b, i, h):
        ht = h2[pl.ds(pl.multiple_of(b * rows + i * WIDE, WIDE), WIDE), :]
        f = dot(ht, u_all(4 + h)) * ratio_out[2:3, chunks[4 + h][1]]
        squared = as_row(jnp.sum(f * f, axis=1, keepdims=True))
        where = 0 if b is c else 1
        if h == 0:
            sq[where, :, wide_at(i)] = squared
        else:
            sq[where, :, wide_at(i)] = sq[where, :, wide_at(i)] + squared
        return f

    def apply_out(h, between=None):
        for i in range(rows // WIDE):
            f_out[wide_at(i), chunks[4 + h][1]] = apply_tile(oc, i, h).astype(BF16)
            if between is None:
                f_copy(i, h).start()
        if between is not None:
            between()
            for i in range(rows // WIDE):
                f_copy(i, h).start()

    def apply_own(h):
        for i in range(rows // WIDE):
            branch[wide_at(i), chunks[4 + h][1]] = apply_tile(c, i, h)

    start(x_w)
    for copy in x_k:
        copy.start()
    start(x_e)
    soon = jnp.logical_and(c == 0, asks)
    for i in range(BACK):
        start(x_q[i], soon, False)
    for copy in x_v:
        copy.start()
    for i in range(tiles):
        if i < BACK:
            start(x_q[i], jnp.logical_not(soon), False)
        else:
            x_q[i].start()
    for j in range(3):
        gather_send(j, 1)

    @pl.when(asks)
    def _():
        for x in (kx, vx):
            x[:back, :] = jnp.zeros((back, hd), BF16)

    @pl.when(m == 0)
    def _():
        for x in (kx, vx):
            x[:WINDOW, :] = jnp.zeros((WINDOW, hd), BF16)

    for copy in loads[3:]:
        copy.wait()
    with scope("b_relay0"):
        if line > 2:
            for j in range(3):
                gather_send(j, 2)
    with scope("b_xw"):
        x_w.wait_recv()
    for j in range(3):
        gather_send(3 + j, 1)
    def forward_halo(copies, i, when):
        sent_on = to_other if i < BACK else has_next
        start(copies[i], jnp.logical_and(sent_on, when), False)

    for i in range(2 * tiles):
        forward_halo((halo_k, halo_v)[i // tiles], i % tiles, jnp.logical_and(c == 1, m == 0))

    def pass_keys(when):
        for i in range(tiles):
            wait(x_k[i], when)
            forward_halo(halo_k, i, jnp.logical_and(c == 0, when))

    def pass_value(i):
        with scope("b_xv"):
            x_v[i].wait_recv()
        forward_halo(halo_v, i, c == 0)

    pass_keys(m == 0)
    with scope("b_relay"):
        if line > 2:
            for j in range(3):
                gather_send(3 + j, 2)
        for s in range(3, line):
            for j in range(3):
                gather_send(j, s)
                gather_send(3 + j, s)
    for i in range(2 * tiles):
        forward_halo((halo_k, halo_v)[i // tiles], i % tiles, jnp.logical_and(c == 1, m > 0))
    for copy in q_back:
        start(copy, jnp.logical_and(c == 0, asks), False)
    with scope("b_xk"):
        pass_keys(m > 0)
    def tokens_in(when, some):
        for i in some:
            wait(x_q[i], when)

    with scope("b_qb"):
        ask = jnp.logical_and(c == 1, asks)
        tokens_in(ask, range(BACK))
        for copy in q_back:
            start(copy, ask, False)
    with scope("b_kt"):
        kt[...] = jnp.transpose(kx[WINDOW:, :])
    for i in range(tiles // 2):
        pass_value(i)
    with scope("b_w13"):
        for j in range(2):
            gather_finish(j)
            gather_finish(3 + j)
    with scope("b_fwd_own"):
        forward(c)
    for i in range(tiles // 2, tiles - 1):
        pass_value(i)
    with scope("b_fwd_oc"):
        forward(oc)
    for j in range(2):
        ratio_out[j:j + 1] = jnp.sqrt(squares(wg[j].reshape(n * shard, hd)))
    with scope("b_w2"):
        gather_finish(2)
        gather_finish(5)
    with scope("b_bwd_own"):
        for i in range(rows // WIDE):
            backward(c, i)
        ratio_out[2:3] = jnp.sqrt(squares(wg[2].reshape(n * shard, hd)))
    x_e.wait_recv()
    with scope("b_bwd_oc"):
        for i in range(rows // WIDE - 1):
            backward(oc, i)
    pass_value(tiles - 1)
    with scope("b_bwd_last"):
        backward(oc, rows // WIDE - 1)

    for h in range(3):
        group_of = ((0, 1), (2, 3), (4, 5, 6, 7))[h]
        sent_first = parts(0) // 2 if h == 0 else 0
        with scope("prod%d" % h):
            product(h, 0)
            for r in range(sent_first):
                sum_first(0, r)
            product(h, 1)
        for i in group_of:
            for r in range(sent_first if i == 0 else 0, parts(i)):
                sum_first(i, r)

    def halo_wait():
        for i in range(tiles):
            for copies in (halo_k, halo_v):
                wait(
                    copies[i],
                    takes_all if i < BACK else has_prev,
                )

    def first_tokens():
        tokens_in(c == 0, range(tiles))

    def rest_tokens():
        tokens_in(jnp.logical_and(c == 1, jnp.logical_not(asks)), range(BACK))
        tokens_in(c == 1, range(BACK, tiles))
        halo_wait()

    def attend(b, i):
        return lambda: local_attention(b, i)

    ones = [attend(1, i) for i in range(tiles)]
    zeros = [attend(0, i) for i in range(BACK, tiles)] + [attend(0, i) for i in range(BACK)]
    tasks = (
        [lambda: (first_tokens(), ones[0]())]
        + ones[1:]
        + [lambda: (attention_out(c == 0, range(tiles)), rest_tokens(), zeros[0]())]
        + zeros[1:]
        + [lambda: attention_out(c == 1, range(BACK, tiles))]
        + [lambda i=i: combine(i) for i in range(BACK)]
        + [lambda: attention_out(c == 1, range(BACK))]
    )
    done = []
    with scope("b_next"):
        for i in range(BACK):
            next_attention(i)

    def task():
        if tasks:
            with scope("task%d" % len(done)):
                tasks.pop(0)()
            done.append(0)

    def finished(i):
        set_ratio(i)
        x_g[i].start()
        if i == 1 or i == 3:
            for b in range(2 * rows // WIDE):
                tasks.append(lambda b=b: hidden_two(i // 2, b))

    pieces = [(i, r) for i in range(8) for r in range(parts(i))]
    for p in range(len(pieces) + LAG):
        with scope("p%d" % p):
            if p < len(pieces):
                sum_on(*pieces[p])
            if p >= LAG:
                sum_back(*pieces[p - LAG])
        if p >= LAG:
            i, r = pieces[p - LAG]
            if r == parts(i) - 1:
                finished(i)
                if 4 <= i < 7:
                    while tasks:
                        task()
                    with scope("apply%d" % i):
                        apply_out(i - 4)
                        apply_own(i - 4)
        for _ in range(0 if p < FIRST else 1 if p < len(pieces) - LAG * 2 else 2):
            task()

    def square_to(src, slot, **where):
        return remote(sq.at[src, 0:1], sq_in.at[slot, 0:1], sends["q"], sends["qr"], **where)

    def squares_across():
        for d in range(hn):
            square_to(1, hn - 1 + d, seq=partner, head=lax.rem(hme + d, hn)).start()

    with scope("t_out"):
        start(x_n)
        apply_out(3, squares_across)
    with scope("t_own"):
        apply_own(3)
        for d in range(1, hn):
            square_to(0, d - 1, head=lax.rem(hme + d, hn)).start()
    with scope("t_outs"):
        x_n.wait_recv()
        for t in range(2):
            group(gis[t], g_r.at[t], g_r.at[t]).wait_recv()
        for i, (j, cols) in enumerate(chunks):
            out = o_all.at[j]
            new = chunk(us, i)[m, c].astype(F32) * ratio_out[j:j + 1, cols]
            out[c, :, cols] = new
            other = chunk(gis, i)[...].astype(F32) * ratio_in[j:j + 1, cols]
            out[oc, :, cols] = other
    stores = [
        pltpu.make_async_copy(o_all.at[j], out, sends["new"])
        for j, out in enumerate((o1_to, o3_to, o2_to))
    ]
    for copy in stores:
        copy.start()
    every_square = sq_in.at[:, 0:1]
    with scope("t_sq"):
        group(every_square, sends["q"], sends["qr"]).wait_recv()
        total = sq[0, 0:1]
        for slot in range(2 * hn - 1):
            total = total + sq_in[slot, 0:1]
        group(every_square, sends["q"], sends["qr"]).wait_send()
        inv_row = lax.rsqrt(total * (1.0 / (hn * width)) + EPS)
        for i in range(tiles):
            at = slice(i * TILE, (i + 1) * TILE)
            inv_all[at, :] = column(inv_row[:, at])

    def inverse(at, columns):
        return jnp.concatenate([inv_all[at, :]] * (columns // TILE), axis=1)

    def tile_store(i, b):
        piece = (tile_at(i), lanes(b))
        return pltpu.make_async_copy(mixed.at[piece], mixed_to.at[piece], sends["mixed"])

    def mix_other(i, cols):
        at = slice(i * TILE, (i + 1) * TILE)
        first = oc * hd + cols.start
        to = pl.ds(pl.multiple_of(first, TILE), cols.stop - cols.start)
        inv = inverse(at, cols.stop - cols.start)
        other = f_in[at, cols].astype(F32) * inv * gain_in[:, to]
        mixed[at, to] = (attn_in[at, cols].astype(F32) + other).astype(BF16)

    with scope("t_mix_own"):
        for i in range(tiles):
            at = slice(i * TILE, (i + 1) * TILE)
            own_part = branch[at, :] * inverse(at, hd) * gain_in[:, lanes(c)]
            mixed[at, lanes(c)] = (attn[c, at, :] + own_part).astype(BF16)
            tile_store(i, c).start()
    with scope("t_sends"):
        for copy, when in pending:
            if when is None:
                copy.wait_send()
            else:
                pl.when(when)(copy.wait_send)

        def sent(ref, name, when=None):
            copy = group(ref, sends[name] if isinstance(name, str) else name, sends["ar"])
            if when is None:
                copy.wait_send()
            else:
                pl.when(when)(copy.wait_send)

        for d in range(2):
            for s in range(1, line):
                sent(
                    wg.at[:, 0], ag_s.at[d, s - 1],
                    jnp.logical_and(ahead(d) >= 1, ahead(1 - d) >= s - 1),
                )
        for t, name in enumerate(("a", "b")):
            sent(outs[t], "in_" + name)
            sent(us[t], "out_" + name, edge > 0)
            sent(gis[t], "g_" + name)
        sent(attn_out, "k")
        sent(attn_out, "v")
        sent(attn_out, "xq")
        for x, name in ((kx, "hk"), (vx, "hv")):
            sent(x.at[:WINDOW], name, to_other)
            sent(x.at[back:WINDOW], name, answers)
        sent(part_out, "pt", answers)
        sent(qn, "qb", asks)
        sent(attn_out, "a")
        sent(f_out, "f")
    with scope("t_mix_oc"):
        group(attn_in, sends["a"], sends["ar"]).wait_recv()
        group(f_in.at[:, :3 * quarter], sends["f"], sends["fr"]).wait_recv()
        for i in range(tiles):
            mix_other(i, slice(0, 3 * quarter))
    with scope("t_last"):
        group(f_in.at[:, 3 * quarter:], sends["f"], sends["fr_last"]).wait_recv()
        for i in range(tiles):
            mix_other(i, slice(3 * quarter, hd))
            tile_store(i, oc).start()
    with scope("t_stores"):
        pltpu.make_async_copy(o_all, o_all, sends["new"]).wait()
        pltpu.make_async_copy(mixed, mixed_to, sends["mixed"]).wait()


def store(*refs):
    sems = refs[-1]
    copies = [pltpu.make_async_copy(refs[i], refs[4 + i], sems.at[i]) for i in range(4)]
    for at in range(0, refs[0].shape[0], TILE):
        piece = pl.ds(at, TILE)
        pltpu.make_async_copy(refs[0].at[piece], refs[4].at[piece], sems.at[0]).start()
    for copy in copies[1:]:
        copy.start()
    for copy in copies:
        copy.wait()


def local(n, hn, queries, keys, values, rate, fast_gate, fast_up, fast_down, out_gain):
    rows, width = queries.shape
    heads, shard, hd = fast_gate.shape
    line = n // 2
    half = hd // 2
    tiles = rows // TILE
    sums = (4, line, 2, shard, half)
    sums_b = (4, line, 2, shard, hd // 4)
    dma = pltpu.SemaphoreType.DMA
    vmem = pl.BlockSpec(memory_space=pltpu.VMEM)
    hbm = pl.BlockSpec(memory_space=pltpu.HBM)
    results = pl.pallas_call(
        functools.partial(kernel, n, hn),
        out_shape=(
            pltpu.VMEM((rows, width), BF16),
            pltpu.VMEM(fast_gate.shape, F32),
            pltpu.VMEM(fast_up.shape, F32),
            pltpu.VMEM(fast_down.shape, F32),
        ),
        in_specs=[hbm] * 8,
        out_specs=(pl.BlockSpec(memory_space=pl.ANY),) * 4,
        scratch_shapes=[
            pltpu.VMEM((rows, width), BF16),
            pltpu.VMEM((3,) + fast_gate.shape, F32),
            pltpu.VMEM((3, 2, shard, hd), F32),
            pltpu.VMEM(rate.shape, F32),
            pltpu.VMEM((1, width), F32),
            pltpu.VMEM((3, line, 2, shard, hd), BF16),
            pltpu.VMEM(sums, BF16),
            pltpu.VMEM(sums_b, BF16),
            pltpu.VMEM(sums, F32),
            pltpu.VMEM(sums_b, F32),
            pltpu.VMEM(sums, BF16),
            pltpu.VMEM(sums_b, BF16),
            pltpu.VMEM(sums, BF16),
            pltpu.VMEM(sums_b, BF16),
            pltpu.VMEM(sums, BF16),
            pltpu.VMEM(sums_b, BF16),
            pltpu.VMEM((3, shard, hd), BF16),
            pltpu.VMEM((4, shard, half), BF16),
            pltpu.VMEM((4, shard, hd // 4), BF16),
            pltpu.VMEM((8, hd), F32),
            pltpu.VMEM((8, hd), F32),
            pltpu.VMEM((2 * rows, hd), BF16),
            pltpu.VMEM((WINDOW + 2 * rows, hd), BF16),
            pltpu.VMEM((WINDOW + 2 * rows, hd), BF16),
            pltpu.VMEM((hd, 2 * rows), BF16),
            pltpu.VMEM(rate.shape, F32),
            pltpu.VMEM((2 * rows, hd), BF16),
            pltpu.VMEM((2 * rows, hd), BF16),
            pltpu.VMEM((2, 2 * rows, hd), BF16),
            pltpu.VMEM((2, 2 * rows, hd), F32),
            pltpu.VMEM((2, rows, hd), F32),
            pltpu.VMEM((rows, TILE), F32),
            pltpu.VMEM((BACK * TILE, TILE), F32),
            pltpu.VMEM((BACK * TILE, hd), BF16),
            pltpu.VMEM((BACK * TILE, hd), BF16),
            pltpu.VMEM((BACK * TILE, hd), BF16),
            pltpu.VMEM((8, BACK * TILE), F32),
            pltpu.VMEM((8, BACK * TILE), F32),
            pltpu.VMEM((rows, hd), BF16),
            pltpu.VMEM((rows, hd), BF16),
            pltpu.VMEM((2 * rows, hd), BF16),
            pltpu.VMEM((rows, hd), F32),
            pltpu.VMEM((rows, hd), BF16),
            pltpu.VMEM((rows, hd), BF16),
            pltpu.VMEM((2, 8, rows), F32),
            pltpu.VMEM((2 * hn - 1, 8, rows), F32),
        ]
        + [dma((2, line - 1)), dma((2, 6, line - 1))]
        + [dma((4 * math.gcd(PARTS, line) + 4 * math.gcd(PARTS // 2, line),))] * 2
        + [dma((8,)), dma((4,)), dma((4,)), dma((tiles,)), dma((tiles,))]
        + [dma((2 * WINDOW // TILE,)), dma((tiles,)), dma((BACK,)), dma((BACK + 1,))]
        + [dma((23,)), dma((2,))],
        compiler_params=pltpu.CompilerParams(
            collective_id=0, has_side_effects=True, vmem_limit_bytes=42 * 1024 * 1024
        ),
        name="ttt_layer",
    )(
        *(
            pltpu.with_memory_space_constraint(x, pltpu.HBM)
            for x in (
                queries, keys, values, rate, out_gain.reshape(1, width),
                fast_gate, fast_up, fast_down,
            )
        )
    )
    return pl.pallas_call(
        store,
        out_shape=tuple(jax.ShapeDtypeStruct(x.shape, x.dtype) for x in results),
        in_specs=[vmem] * 4,
        out_specs=(hbm,) * 4,
        scratch_shapes=[dma((4,))],
        compiler_params=pltpu.CompilerParams(vmem_limit_bytes=1024 * 1024),
        name="store",
    )(*results)


def solution(mesh):
    weights = P("head", "seq", None)
    tokens = P("seq", "head")
    return jax.shard_map(
        functools.partial(local, mesh.shape["seq"], mesh.shape["head"]),
        mesh=mesh,
        in_specs=(tokens, tokens, tokens, P("head", "seq"), weights, weights, weights, P("head")),
        out_specs=(tokens, weights, weights, weights),
        check_vma=False,
    )
```

```python
import functools
import math

import jax
import jax.numpy as jnp
from jax import lax
from jax.experimental import pallas as pl
from jax.experimental.pallas import tpu as pltpu
from jax.sharding import PartitionSpec as P

WINDOW = 512
EPS = 1e-06
TILE = 128
WIDE = 256
LAG = 3
SOON = 2
FIRST = 2
PARTS = 4
BACK = 1
NONE = -1e30
MESH = pl.DeviceIdType.MESH
F32 = jnp.float32
BF16 = jnp.bfloat16
scope = jax.named_scope


def dot(a, b):
    return jnp.dot(a, b, preferred_element_type=F32)


def dot_lhs_t(a, b):
    return lax.dot_general(a, b, (((0,), (0,)), ((), ())), preferred_element_type=F32)


def dot_rhs_t(a, b):
    return lax.dot_general(a, b, (((1,), (1,)), ((), ())), preferred_element_type=F32)


def kernel(
    n, hn,
    q, k, v, rate, gain, w1, w3, w2,
    mixed_to, o1_to, o3_to, o2_to,
    mixed, o_all, w_in, rate_in, gain_in, wg, ug_a, ug_b, pg_a, pg_b, out_a, out_b, in_a, in_b, ex_a, ex_b, wb_out, gi_a, gi_b,
    ratio_out, ratio_in, qx, kx, vx, kt, eta_x, gv, hid, dab, pre, attn,
    inv_all, lse, qn, part_out, part_in, lse_out, lse_in,
    attn_out, attn_in, h2, branch, f_out, f_in, sq, sq_in,
    ag_s, ag_r, in_r, back_r, l_s, x_s, x_r, k_r, v_r, halo_r, q_r, qb_r, pt_r, one_s, g_r,
):
    rows, width = q.shape
    heads, shard, hd = w1.shape
    half = hd // 2
    line = n // 2
    tiles = rows // TILE
    me = lax.axis_index("seq")
    hme = lax.axis_index("head")
    m = lax.div(me, 2)
    c = lax.rem(me, 2)
    oc = 1 - c
    partner = 2 * m + oc
    step_to = (1, -1)
    quarter = hd // 4
    chunks = [
        (j, slice(h * half, (h + 1) * half)) for h in range(2) for j in range(2)
    ] + [(2, slice(h * quarter, (h + 1) * quarter)) for h in range(4)]
    sends = {
        name: one_s.at[i]
        for i, name in enumerate(
            ("in_a", "in_b", "out_a", "out_b", "k", "v", "hk", "hv", "g_a", "g_b", "a", "ar",
             "f", "fr", "q", "qr", "mixed", "new", "xq", "qb", "pt", "pl",
             "fr_last")
        )
    }
    us, pgs = (ug_a, ug_b), (pg_a, pg_b)
    outs, ins, exs, gis = (out_a, out_b), (in_a, in_b), (ex_a, ex_b), (gi_a, gi_b)
    middle = line // 2

    def parts(i):
        return math.gcd(PARTS if i < 4 else PARTS // 2, line)

    def chunk(bufs, i):
        return bufs[0].at[i] if i < 4 else bufs[1].at[i - 4]

    def part(bufs, i, r):
        deep = line // parts(i)
        return chunk(bufs, i).at[r * deep:(r + 1) * deep]

    left = m < middle
    inward = jnp.where(left, 1, -1)
    edge = jnp.where(left, m, line - 1 - m)
    inner = edge == middle - 1

    def seq_at(b):
        return 2 * lax.rem(b + line, line) + c

    def lanes(i):
        return pl.ds(pl.multiple_of(i * hd, hd), hd)

    def block(i):
        return pl.ds(pl.multiple_of(i * rows, rows), rows)

    def after_pad(i):
        return pl.ds(pl.multiple_of(WINDOW + i * rows, TILE), rows)

    def tile_at(i):
        return pl.ds(pl.multiple_of(i * TILE, TILE), TILE)

    def halves(h):
        return slice(h * half, (h + 1) * half)

    barrier = pltpu.get_barrier_semaphore()
    for s in (partner, seq_at(m + 1), seq_at(m - 1)):
        pl.semaphore_signal(barrier, inc=1, device_id={"seq": s}, device_id_type=MESH)
    for d in range(1, hn):
        peer = lax.rem(hme + d, hn)
        for s in (me, partner):
            pl.semaphore_signal(
                barrier, inc=1, device_id={"seq": s, "head": peer}, device_id_type=MESH
            )

    loads = [
        pltpu.make_async_copy(src, dst, l_s.at[i])
        for i, (src, dst) in enumerate(
            (
                (w1, w_in.at[0]), (w3, w_in.at[1]), (w2, w_in.at[2]),
                (k.at[:, lanes(c)], kx.at[after_pad(c)]),
                (v.at[:, lanes(c)], vx.at[after_pad(c)]),
                (q.at[:, lanes(c)], qx.at[block(c)]),
                (rate, rate_in), (gain, gain_in),
            )
        )
    ]
    for copy in loads:
        copy.start()
    with scope("a_load"):
        for j in range(3):
            loads[j].wait()
            wg[j, m, c] = w_in[j, c].astype(BF16)
            wb_out[j] = w_in[j, oc].astype(BF16)
    with scope("a_barrier"):
        pl.semaphore_wait(barrier, 3 + 2 * (hn - 1))

    pending = []

    def start(copy, when=None, alone=True):
        if when is None:
            copy.start()
        else:
            pl.when(when)(copy.start)
        if alone:
            pending.append((copy, when))

    def wait(copy, when):
        pl.when(when)(copy.wait_recv)

    def remote(src, dst, ss, rr, **where):
        return pltpu.make_async_remote_copy(
            src_ref=src, dst_ref=dst, send_sem=ss, recv_sem=rr,
            device_id=where, device_id_type=MESH,
        )

    def group(ref, ss, rr):
        return remote(ref, ref, ss, rr, seq=partner)

    def to_partner(i, src, dst):
        return remote(src, dst, x_s.at[i], x_r.at[i], seq=partner)

    x_w = to_partner(0, wb_out, wg.at[:, m, c])
    def token_copies(src, dst, name, rr):
        return [
            remote(
                src.at[i * TILE:(i + 1) * TILE, lanes(oc)],
                dst.at[pl.ds(pl.multiple_of(WINDOW + c * rows + i * TILE, TILE), TILE)],
                sends[name], rr.at[i], seq=partner,
            )
            for i in range(tiles)
        ]

    x_k = token_copies(k, kx, "k", k_r)
    x_v = token_copies(v, vx, "v", v_r)
    x_e = to_partner(1, rate, eta_x)
    x_q = [
        remote(
            q.at[i * TILE:(i + 1) * TILE, lanes(oc)],
            qx.at[pl.ds(pl.multiple_of(c * rows + i * TILE, TILE), TILE)],
            sends["xq"], q_r.at[i], seq=partner,
        )
        for i in range(tiles)
    ]
    x_n = to_partner(3, ratio_out, ratio_in)
    x_g = [
        remote(
            chunk(us, i).at[m, oc], chunk(gis, i), sends["g_a" if i < 4 else "g_b"],
            g_r.at[0 if i < 4 else 1], seq=partner,
        )
        for i in range(8)
    ]
    has_next = m < line - 1
    has_prev = m > 0
    asks = jnp.logical_and(has_prev, m >= middle)
    answers = jnp.logical_and(has_next, m + 1 >= middle)
    to_other = jnp.logical_and(has_next, jnp.logical_not(answers))
    takes_all = jnp.logical_and(has_prev, jnp.logical_not(asks))

    def halo(x, i, base):
        return remote(
            x.at[2 * rows + i * TILE:2 * rows + (i + 1) * TILE],
            x.at[i * TILE:(i + 1) * TILE],
            sends["hv" if base else "hk"], halo_r.at[base + i], seq=seq_at(m + 1),
        )

    halo_k = [halo(kx, i, 0) for i in range(tiles)]
    halo_v = [halo(vx, i, tiles) for i in range(tiles)]
    back = BACK * TILE

    def back_tile(i):
        return slice(i * TILE, (i + 1) * TILE)

    q_back = [
        remote(
            qx.at[back_tile(i)], qn.at[back_tile(i)], sends["qb"], qb_r.at[i], seq=seq_at(m - 1)
        )
        for i in range(BACK)
    ]
    part_on = [
        remote(
            part_out.at[back_tile(i)], part_in.at[back_tile(i)], sends["pt"], pt_r.at[i],
            seq=seq_at(m + 1),
        )
        for i in range(BACK)
    ]
    lse_on = remote(lse_out, lse_in, sends["pl"], pt_r.at[BACK], seq=seq_at(m + 1))

    def link(ss, rr, src, dst, d, i, s):
        return remote(
            src, dst, ss.at[d, s - 1], rr.at[d, i, s - 1], seq=seq_at(m + step_to[d])
        )

    def ahead(d):
        return line - 1 - m if d == 0 else m

    def w_piece(i, b):
        return wg.at[i % 3, b, c if i < 3 else oc]

    def gather_copy(i, d, s):
        b = lax.rem(m - step_to[d] * (s - 1) + line, line)
        return link(ag_s, ag_r, w_piece(i, b), w_piece(i, b), d, i, s)

    def gather_arrived(i, d, s, passing):
        b = lax.rem(m - step_to[d] * s + line, line)
        onward = ahead(d) >= 1 if passing else ahead(d) == 0
        wait(
            link(ag_s, ag_r, w_piece(i, b), w_piece(i, b), d, i, s),
            jnp.logical_and(ahead(1 - d) >= s, onward),
        )

    def gather_send(i, s):
        for d in range(2):
            if s > 1:
                gather_arrived(i, d, s - 1, True)
            start(
                gather_copy(i, d, s),
                jnp.logical_and(ahead(d) >= 1, ahead(1 - d) >= s - 1), False,
            )

    def gather_finish(i):
        for d in range(2):
            for s in range(1, line):
                gather_arrived(i, d, s, False)

    def number(i, r):
        return sum(parts(t) for t in range(i)) + r

    def inward_copy(i, r, across):
        return remote(
            part(outs, i, r), part(exs if across else ins, i, r),
            sends["in_a" if i < 4 else "in_b"], (back_r if across else in_r).at[number(i, r)],
            seq=seq_at(m + inward),
        )

    def outward_copy(i, r):
        piece = part(us, i, r)
        return remote(
            piece, piece, sends["out_a" if i < 4 else "out_b"], back_r.at[number(i, r)],
            seq=seq_at(m - inward),
        )

    def sum_first(i, r):
        @pl.when(edge == 0)
        def _():
            part(outs, i, r)[...] = part(pgs, i, r)[...].astype(BF16)

        start(inward_copy(i, r, False), jnp.logical_and(edge == 0, jnp.logical_not(inner)), False)
        start(inward_copy(i, r, True), jnp.logical_and(edge == 0, inner), False)

    def sum_on(i, r):
        @pl.when(edge > 0)
        def _():
            inward_copy(i, r, False).wait_recv()
            total = part(pgs, i, r)[...] + part(ins, i, r)[...].astype(F32)
            part(pgs, i, r)[...] = total
            part(outs, i, r)[...] = total.astype(BF16)

        start(inward_copy(i, r, False), jnp.logical_and(edge > 0, jnp.logical_not(inner)), False)
        start(inward_copy(i, r, True), jnp.logical_and(edge > 0, inner), False)

    soon_back = jnp.logical_and(inner, left == (c == 0))

    def sum_back(i, r, first):
        j, cols = chunks[i]
        deep = line // parts(i)
        turn = soon_back if first else jnp.logical_and(inner, jnp.logical_not(soon_back))

        @pl.when(turn)
        def _():
            inward_copy(i, r, True).wait_recv()
            total = part(pgs, i, r)[...] + part(exs, i, r)[...].astype(F32)
            old = wg[j, r * deep:(r + 1) * deep, :, :, cols].astype(F32)
            part(us, i, r)[...] = (total + old).astype(BF16)

        if first:
            start(outward_copy(i, r), jnp.logical_and(edge > 0, soon_back), False)
        else:
            wait(outward_copy(i, r), jnp.logical_not(inner))
            start(
                outward_copy(i, r), jnp.logical_and(edge > 0, jnp.logical_not(soon_back)), False
            )

    def column(row):
        return jnp.transpose(jnp.broadcast_to(row, (TILE, row.shape[1])))

    def as_row(col):
        return jnp.transpose(jnp.broadcast_to(col, (col.shape[0], TILE)))[:8]

    def w_cols(j, h):
        return wg[j, :, :, :, halves(h)].reshape(n * shard, half)

    def w_rows(j, h):
        return wg[j].reshape(n * shard, hd)[halves(h)]

    def u_all(i):
        u = chunk(us, i)[...]
        return u.reshape(n * shard, u.shape[-1])

    def forward(b):
        for h in range(2):

            @pl.loop(0, rows // WIDE)
            def _(i):
                at = pl.ds(pl.multiple_of(b * rows + i * WIDE, WIDE), WIDE)
                kt = kx[pl.ds(pl.multiple_of(WINDOW + b * rows + i * WIDE, WIDE), WIDE), :]
                a = dot(kt, w_cols(0, h))
                up = dot(kt, w_cols(1, h))
                g = jax.nn.sigmoid(a)
                ag = a * g
                hid[at, halves(h)] = (ag * up).astype(BF16)
                pre[0, at, halves(h)] = up * g * (1.0 + a * (1.0 - g))
                pre[1, at, halves(h)] = ag

    def scaled_values(b, i):
        at = pl.ds(pl.multiple_of(b * rows + i * WIDE, WIDE), WIDE)
        lane = slice(i * WIDE, (i + 1) * WIDE)
        eta = column((rate_in if b is c else eta_x)[pl.ds(c, 1), lane])[:, :1]
        vb = vx[pl.ds(pl.multiple_of(WINDOW + b * rows + i * WIDE, TILE), WIDE), :]
        gv[at, :] = (eta * vb.astype(F32)).astype(BF16)

    def backward(b, i):
        scaled_values(b, i)
        at = pl.ds(pl.multiple_of(b * rows + i * WIDE, WIDE), WIDE)
        for h in range(2):
            back = dot_rhs_t(gv[at, :], w_rows(2, h))
            dab[h, at, halves(0)] = (back * pre[0, at, halves(h)]).astype(BF16)
            dab[h, at, halves(1)] = (back * pre[1, at, halves(h)]).astype(BF16)

    def product(h, top):
        deep = line // parts(0) * (parts(0) // 2) if parts(0) > 1 else line
        count = line // deep
        if top >= count:
            return
        size = n * shard // count
        at_rows = slice(top * size, (top + 1) * size)
        g = (
            dot(kt[at_rows, :], dab[h]) if h < 2
            else dot_lhs_t(hid[:, at_rows], gv[...])
        )
        for i, at in ((2 * h, 0), (2 * h + 1, half)) if h < 2 else zip(
            range(4, 8), range(0, hd, quarter)
        ):
            dst = chunk(pgs, i).at[top * deep:(top + 1) * deep]
            dst[...] = g[:, at:at + dst.shape[-1]].reshape(dst.shape)

    def softmax(s, ok):
        s = jnp.where(ok, s * (1.0 / math.sqrt(hd)), NONE)
        top = jnp.max(s, axis=1, keepdims=True)
        e = jnp.exp(s - top)
        total = jnp.sum(e, axis=1, keepdims=True)
        return (e * (1.0 / total)).astype(BF16), top + jnp.log(total)

    first_key = jnp.where(m == 0, WINDOW, jnp.where(asks, back, 0))

    def local_attention(b, i):
        span = WINDOW + TILE
        base = pl.multiple_of(b * rows + i * TILE, TILE)
        s = dot_rhs_t(qx[pl.ds(base, TILE), :], kx[pl.ds(base, span), :])
        r = lax.broadcasted_iota(jnp.int32, (TILE, span), 0)
        u = lax.broadcasted_iota(jnp.int32, (TILE, span), 1)
        ok = (u > r) & (u <= r + WINDOW) & (base + u >= first_key)
        p, stat = softmax(s, ok)
        attn[b, tile_at(i), :] = dot(p, vx[pl.ds(base, span), :])
        if b == 0 and i < BACK:
            lse[back_tile(i), :] = jnp.broadcast_to(stat, (TILE, TILE))

    def next_attention(i):
        keys = slice(WINDOW + rows + i * TILE, WINDOW + rows + back)
        span = back - i * TILE

        @pl.when(answers)
        def _():
            q_back[i].wait_recv()
            s = dot_rhs_t(qn[back_tile(i), :], kx[keys, :])
            r = lax.broadcasted_iota(jnp.int32, (TILE, span), 0)
            u = lax.broadcasted_iota(jnp.int32, (TILE, span), 1)
            p, stat = softmax(s, u > r)
            stat = jnp.where(lax.broadcasted_iota(jnp.int32, stat.shape, 0) < span - 1, stat, NONE)
            part_out[back_tile(i), :] = dot(p, vx[keys, :]).astype(BF16)
            lse_out[:, back_tile(i)] = as_row(stat)

        if i == BACK - 1:
            start(lse_on, answers)
        start(part_on[i], answers, False)

    def combine(i):
        at = back_tile(i)

        @pl.when(asks)
        def _():
            if i == 0:
                lse_on.wait_recv()
            part_on[i].wait_recv()
            here = lse[at, :1]
            before = column(lse_in[0:1, at])[:, :1]
            keep = jax.nn.sigmoid(here - before)
            attn[0, at, :] = keep * attn[0, at, :] + (1.0 - keep) * part_in[at, :].astype(F32)

    def attn_to(i):
        at = slice(i * TILE, (i + 1) * TILE)
        return remote(attn_out.at[at], attn_in.at[at], sends["a"], sends["ar"], seq=partner)

    def attention_out(when, some):
        @pl.when(when)
        def _():
            for i in some:
                at = slice(i * TILE, (i + 1) * TILE)
                attn_out[at, :] = attn[oc, at, :].astype(BF16)
                attn_to(i).start()

    def squares(x):
        x = x.astype(F32)
        return jnp.sum(x * x, axis=0, keepdims=True)

    def set_ratio(i):
        j, cols = chunks[i]
        old = ratio_out[j:j + 1, cols]
        ratio_out[j:j + 1, cols] = old / jnp.sqrt(squares(u_all(i)) + EPS)

    def hidden_two(h, i):
        at = slice(i * WIDE, (i + 1) * WIDE)
        a = dot(qx[at, :], u_all(2 * h)) * ratio_out[0:1, halves(h)]
        g = dot(qx[at, :], u_all(2 * h + 1)) * ratio_out[1:2, halves(h)]
        h2[at, halves(h)] = (a * jax.nn.sigmoid(a) * g).astype(BF16)

    def wide_at(i):
        return pl.ds(pl.multiple_of(i * WIDE, WIDE), WIDE)

    def f_copy(i, h):
        piece = (wide_at(i), chunks[4 + h][1])
        arrived = sends["fr" if h < 3 else "fr_last"]
        return remote(f_out.at[piece], f_in.at[piece], sends["f"], arrived, seq=partner)

    def apply_tile(b, i, h):
        ht = h2[pl.ds(pl.multiple_of(b * rows + i * WIDE, WIDE), WIDE), :]
        f = dot(ht, u_all(4 + h)) * ratio_out[2:3, chunks[4 + h][1]]
        squared = as_row(jnp.sum(f * f, axis=1, keepdims=True))
        where = 0 if b is c else 1
        if h == 0:
            sq[where, :, wide_at(i)] = squared
        else:
            sq[where, :, wide_at(i)] = sq[where, :, wide_at(i)] + squared
        return f

    def apply_out(h, between=None):
        for i in range(rows // WIDE):
            f_out[wide_at(i), chunks[4 + h][1]] = apply_tile(oc, i, h).astype(BF16)
            if between is None:
                f_copy(i, h).start()
        if between is not None:
            between()
            for i in range(rows // WIDE):
                f_copy(i, h).start()

    def apply_own(h):
        for i in range(rows // WIDE):
            branch[wide_at(i), chunks[4 + h][1]] = apply_tile(c, i, h)

    start(x_w)
    for copy in x_k:
        copy.start()
    start(x_e)
    soon = jnp.logical_and(c == 0, asks)
    for i in range(BACK):
        start(x_q[i], soon, False)
    for copy in x_v:
        copy.start()
    for i in range(tiles):
        if i < BACK:
            start(x_q[i], jnp.logical_not(soon), False)
        else:
            x_q[i].start()
    for j in range(3):
        gather_send(j, 1)

    @pl.when(asks)
    def _():
        for x in (kx, vx):
            x[:back, :] = jnp.zeros((back, hd), BF16)

    @pl.when(m == 0)
    def _():
        for x in (kx, vx):
            x[:WINDOW, :] = jnp.zeros((WINDOW, hd), BF16)

    for copy in loads[3:]:
        copy.wait()
    with scope("b_relay0"):
        if line > 2:
            for j in range(3):
                gather_send(j, 2)
    with scope("b_xw"):
        x_w.wait_recv()
    for j in range(3):
        gather_send(3 + j, 1)
    def forward_halo(copies, i, when):
        sent_on = to_other if i < BACK else has_next
        start(copies[i], jnp.logical_and(sent_on, when), False)

    for i in range(2 * tiles):
        forward_halo((halo_k, halo_v)[i // tiles], i % tiles, jnp.logical_and(c == 1, m == 0))

    def pass_keys(when):
        for i in range(tiles):
            wait(x_k[i], when)
            forward_halo(halo_k, i, jnp.logical_and(c == 0, when))

    def pass_value(i):
        with scope("b_xv"):
            x_v[i].wait_recv()
        forward_halo(halo_v, i, c == 0)

    pass_keys(m == 0)
    with scope("b_relay"):
        if line > 2:
            for j in range(3):
                gather_send(3 + j, 2)
        for s in range(3, line):
            for j in range(3):
                gather_send(j, s)
                gather_send(3 + j, s)
    for i in range(2 * tiles):
        forward_halo((halo_k, halo_v)[i // tiles], i % tiles, jnp.logical_and(c == 1, m > 0))
    for copy in q_back:
        start(copy, jnp.logical_and(c == 0, asks), False)
    with scope("b_xk"):
        pass_keys(m > 0)
    def tokens_in(when, some):
        for i in some:
            wait(x_q[i], when)

    with scope("b_qb"):
        ask = jnp.logical_and(c == 1, asks)
        tokens_in(ask, range(BACK))
        for copy in q_back:
            start(copy, ask, False)
    with scope("b_kt"):
        kt[...] = jnp.transpose(kx[WINDOW:, :])
    for i in range(tiles // 2):
        pass_value(i)
    with scope("b_w13"):
        for j in range(2):
            gather_finish(j)
            gather_finish(3 + j)
    with scope("b_fwd_own"):
        forward(c)
    for i in range(tiles // 2, tiles - 1):
        pass_value(i)
    with scope("b_fwd_oc"):
        forward(oc)
    for j in range(2):
        ratio_out[j:j + 1] = jnp.sqrt(squares(wg[j].reshape(n * shard, hd)))
    with scope("b_w2"):
        gather_finish(2)
        gather_finish(5)
    with scope("b_bwd_own"):
        for i in range(rows // WIDE):
            backward(c, i)
        ratio_out[2:3] = jnp.sqrt(squares(wg[2].reshape(n * shard, hd)))
    x_e.wait_recv()
    with scope("b_bwd_oc"):
        for i in range(rows // WIDE - 1):
            backward(oc, i)
    pass_value(tiles - 1)
    with scope("b_bwd_last"):
        backward(oc, rows // WIDE - 1)

    for h in range(3):
        group_of = ((0, 1), (2, 3), (4, 5, 6, 7))[h]
        sent_first = parts(0) // 2 if h == 0 else 0
        with scope("prod%d" % h):
            product(h, 0)
            for r in range(sent_first):
                sum_first(0, r)
            product(h, 1)
        for i in group_of:
            for r in range(sent_first if i == 0 else 0, parts(i)):
                sum_first(i, r)

    def halo_wait():
        for i in range(tiles):
            for copies in (halo_k, halo_v):
                wait(
                    copies[i],
                    takes_all if i < BACK else has_prev,
                )

    def first_tokens():
        tokens_in(c == 0, range(tiles))

    def rest_tokens():
        tokens_in(jnp.logical_and(c == 1, jnp.logical_not(asks)), range(BACK))
        tokens_in(c == 1, range(BACK, tiles))
        halo_wait()

    def attend(b, i):
        return lambda: local_attention(b, i)

    ones = [attend(1, i) for i in range(tiles)]
    zeros = [attend(0, i) for i in range(BACK, tiles)] + [attend(0, i) for i in range(BACK)]
    tasks = (
        [lambda: (first_tokens(), ones[0]())]
        + ones[1:]
        + [lambda: (attention_out(c == 0, range(tiles)), rest_tokens(), zeros[0]())]
        + zeros[1:]
        + [lambda: attention_out(c == 1, range(BACK, tiles))]
        + [lambda i=i: combine(i) for i in range(BACK)]
        + [lambda: attention_out(c == 1, range(BACK))]
    )
    done = []
    with scope("b_next"):
        for i in range(BACK):
            next_attention(i)

    def task():
        if tasks:
            with scope("task%d" % len(done)):
                tasks.pop(0)()
            done.append(0)

    def finished(i):
        set_ratio(i)
        x_g[i].start()
        if i == 1 or i == 3:
            for b in range(2 * rows // WIDE):
                tasks.append(lambda b=b: hidden_two(i // 2, b))

    pieces = [(i, r) for i in range(8) for r in range(parts(i))]
    for p in range(len(pieces) + LAG):
        with scope("p%d" % p):
            if p < len(pieces):
                sum_on(*pieces[p])
            if 0 <= p - SOON < len(pieces):
                sum_back(*pieces[p - SOON], True)
            if p >= LAG:
                sum_back(*pieces[p - LAG], False)
        if p >= LAG:
            i, r = pieces[p - LAG]
            if r == parts(i) - 1:
                finished(i)
                if 4 <= i < 7:
                    while tasks:
                        task()
                    with scope("apply%d" % i):
                        apply_out(i - 4)
                        apply_own(i - 4)
        for _ in range(0 if p < FIRST else 1 if p < len(pieces) - LAG * 2 else 2):
            task()

    def square_to(src, slot, **where):
        return remote(sq.at[src, 0:1], sq_in.at[slot, 0:1], sends["q"], sends["qr"], **where)

    def squares_across():
        for d in range(hn):
            square_to(1, hn - 1 + d, seq=partner, head=lax.rem(hme + d, hn)).start()

    with scope("t_out"):
        start(x_n)
        apply_out(3, squares_across)
    with scope("t_own"):
        apply_own(3)
        for d in range(1, hn):
            square_to(0, d - 1, head=lax.rem(hme + d, hn)).start()
    with scope("t_outs"):
        x_n.wait_recv()
        for t in range(2):
            group(gis[t], g_r.at[t], g_r.at[t]).wait_recv()
        for i, (j, cols) in enumerate(chunks):
            out = o_all.at[j]
            new = chunk(us, i)[m, c].astype(F32) * ratio_out[j:j + 1, cols]
            out[c, :, cols] = new
            other = chunk(gis, i)[...].astype(F32) * ratio_in[j:j + 1, cols]
            out[oc, :, cols] = other
    stores = [
        pltpu.make_async_copy(o_all.at[j], out, sends["new"])
        for j, out in enumerate((o1_to, o3_to, o2_to))
    ]
    for copy in stores:
        copy.start()
    every_square = sq_in.at[:, 0:1]
    with scope("t_sq"):
        group(every_square, sends["q"], sends["qr"]).wait_recv()
        total = sq[0, 0:1]
        for slot in range(2 * hn - 1):
            total = total + sq_in[slot, 0:1]
        group(every_square, sends["q"], sends["qr"]).wait_send()
        inv_row = lax.rsqrt(total * (1.0 / (hn * width)) + EPS)
        for i in range(tiles):
            at = slice(i * TILE, (i + 1) * TILE)
            inv_all[at, :] = column(inv_row[:, at])

    def inverse(at, columns):
        return jnp.concatenate([inv_all[at, :]] * (columns // TILE), axis=1)

    def tile_store(i, b):
        piece = (tile_at(i), lanes(b))
        return pltpu.make_async_copy(mixed.at[piece], mixed_to.at[piece], sends["mixed"])

    def mix_other(i, cols):
        at = slice(i * TILE, (i + 1) * TILE)
        first = oc * hd + cols.start
        to = pl.ds(pl.multiple_of(first, TILE), cols.stop - cols.start)
        inv = inverse(at, cols.stop - cols.start)
        other = f_in[at, cols].astype(F32) * inv * gain_in[:, to]
        mixed[at, to] = (attn_in[at, cols].astype(F32) + other).astype(BF16)

    with scope("t_mix_own"):
        for i in range(tiles):
            at = slice(i * TILE, (i + 1) * TILE)
            own_part = branch[at, :] * inverse(at, hd) * gain_in[:, lanes(c)]
            mixed[at, lanes(c)] = (attn[c, at, :] + own_part).astype(BF16)
            tile_store(i, c).start()
    with scope("t_sends"):
        for copy, when in pending:
            if when is None:
                copy.wait_send()
            else:
                pl.when(when)(copy.wait_send)

        def sent(ref, name, when=None):
            copy = group(ref, sends[name] if isinstance(name, str) else name, sends["ar"])
            if when is None:
                copy.wait_send()
            else:
                pl.when(when)(copy.wait_send)

        for d in range(2):
            for s in range(1, line):
                sent(
                    wg.at[:, 0], ag_s.at[d, s - 1],
                    jnp.logical_and(ahead(d) >= 1, ahead(1 - d) >= s - 1),
                )
        for t, name in enumerate(("a", "b")):
            sent(outs[t], "in_" + name)
            sent(us[t], "out_" + name, edge > 0)
            sent(gis[t], "g_" + name)
        sent(attn_out, "k")
        sent(attn_out, "v")
        sent(attn_out, "xq")
        for x, name in ((kx, "hk"), (vx, "hv")):
            sent(x.at[:WINDOW], name, to_other)
            sent(x.at[back:WINDOW], name, answers)
        sent(part_out, "pt", answers)
        sent(qn, "qb", asks)
        sent(attn_out, "a")
        sent(f_out, "f")
    with scope("t_mix_oc"):
        group(attn_in, sends["a"], sends["ar"]).wait_recv()
        group(f_in.at[:, :3 * quarter], sends["f"], sends["fr"]).wait_recv()
        for i in range(tiles):
            mix_other(i, slice(0, 3 * quarter))
    with scope("t_last"):
        group(f_in.at[:, 3 * quarter:], sends["f"], sends["fr_last"]).wait_recv()
        for i in range(tiles):
            mix_other(i, slice(3 * quarter, hd))
            tile_store(i, oc).start()
    with scope("t_stores"):
        pltpu.make_async_copy(o_all, o_all, sends["new"]).wait()
        pltpu.make_async_copy(mixed, mixed_to, sends["mixed"]).wait()


def store(*refs):
    sems = refs[-1]
    copies = [pltpu.make_async_copy(refs[i], refs[4 + i], sems.at[i]) for i in range(4)]
    for at in range(0, refs[0].shape[0], TILE):
        piece = pl.ds(at, TILE)
        pltpu.make_async_copy(refs[0].at[piece], refs[4].at[piece], sems.at[0]).start()
    for copy in copies[1:]:
        copy.start()
    for copy in copies:
        copy.wait()


def local(n, hn, queries, keys, values, rate, fast_gate, fast_up, fast_down, out_gain):
    rows, width = queries.shape
    heads, shard, hd = fast_gate.shape
    line = n // 2
    half = hd // 2
    tiles = rows // TILE
    sums = (4, line, 2, shard, half)
    sums_b = (4, line, 2, shard, hd // 4)
    dma = pltpu.SemaphoreType.DMA
    vmem = pl.BlockSpec(memory_space=pltpu.VMEM)
    hbm = pl.BlockSpec(memory_space=pltpu.HBM)
    results = pl.pallas_call(
        functools.partial(kernel, n, hn),
        out_shape=(
            pltpu.VMEM((rows, width), BF16),
            pltpu.VMEM(fast_gate.shape, F32),
            pltpu.VMEM(fast_up.shape, F32),
            pltpu.VMEM(fast_down.shape, F32),
        ),
        in_specs=[hbm] * 8,
        out_specs=(pl.BlockSpec(memory_space=pl.ANY),) * 4,
        scratch_shapes=[
            pltpu.VMEM((rows, width), BF16),
            pltpu.VMEM((3,) + fast_gate.shape, F32),
            pltpu.VMEM((3, 2, shard, hd), F32),
            pltpu.VMEM(rate.shape, F32),
            pltpu.VMEM((1, width), F32),
            pltpu.VMEM((3, line, 2, shard, hd), BF16),
            pltpu.VMEM(sums, BF16),
            pltpu.VMEM(sums_b, BF16),
            pltpu.VMEM(sums, F32),
            pltpu.VMEM(sums_b, F32),
            pltpu.VMEM(sums, BF16),
            pltpu.VMEM(sums_b, BF16),
            pltpu.VMEM(sums, BF16),
            pltpu.VMEM(sums_b, BF16),
            pltpu.VMEM(sums, BF16),
            pltpu.VMEM(sums_b, BF16),
            pltpu.VMEM((3, shard, hd), BF16),
            pltpu.VMEM((4, shard, half), BF16),
            pltpu.VMEM((4, shard, hd // 4), BF16),
            pltpu.VMEM((8, hd), F32),
            pltpu.VMEM((8, hd), F32),
            pltpu.VMEM((2 * rows, hd), BF16),
            pltpu.VMEM((WINDOW + 2 * rows, hd), BF16),
            pltpu.VMEM((WINDOW + 2 * rows, hd), BF16),
            pltpu.VMEM((hd, 2 * rows), BF16),
            pltpu.VMEM(rate.shape, F32),
            pltpu.VMEM((2 * rows, hd), BF16),
            pltpu.VMEM((2 * rows, hd), BF16),
            pltpu.VMEM((2, 2 * rows, hd), BF16),
            pltpu.VMEM((2, 2 * rows, hd), F32),
            pltpu.VMEM((2, rows, hd), F32),
            pltpu.VMEM((rows, TILE), F32),
            pltpu.VMEM((BACK * TILE, TILE), F32),
            pltpu.VMEM((BACK * TILE, hd), BF16),
            pltpu.VMEM((BACK * TILE, hd), BF16),
            pltpu.VMEM((BACK * TILE, hd), BF16),
            pltpu.VMEM((8, BACK * TILE), F32),
            pltpu.VMEM((8, BACK * TILE), F32),
            pltpu.VMEM((rows, hd), BF16),
            pltpu.VMEM((rows, hd), BF16),
            pltpu.VMEM((2 * rows, hd), BF16),
            pltpu.VMEM((rows, hd), F32),
            pltpu.VMEM((rows, hd), BF16),
            pltpu.VMEM((rows, hd), BF16),
            pltpu.VMEM((2, 8, rows), F32),
            pltpu.VMEM((2 * hn - 1, 8, rows), F32),
        ]
        + [dma((2, line - 1)), dma((2, 6, line - 1))]
        + [dma((4 * math.gcd(PARTS, line) + 4 * math.gcd(PARTS // 2, line),))] * 2
        + [dma((8,)), dma((4,)), dma((4,)), dma((tiles,)), dma((tiles,))]
        + [dma((2 * WINDOW // TILE,)), dma((tiles,)), dma((BACK,)), dma((BACK + 1,))]
        + [dma((23,)), dma((2,))],
        compiler_params=pltpu.CompilerParams(
            collective_id=0, has_side_effects=True, vmem_limit_bytes=42 * 1024 * 1024
        ),
        name="ttt_layer",
    )(
        *(
            pltpu.with_memory_space_constraint(x, pltpu.HBM)
            for x in (
                queries, keys, values, rate, out_gain.reshape(1, width),
                fast_gate, fast_up, fast_down,
            )
        )
    )
    return pl.pallas_call(
        store,
        out_shape=tuple(jax.ShapeDtypeStruct(x.shape, x.dtype) for x in results),
        in_specs=[vmem] * 4,
        out_specs=(hbm,) * 4,
        scratch_shapes=[dma((4,))],
        compiler_params=pltpu.CompilerParams(vmem_limit_bytes=1024 * 1024),
        name="store",
    )(*results)


def solution(mesh):
    weights = P("head", "seq", None)
    tokens = P("seq", "head")
    return jax.shard_map(
        functools.partial(local, mesh.shape["seq"], mesh.shape["head"]),
        mesh=mesh,
        in_specs=(tokens, tokens, tokens, P("head", "seq"), weights, weights, weights, P("head")),
        out_specs=(tokens, weights, weights, weights),
        check_vma=False,
    )
```
